512 devices in a mesh: seg: 64 (over y, x, core), head: 8 (over z).
Axes of the slice: x: 4, y: 8, z: 8, core: 2. Of those that a mesh axis runs over, the one named last changes fastest.
Arguments:
- head_input: bfloat16 [1536, 131072], P('head', 'seg'), may hold values from -6 to 6
- gate_input: bfloat16 [1536, 131072], P('head', 'seg'), may hold values from -8 to 8
- input_map: bfloat16 [131072, 128], P('seg'), may hold values from -6 to 6
- output_map: bfloat16 [131072, 128], P('seg'), may hold values from -0.5 to 0.5
- step_size: float32 [24, 131072], P('head', 'seg'), may hold values from 0 to 1
- log_decay: float32 [24, 131072], P('head', 'seg'), may hold values from -1 to 0
- skip_gain: float32 [24], P('head'), may hold values from 0.5 to 1.5
- residual: bfloat16 [1536, 131072], P('head', 'seg'), may hold values from -6 to 6
- boundary: int32 [131072], P('seg'), may hold values from 0 to 1, as said below
- norm_gain: bfloat16 [1536], P('head'), may hold values from 0.099609375 to 1.8984375
- out_weight: bfloat16 [1536, 1536], P('head'), may hold values from -0.15625 to 0.15625
Outputs:
- span_rows: bfloat16 [32768, 1536], P(('seg', 'head'))
The draws below stay inside these ranges and needn't reach their ends.
Inputs may be any that keep to these rules, and one draw needn't show every extreme that they name: `boundary`: each segment of 2048 positions holds between 128 and 512 ones, exactly 512 in some segment.
All inputs are finite; a program needn't handle non-finite values.
Results may differ from the reference program's by a relative error of at most 0.015.
Values may be sent and summed in bfloat16 or wider, within the bound.
No kernel may reach another device: no remote copies, remote signals or barrier semaphores. Data moves between devices by JAX's collectives and lax.ppermute only.
A program may use at most 64 MiB of HBM per device.

```python
import jax
import jax.numpy as jnp
from jax import lax

D = 1536
H = 24
P_SIZE = 64
N = 128
L_DEV = 2048
BLOCK = 512
CAP = 512
OCTET_COUNT = 131072
N_SEG = 64


def forgetting_arrangement(key):
    sorting_seed, frequency_seed, flurry_seed = jax.random.split(key, 3)
    order = jax.random.permutation(sorting_seed, H)
    slow_count = H // 2
    slow = order < slow_count
    level = jax.random.uniform(frequency_seed, (H,), jnp.float32)
    slow_rate = jnp.exp(jnp.log(0.2) + level * jnp.log(5.0)) / OCTET_COUNT
    fast_rate = jnp.exp(jnp.log(1.0 / 50.0) + level * jnp.log(50.0 / 30.0))
    cut_probability = jnp.where(slow, slow_rate, fast_rate)
    flurry_extents = jax.random.randint(flurry_seed, (3,), 0, OCTET_COUNT)
    return (cut_probability, flurry_extents)


def draw_log_decay(key, part):
    cut_probability, flurry_extents = forgetting_arrangement(jax.random.fold_in(key, 11))
    key_rough, key_depth = jax.random.split(jax.random.fold_in(key, 21))
    rough = jnp.exp(jax.random.uniform(key_rough, (H, OCTET_COUNT), jnp.float32, jnp.log(0.5), jnp.log(2.0)))
    depth = jax.random.uniform(key_depth, (3,), jnp.float32, 0.22, 0.69)
    cut_indices = jnp.arange(OCTET_COUNT)[None, :] == flurry_extents[:, None]
    extra = jnp.sum(jnp.where(cut_indices, depth[:, None], 0.0), axis=0)
    return (-(cut_probability[:, None] * rough) - extra[None, :]).astype(jnp.float32)


def draw_step_size(key, part):
    cut_probability, flurry_extents = forgetting_arrangement(jax.random.fold_in(key, 11))
    key_rough = jax.random.fold_in(key, 22)
    rough = jnp.exp(jax.random.uniform(key_rough, (H, OCTET_COUNT), jnp.float32, jnp.log(0.5), jnp.log(2.0)))
    steps = jnp.sqrt(2.0 * cut_probability)[:, None] * rough
    return steps.astype(jnp.float32)


def draw_gate_input(key, part):
    columns = (jnp.arange(D) // P_SIZE).astype(jnp.float32)
    reach = columns / max(H - 1, 1)
    values = jnp.clip(jax.random.normal(key, (D, OCTET_COUNT), jnp.float32), -4.0, 4.0)
    scale = jnp.power(3.0, reach) / 1.7
    return (values * scale[:, None]).astype(jnp.bfloat16)


def segment_ranks(key_one):
    return jax.random.permutation(key_one, L_DEV)


def draw_boundary(key, part):
    segments = OCTET_COUNT // L_DEV
    key_count, key_full, key_rank = jax.random.split(key, 3)
    counts = jax.random.randint(key_count, (segments,), CAP // 4, CAP + 1)
    full = jax.random.randint(key_full, (), 0, segments)
    counts = jnp.where(jnp.arange(segments) == full, CAP, counts)
    ranks = jax.vmap(segment_ranks)(jax.random.split(key_rank, segments))
    return (ranks < counts[:, None]).astype(jnp.int32).reshape(OCTET_COUNT)


def levels(stream_key, extent, cuts, smallest, top_value):
    def one(axis_at, shards_of):
        draws = jax.random.uniform(jax.random.fold_in(jax.random.fold_in(stream_key, 6), axis_at), (shards_of,), jnp.float32, smallest / len(cuts), top_value / len(cuts))
        return jnp.repeat(jnp.exp(draws), extent[axis_at] // shards_of).reshape((-1,) + (1,) * (len(extent) - axis_at - 1))

    gain = one(*cuts[0])
    for cut in cuts[1:]:
        gain = gain * one(*cut)
    return gain


def gaussian(key, dims, scale, bound, cuts=(), kind=jnp.bfloat16):
    entries = scale * jax.random.normal(key, dims, jnp.float32)
    if cuts:
        entries = entries * levels(key, dims, cuts, -0.22, 0.18)
    return jnp.clip(entries, -bound, bound).astype(kind)


def setup_inputs(seed: int = 0) -> dict:
    splits = jax.random.split(jax.random.key(seed), 12)
    head_input = gaussian(splits[0], (D, OCTET_COUNT), 1.0, 6.0, ((0, 8), (1, 64)))
    gate_input = draw_gate_input(jax.random.fold_in(splits[11], 71), 0)
    input_map = gaussian(splits[2], (OCTET_COUNT, N), 1.0, 6.0, ((0, 64),))
    output_map = gaussian(splits[3], (OCTET_COUNT, N), N ** -0.5, 0.5, ((0, 64),))
    step_size = draw_step_size(jax.random.fold_in(splits[11], 71), 0)
    log_decay = draw_log_decay(jax.random.fold_in(splits[11], 71), 0)
    skip_gain = jnp.clip(0.5 + 1.0 * jax.random.uniform(splits[6], (H,), jnp.float32) ** levels(splits[6], (H,), ((0, 8),), -0.2, 0.2), 0.5, 1.5)
    residual = gaussian(splits[7], (D, OCTET_COUNT), 1.0, 6.0, ((0, 8), (1, 64)))
    boundary = draw_boundary(jax.random.fold_in(splits[11], 71), 0)
    norm_gain = jnp.clip(1.0 + 0.18 * jax.random.normal(splits[9], (D,), jnp.float32), 0.099609375, 1.8984375).astype(jnp.bfloat16)
    out_weight = gaussian(splits[10], (D, D), D ** -0.5, 0.15625, ((0, 8),))
    return dict(head_input=head_input, gate_input=gate_input, input_map=input_map, output_map=output_map, step_size=step_size, log_decay=log_decay, skip_gain=skip_gain, residual=residual, boundary=boundary, norm_gain=norm_gain, out_weight=out_weight)


def reference(head_input, gate_input, input_map, output_map, step_size, log_decay, skip_gain, residual, boundary, norm_gain, out_weight):
    head_input = head_input.T
    gate_input = gate_input.T
    residual = residual.T
    seq_total = head_input.shape[0]
    heads = step_size.shape[0]
    head_width = head_input.shape[1] // heads
    state_width = input_map.shape[1]
    block_count = seq_total // BLOCK
    inputs_blocked = head_input.reshape(block_count, BLOCK, heads, head_width)
    input_blocked = input_map.reshape(block_count, BLOCK, state_width)
    output_blocked = output_map.reshape(block_count, BLOCK, state_width)
    steps_blocked = step_size.reshape(heads, block_count, BLOCK).transpose(1, 0, 2)
    decay_blocked = log_decay.reshape(heads, block_count, BLOCK).transpose(1, 0, 2)
    lower = jnp.arange(BLOCK)[:, None] >= jnp.arange(BLOCK)[None, :]

    def advance(carry, item):
        x_block, in_block, out_block, step_block, decay_block = item
        running = jnp.cumsum(decay_block, axis=1)
        last = running[:, -1]
        scores = jnp.dot(out_block, in_block.T, preferred_element_type=jnp.float32)
        spread = running[:, :, None] - running[:, None, :]
        decay = jnp.where(lower[None], jnp.exp(jnp.where(lower[None], spread, 0.0)), 0.0)
        weights = (scores[None] * decay * step_block[:, None, :]).astype(jnp.bfloat16)
        inner = jnp.einsum('hts,shp->thp', weights.astype(jnp.float32), x_block.astype(jnp.float32))
        state_half = carry.astype(jnp.bfloat16)
        outer = jnp.einsum('tn,hpn->thp', out_block.astype(jnp.float32), state_half.astype(jnp.float32))
        outer = outer * jnp.exp(running).T[:, :, None]
        result = (inner + outer + skip_gain[None, :, None] * x_block.astype(jnp.float32)).astype(jnp.bfloat16)
        factor = (step_block * jnp.exp(last[:, None] - running)).T
        scaled = (x_block.astype(jnp.float32) * factor[:, :, None]).astype(jnp.bfloat16)
        added = jnp.einsum('shp,sn->hpn', scaled.astype(jnp.float32), in_block.astype(jnp.float32))
        return (jnp.exp(last)[:, None, None] * carry + added, result)
    start = jnp.zeros((heads, head_width, state_width), jnp.float32)
    final, outputs = lax.scan(advance, start, (inputs_blocked, input_blocked, output_blocked, steps_blocked, decay_blocked))
    ssd_out = outputs.reshape(seq_total, heads * head_width)
    flags = boundary.reshape(N_SEG, L_DEV)
    running_flags = jnp.cumsum(flags, axis=1).astype(jnp.int32)
    counts = running_flags[:, -1]
    slots = jnp.arange(CAP, dtype=jnp.int32)

    def locate(row):
        return lax.optimization_barrier(jnp.sum((row[None, :] <= slots[:, None]).astype(jnp.int32), axis=1)).astype(jnp.int32)
    positions = lax.map(locate, running_flags)
    offsets = (jnp.arange(N_SEG, dtype=jnp.int32) * L_DEV)[:, None]
    global_pos = (positions + offsets).reshape(-1).astype(jnp.int32)
    used = (slots[None, :] < counts[:, None]).reshape(-1)
    y_rows = jnp.take(ssd_out, global_pos, axis=0).astype(jnp.float32)
    gate_rows = jnp.take(gate_input, global_pos, axis=0).astype(jnp.float32)
    resid_rows = jnp.take(residual, global_pos, axis=0).astype(jnp.float32)
    gated = y_rows * jax.nn.silu(gate_rows)
    squares = lax.optimization_barrier(jnp.sum(gated * gated, axis=1)) / D
    normed = (gated * lax.rsqrt(squares + 1e-05)[:, None] * norm_gain.astype(jnp.float32)[None, :]).astype(jnp.bfloat16)
    projected = jnp.dot(normed, out_weight, preferred_element_type=jnp.float32) + resid_rows
    return jnp.where(used[:, None], projected, 0.0).astype(jnp.bfloat16)
```

```python
import functools

import jax
import jax.numpy as jnp
from jax import lax
from jax.experimental import pallas as pl
from jax.experimental.pallas import tpu as pltpu
from jax.sharding import Mesh
from jax.sharding import PartitionSpec as P

F32 = jnp.float32
BF16 = jnp.bfloat16
Q = 128
NT = (((1,), (1,)), ((), ()))
NN = (((1,), (0,)), ((), ()))


def dot(a, b, dims=NN):
    return lax.dot_general(a, b, dims, preferred_element_type=F32)


def pieces(v):
    hi = v.astype(BF16)
    rest = v - hi.astype(F32)
    mid = rest.astype(BF16)
    low = (rest - mid.astype(F32)).astype(BF16)
    return hi, mid, low


def dot3(v, b, dims=NN):
    return sum(dot(p, b, dims) for p in pieces(v))


def dot3r(a, v, dims=NT):
    return sum(dot(a, p, dims) for p in pieces(v))


def below(shape, strict=False):
    i = lax.broadcasted_iota(jnp.int32, shape, 0)
    j = lax.broadcasted_iota(jnp.int32, shape, 1)
    return jnp.where((i < j) if strict else (i <= j), 1.0, 0.0).astype(BF16)


def chunk_rows(ref, heads):
    n = ref.shape[1] // Q
    return jnp.concatenate([ref[:, c * Q : (c + 1) * Q] for c in range(n)], axis=0)


def log_tile(total, rows):
    heads = total.shape[0]
    lane = lax.broadcasted_iota(jnp.int32, (heads, Q), 1)
    hi, mid, low = pieces(jnp.broadcast_to(total, (heads, Q)))
    tile = jnp.where(
        lane == 0,
        hi.astype(F32),
        jnp.where(lane == 1, mid.astype(F32), jnp.where(lane == 2, low.astype(F32), 0.0)),
    )
    return jnp.concatenate([tile, jnp.zeros((rows - heads, Q), F32)], axis=0)


def final_state_kernel(heads, parts, x_ref, in_ref, step_ref, decay_ref, out_ref, scaled):
    width = x_ref.shape[0] // heads
    length = x_ref.shape[1]
    chunks = length // Q
    rows = width // parts
    logs = chunk_rows(decay_ref, heads)
    after = lax.broadcasted_iota(jnp.int32, (Q, Q), 0) > lax.broadcasted_iota(
        jnp.int32, (Q, Q), 1
    )
    suffix = dot3(logs, jnp.where(after, 1.0, 0.0).astype(BF16))
    sums = jnp.sum(logs, axis=1, keepdims=True)
    later = jnp.zeros((heads, 1), F32)
    for c in reversed(range(chunks)):
        here = slice(c * heads, (c + 1) * heads)
        lanes = slice(c * Q, (c + 1) * Q)
        factor = step_ref[:, lanes] * jnp.exp(suffix[here] + later)
        for h in range(heads):
            part = slice(h * width, (h + 1) * width)
            scaled[part, lanes] = (x_ref[part, lanes].astype(F32) * factor[h : h + 1]).astype(BF16)
        later = later + sums[here]
    state = dot(scaled[...], in_ref[...])
    tail = log_tile(later, out_ref.shape[1] - heads * rows)
    for j in range(parts):
        own = [state[h * width + j * rows : h * width + (j + 1) * rows] for h in range(heads)]
        out_ref[j] = jnp.concatenate(own + [tail], axis=0).astype(BF16)


def read_logs(block, heads, start):
    sums = jnp.sum(block[start:].astype(F32), axis=1, keepdims=True)
    return sums[:heads]


def spread(column, rows):
    return jnp.concatenate(
        [jnp.broadcast_to(column[h : h + 1], (rows, Q)) for h in range(column.shape[0])], axis=0
    )


def group_scan_kernel(heads, in_ref, before_ref, factor_ref, total_ref):
    parts = in_ref.shape[0]
    used = before_ref.shape[1]
    rows = used // heads
    state = jnp.zeros((used, Q), F32)
    log = jnp.zeros((heads, 1), F32)
    for i in range(parts):
        block = in_ref[i].astype(F32)
        before_ref[i] = state
        factor_ref[i] = spread(jnp.exp(log), rows)
        own = read_logs(block, heads, used)
        state = spread(jnp.exp(own), rows) * state + block[:used]
        log = log + own
    tail = log_tile(log, in_ref.shape[1] - used)
    whole = jnp.concatenate([state, tail], axis=0).astype(BF16)
    for j in range(total_ref.shape[0]):
        total_ref[j] = whole


def combine_kernel(heads, in_ref, before_ref, factor_ref, out_ref):
    used = before_ref.shape[1]
    rows = used // heads
    me = lax.axis_index("y")
    state = jnp.zeros((used, Q), F32)
    for g in range(in_ref.shape[0] - 1):
        block = in_ref[g].astype(F32)
        moved = spread(jnp.exp(read_logs(block, heads, used)), rows) * state + block[:used]
        state = jnp.where(g < me, moved, state)
    for i in range(before_ref.shape[0]):
        out_ref[i] = (before_ref[i] + factor_ref[i] * state).astype(BF16)


def local_kernel(
    heads,
    skip_ref,
    x_ref,
    gate_ref,
    res_ref,
    in_ref,
    out_map_ref,
    step_ref,
    decay_ref,
    flag_ref,
    value_ref,
    factor_ref,
    rows_ref,
    picked_ref,
    y_all,
    cums,
    pick,
):
    width = x_ref.shape[0] // heads
    length = x_ref.shape[1]
    chunks = length // Q
    upto = below((Q, Q))
    row = lax.broadcasted_iota(jnp.int32, (Q, Q), 0)
    col = lax.broadcasted_iota(jnp.int32, (Q, Q), 1)
    mask = row <= col
    eye = jnp.where(row == col, 1.0, 0.0).astype(BF16)
    down = jnp.where(col <= row, 1.0, 0.0).astype(BF16)
    logs = chunk_rows(decay_ref, heads)
    steps = chunk_rows(step_ref, heads)
    run_row = dot3(logs, upto)
    run_col = dot3r(down, logs)
    step_col = dot3r(eye, steps)
    state = [jnp.zeros((width, Q), F32) for _ in range(heads)]
    before = [jnp.zeros((1, 1), F32) for _ in range(heads)]
    for c in range(chunks):
        lanes = slice(c * Q, (c + 1) * Q)
        b = in_ref[lanes, :]
        o = out_map_ref[lanes, :]
        scores = dot(b, o, NT)
        for h in range(heads):
            k = c * heads + h
            part = slice(h * width, (h + 1) * width)
            run = run_row[k : k + 1]
            last = run[:, Q - 1 : Q]
            spread_log = run - run_col[:, k : k + 1]
            decay = jnp.where(mask, jnp.exp(spread_log), 0.0)
            weights = (scores * decay * step_col[:, k : k + 1]).astype(BF16)
            x = x_ref[part, lanes]
            xf = x.astype(F32)
            y = dot(x, weights) + skip_ref[h] * xf
            y = y + dot(state[h].astype(BF16), o, NT) * jnp.exp(run)
            y_all[part, lanes] = y.astype(BF16)
            scaled = (xf * (steps[k : k + 1] * jnp.exp(last - run))).astype(BF16)
            state[h] = jnp.exp(last) * state[h] + dot(scaled, b)
            for i, piece in enumerate(pieces(run + before[h])):
                cums[i * 8 + h : i * 8 + h + 1, lanes] = piece.astype(F32)
            before[h] = before[h] + last

    flags = flag_ref[...].astype(F32)
    within = dot(flags.astype(BF16), upto)
    rows = lax.broadcasted_iota(jnp.int32, (chunks, chunks), 0)
    cols = lax.broadcasted_iota(jnp.int32, (chunks, chunks), 1)
    sums = jnp.broadcast_to(within[:, Q - 1 : Q], (chunks, Q)).astype(BF16)
    earlier = dot(jnp.where(cols < rows, 1.0, 0.0).astype(BF16), sums)
    rank = jnp.where(flags > 0.0, within + earlier, 0.0) - 1.0
    slots = value_ref.shape[0]
    tile = 128
    slot = lax.broadcasted_iota(jnp.int32, (tile, Q), 0).astype(F32)
    for g in range(slots // tile):
        for c in range(chunks):
            hit = (rank[c : c + 1] - float(g * tile)) == slot
            pick[g * tile : (g + 1) * tile, c * Q : (c + 1) * Q] = jnp.where(hit, 1.0, 0.0).astype(
                BF16
            )
    log_pieces = cums[...].astype(BF16)
    for g in range(slots // tile):
        these = slice(g * tile, (g + 1) * tile)
        chosen = pick[these]
        gate = dot(chosen, gate_ref[...], NT)
        silu = gate / (1.0 + jnp.exp(-gate))
        value_ref[these] = dot(chosen, y_all[...], NT) * silu
        logs_at = dot(chosen, log_pieces, NT)
        for h in range(heads):
            run = logs_at[:, h : h + 1] + logs_at[:, 8 + h : 9 + h] + logs_at[:, 16 + h : 17 + h]
            part = slice(h * width, (h + 1) * width)
            factor_ref[these, part] = jnp.exp(run) * silu[:, part]
        rows_ref[these] = dot(chosen, out_map_ref[...]).astype(BF16)
        per = picked_ref.shape[1]
        taken = dot(chosen, res_ref[...], NT).astype(BF16)
        step = min(per, tile)
        for j in range(0, tile, step):
            to, at = divmod(g * tile + j, per)
            picked_ref[to, at : at + step] = taken[j : j + step]


def gate_kernel(heads, in_ref, rows_ref, value_ref, factor_ref, gain_ref, out_ref):
    parts = in_ref.shape[0]
    rows = in_ref.shape[1] // heads
    per = out_ref.shape[1]
    columns = value_ref.shape[1]
    held = in_ref[...].astype(F32)
    states = [held[:, h * rows : (h + 1) * rows].reshape(parts * rows, Q) for h in range(heads)]
    incoming = jnp.concatenate(states, axis=0).astype(BF16)
    outer = dot(rows_ref[...], incoming, NT)
    gated = value_ref[...] + factor_ref[...] * outer
    squares = jnp.sum(gated * gated, axis=1, keepdims=True)
    scaled = (gated * gain_ref[...].astype(F32)).astype(BF16)
    slots = gated.shape[0]
    pad = out_ref.shape[2] - columns
    lane = lax.broadcasted_iota(jnp.int32, (slots, pad), 1)
    hi, mid, low = pieces(jnp.broadcast_to(squares, (slots, pad)))
    extra = jnp.where(
        lane == 0,
        hi.astype(F32),
        jnp.where(lane == 1, mid.astype(F32), jnp.where(lane == 2, low.astype(F32), 0.0)),
    ).astype(BF16)
    for j in range(slots // per):
        these = slice(j * per, (j + 1) * per)
        out_ref[j, :, :columns] = scaled[these]
        out_ref[j, :, columns:] = extra[these]


def project_kernel(full_width, in_ref, res_ref, weight_ref, out_ref, lhs, res):
    groups, per, _ = in_ref.shape
    columns = res_ref.shape[2]
    halves = weight_ref.shape[0]
    half = weight_ref.shape[2]
    squares = jnp.zeros((per, 1), F32)
    for z in range(groups):
        block = in_ref[z]
        lhs[:, z * columns : (z + 1) * columns] = block[:, :columns]
        res[:, z * columns : (z + 1) * columns] = res_ref[z]
        squares = squares + jnp.sum(block[:, columns:].astype(F32), axis=1, keepdims=True)
    scale = lax.rsqrt(squares / full_width + 1e-05)
    for k in range(halves):
        part = slice(k * half, (k + 1) * half)
        done = dot(lhs[...], weight_ref[k])
        out_ref[:, part] = (done * scale + res[:, part].astype(F32)).astype(BF16)


def call(kernel, outs, args, scratch=(), smem=0, name=None):
    vmem = pl.BlockSpec(memory_space=pltpu.VMEM)
    specs = [pl.BlockSpec(memory_space=pltpu.SMEM)] * smem + [vmem] * (len(args) - smem)
    many = isinstance(outs, (tuple, list))
    return pl.pallas_call(
        kernel,
        out_shape=outs,
        in_specs=specs,
        out_specs=[vmem] * len(outs) if many else vmem,
        scratch_shapes=list(scratch),
        name=name,
    )(*args)


def on_device(
    head_input,
    gate_input,
    input_map,
    output_map,
    step_size,
    log_decay,
    skip_gain,
    residual,
    boundary,
    norm_gain,
    out_weight,
):
    S = jax.ShapeDtypeStruct
    group = ("x", "core")
    parts = lax.axis_size(group)
    groups = lax.axis_size("y")
    shares = lax.axis_size("head")
    local_width, length = head_input.shape
    heads = step_size.shape[0]
    full_width = out_weight.shape[1]
    slots = length // 4
    per = slots // shares
    used = local_width // parts
    height = used + 8

    half = full_width // lax.axis_size("core")
    own = lax.dynamic_slice_in_dim(out_weight, lax.axis_index("core") * half, half, 1)
    weight = lax.all_gather(own[None], ("core", "head"), axis=0, tiled=True)
    weight = weight.reshape(lax.axis_size("core"), shares * local_width, half)

    state = call(
        functools.partial(final_state_kernel, heads, parts),
        S((parts, height, Q), BF16),
        (head_input, input_map, step_size, log_decay),
        [pltpu.VMEM((local_width, length), BF16)],
        name="final_state",
    )
    moved = lax.all_to_all(state, group, 0, 0, tiled=True)
    before, factor, total = call(
        functools.partial(group_scan_kernel, heads),
        (
            S((parts, used, Q), F32),
            S((parts, used, Q), F32),
            S((groups, height, Q), BF16),
        ),
        (moved,),
        name="group_scan",
    )
    totals = lax.all_to_all(total, "y", 0, 0, tiled=True)
    value, decay, rows, picked = call(
        functools.partial(local_kernel, heads),
        (
            S((slots, local_width), F32),
            S((slots, local_width), F32),
            S((slots, Q), BF16),
            S((shares, per, local_width), BF16),
        ),
        (
            skip_gain,
            head_input,
            gate_input,
            residual,
            input_map,
            output_map,
            step_size,
            log_decay,
            boundary.reshape(length // Q, Q),
        ),
        [
            pltpu.VMEM((local_width, length), BF16),
            pltpu.VMEM((24, length), F32),
            pltpu.VMEM((slots, length), BF16),
        ],
        smem=1,
        name="local_ssd",
    )
    incoming = call(
        functools.partial(combine_kernel, heads),
        S((parts, used, Q), BF16),
        (totals, before, factor),
        name="combine",
    )
    kept = lax.all_to_all(picked, "head", 0, 0, tiled=True)
    incoming = lax.all_to_all(incoming, group, 0, 0, tiled=True)
    gated = call(
        functools.partial(gate_kernel, heads),
        S((shares, per, -(-(local_width + 3) // Q) * Q), BF16),
        (incoming, rows, value, decay, norm_gain.reshape(1, local_width)),
        name="gated",
    )
    gathered = lax.all_to_all(gated, "head", 0, 0, tiled=True)
    return call(
        functools.partial(project_kernel, full_width),
        S((per, full_width), BF16),
        (gathered, kept, weight),
        [pltpu.VMEM((per, full_width), BF16), pltpu.VMEM((per, full_width), BF16)],
        name="project",
    )


def solution(mesh):
    heads = mesh.shape["head"]
    segs = mesh.shape["seg"]
    core, x = (2, 4) if segs % 8 == 0 else (1, 1)
    if segs == 8:
        x = 2
    fine = Mesh(mesh.devices.reshape(segs // (x * core), x, core, heads), ("y", "x", "core", "head"))
    seg = ("y", "x", "core")
    return jax.shard_map(
        on_device,
        mesh=fine,
        in_specs=(
            P("head", seg),
            P("head", seg),
            P(seg, None),
            P(seg, None),
            P("head", seg),
            P("head", seg),
            P("head"),
            P("head", seg),
            P(seg),
            P("head"),
            P("head", None),
        ),
        out_specs=P((*seg, "head"), None),
        check_vma=False,
    )
```

```python
import functools

import jax
import jax.numpy as jnp
from jax import lax
from jax.experimental import pallas as pl
from jax.experimental.pallas import tpu as pltpu
from jax.sharding import Mesh
from jax.sharding import PartitionSpec as P

F32 = jnp.float32
BF16 = jnp.bfloat16
Q = 128
NT = (((1,), (1,)), ((), ()))
NN = (((1,), (0,)), ((), ()))


def dot(a, b, dims=NN):
    return lax.dot_general(a, b, dims, preferred_element_type=F32)


def pieces(v):
    hi = v.astype(BF16)
    rest = v - hi.astype(F32)
    mid = rest.astype(BF16)
    low = (rest - mid.astype(F32)).astype(BF16)
    return hi, mid, low


def dot3(v, b, dims=NN):
    return sum(dot(p, b, dims) for p in pieces(v))


def dot3r(a, v, dims=NT):
    return sum(dot(a, p, dims) for p in pieces(v))


def below(shape, strict=False):
    i = lax.broadcasted_iota(jnp.int32, shape, 0)
    j = lax.broadcasted_iota(jnp.int32, shape, 1)
    return jnp.where((i < j) if strict else (i <= j), 1.0, 0.0).astype(BF16)


def chunk_rows(ref, heads):
    n = ref.shape[1] // Q
    return jnp.concatenate([ref[:, c * Q : (c + 1) * Q] for c in range(n)], axis=0)


def log_tile(total, rows):
    heads = total.shape[0]
    lane = lax.broadcasted_iota(jnp.int32, (heads, Q), 1)
    hi, mid, low = pieces(jnp.broadcast_to(total, (heads, Q)))
    tile = jnp.where(
        lane == 0,
        hi.astype(F32),
        jnp.where(lane == 1, mid.astype(F32), jnp.where(lane == 2, low.astype(F32), 0.0)),
    )
    return jnp.concatenate([tile, jnp.zeros((rows - heads, Q), F32)], axis=0)


def final_state_kernel(heads, parts, x_ref, in_ref, step_ref, decay_ref, out_ref, scaled):
    width = x_ref.shape[0] // heads
    length = x_ref.shape[1]
    chunks = length // Q
    rows = width // parts
    logs = chunk_rows(decay_ref, heads)
    after = lax.broadcasted_iota(jnp.int32, (Q, Q), 0) > lax.broadcasted_iota(
        jnp.int32, (Q, Q), 1
    )
    suffix = dot3(logs, jnp.where(after, 1.0, 0.0).astype(BF16))
    sums = jnp.sum(logs, axis=1, keepdims=True)
    later = jnp.zeros((heads, 1), F32)
    for c in reversed(range(chunks)):
        here = slice(c * heads, (c + 1) * heads)
        lanes = slice(c * Q, (c + 1) * Q)
        factor = step_ref[:, lanes] * jnp.exp(suffix[here] + later)
        for h in range(heads):
            part = slice(h * width, (h + 1) * width)
            scaled[part, lanes] = (x_ref[part, lanes].astype(F32) * factor[h : h + 1]).astype(BF16)
        later = later + sums[here]
    state = dot(scaled[...], in_ref[...])
    tail = log_tile(later, out_ref.shape[1] - heads * rows)
    for j in range(parts):
        own = [state[h * width + j * rows : h * width + (j + 1) * rows] for h in range(heads)]
        out_ref[j] = jnp.concatenate(own + [tail], axis=0).astype(BF16)


def read_logs(block, heads, start):
    sums = jnp.sum(block[start:].astype(F32), axis=1, keepdims=True)
    return sums[:heads]


def spread(column, rows):
    return jnp.concatenate(
        [jnp.broadcast_to(column[h : h + 1], (rows, Q)) for h in range(column.shape[0])], axis=0
    )


def group_scan_kernel(heads, in_ref, before_ref, factor_ref, total_ref):
    parts = in_ref.shape[0]
    used = before_ref.shape[1]
    rows = used // heads
    state = jnp.zeros((used, Q), F32)
    log = jnp.zeros((heads, 1), F32)
    for i in range(parts):
        block = in_ref[i].astype(F32)
        before_ref[i] = state
        factor_ref[i] = spread(jnp.exp(log), rows)
        own = read_logs(block, heads, used)
        state = spread(jnp.exp(own), rows) * state + block[:used]
        log = log + own
    tail = log_tile(log, in_ref.shape[1] - used)
    whole = jnp.concatenate([state, tail], axis=0).astype(BF16)
    for j in range(total_ref.shape[0]):
        total_ref[j] = whole


def combine_kernel(heads, in_ref, before_ref, factor_ref, out_ref):
    used = before_ref.shape[1]
    rows = used // heads
    me = lax.axis_index("y")
    state = jnp.zeros((used, Q), F32)
    for g in range(in_ref.shape[0] - 1):
        block = in_ref[g].astype(F32)
        moved = spread(jnp.exp(read_logs(block, heads, used)), rows) * state + block[:used]
        state = jnp.where(g < me, moved, state)
    for i in range(before_ref.shape[0]):
        out_ref[i] = (before_ref[i] + factor_ref[i] * state).astype(BF16)


def ranks(flag_ref):
    chunks = flag_ref.shape[0]
    flags = flag_ref[...].astype(F32)
    within = dot(flags.astype(BF16), below((Q, Q)))
    sums = jnp.broadcast_to(within[:, Q - 1 : Q], (chunks, Q)).astype(BF16)
    earlier = dot(below((chunks, chunks), strict=True).T, sums)
    return jnp.where(flags > 0.0, within + earlier, 0.0) - 1.0


def fill_pick(pick, flag_ref):
    rank = ranks(flag_ref)
    slot = lax.broadcasted_iota(jnp.int32, (Q, Q), 0).astype(F32)
    for g in range(pick.shape[0] // Q):
        for c in range(flag_ref.shape[0]):
            hit = (rank[c : c + 1] - float(g * Q)) == slot
            pick[g * Q : (g + 1) * Q, c * Q : (c + 1) * Q] = jnp.where(hit, 1.0, 0.0).astype(BF16)


def pick_kernel(
    heads,
    gate_ref,
    res_ref,
    out_map_ref,
    decay_ref,
    flag_ref,
    silu_ref,
    factor_ref,
    rows_ref,
    picked_ref,
    cums,
    pick,
):
    width = gate_ref.shape[0] // heads
    chunks = flag_ref.shape[0]
    run_row = dot3(chunk_rows(decay_ref, heads), below((Q, Q)))
    before = jnp.zeros((heads, 1), F32)
    for c in range(chunks):
        run = run_row[c * heads : (c + 1) * heads]
        for i, piece in enumerate(pieces(run + before)):
            cums[i * 8 : i * 8 + heads, c * Q : (c + 1) * Q] = piece.astype(F32)
        before = before + run[:, Q - 1 : Q]
    fill_pick(pick, flag_ref)
    log_pieces = cums[...].astype(BF16)
    per = picked_ref.shape[1]
    step = min(per, Q)
    for g in range(pick.shape[0] // Q):
        these = slice(g * Q, (g + 1) * Q)
        chosen = pick[these]
        gate = dot(chosen, gate_ref[...], NT)
        silu_ref[these] = gate / (1.0 + jnp.exp(-gate))
        logs_at = dot(chosen, log_pieces, NT)
        for h in range(heads):
            run = logs_at[:, h : h + 1] + logs_at[:, 8 + h : 9 + h] + logs_at[:, 16 + h : 17 + h]
            factor_ref[these, h * width : (h + 1) * width] = jnp.broadcast_to(
                jnp.exp(run), (Q, width)
            )
        rows_ref[these] = dot(chosen, out_map_ref[...]).astype(BF16)
        taken = dot(chosen, res_ref[...], NT).astype(BF16)
        for j in range(0, Q, step):
            to, at = divmod(g * Q + j, per)
            picked_ref[to, at : at + step] = taken[j : j + step]


def ssd_kernel(
    heads,
    skip_ref,
    x_ref,
    in_ref,
    out_map_ref,
    step_ref,
    decay_ref,
    flag_ref,
    value_ref,
    y_all,
    scaled,
    state,
    pick,
):
    width = x_ref.shape[0] // heads
    chunks = flag_ref.shape[0]
    row = lax.broadcasted_iota(jnp.int32, (Q, Q), 0)
    col = lax.broadcasted_iota(jnp.int32, (Q, Q), 1)
    mask = row <= col
    logs = chunk_rows(decay_ref, heads)
    run_row = dot3(logs, below((Q, Q)))
    run_col = dot3r(jnp.where(col <= row, 1.0, 0.0).astype(BF16), logs)
    state[...] = jnp.zeros_like(state)
    for c in range(chunks):
        lanes = slice(c * Q, (c + 1) * Q)
        b = in_ref[lanes, :]
        o = out_map_ref[lanes, :]
        scores = dot(b, o, NT)
        outer = dot(state[...].astype(BF16), o, NT)
        for h in range(heads):
            k = c * heads + h
            part = slice(h * width, (h + 1) * width)
            run = run_row[k : k + 1]
            last = run[:, Q - 1 : Q]
            decay = jnp.where(mask, jnp.exp(run - run_col[:, k : k + 1]), 0.0)
            weights = (scores * decay).astype(BF16)
            xf = x_ref[part, lanes].astype(F32)
            stepped = xf * step_ref[h : h + 1, lanes]
            y = dot(stepped.astype(BF16), weights) + skip_ref[h] * xf
            y_all[part, lanes] = (y + outer[part] * jnp.exp(run)).astype(BF16)
            scaled[part] = (stepped * jnp.exp(last - run)).astype(BF16)
            state[part] = state[part] * jnp.exp(last)
        if c < chunks - 1:
            state[...] += dot(scaled[...], b)
    fill_pick(pick, flag_ref)
    for g in range(pick.shape[0] // Q):
        these = slice(g * Q, (g + 1) * Q)
        value_ref[these] = dot(pick[these], y_all[...], NT)


def gate_kernel(heads, in_ref, rows_ref, value_ref, factor_ref, silu_ref, gain_ref, out_ref):
    parts = in_ref.shape[0]
    rows = in_ref.shape[1] // heads
    per = out_ref.shape[1]
    columns = value_ref.shape[1]
    held = in_ref[...].astype(F32)
    states = [held[:, h * rows : (h + 1) * rows].reshape(parts * rows, Q) for h in range(heads)]
    incoming = jnp.concatenate(states, axis=0).astype(BF16)
    outer = dot(rows_ref[...], incoming, NT)
    gated = (value_ref[...] + factor_ref[...] * outer) * silu_ref[...]
    squares = jnp.sum(gated * gated, axis=1, keepdims=True)
    scaled = (gated * gain_ref[...].astype(F32)).astype(BF16)
    slots = gated.shape[0]
    pad = out_ref.shape[2] - columns
    lane = lax.broadcasted_iota(jnp.int32, (slots, pad), 1)
    hi, mid, low = pieces(jnp.broadcast_to(squares, (slots, pad)))
    extra = jnp.where(
        lane == 0,
        hi.astype(F32),
        jnp.where(lane == 1, mid.astype(F32), jnp.where(lane == 2, low.astype(F32), 0.0)),
    ).astype(BF16)
    for j in range(slots // per):
        these = slice(j * per, (j + 1) * per)
        out_ref[j, :, :columns] = scaled[these]
        out_ref[j, :, columns:] = extra[these]


def project_kernel(full_width, in_ref, res_ref, weight_ref, out_ref, lhs, res):
    groups, per, _ = in_ref.shape
    columns = res_ref.shape[2]
    halves = weight_ref.shape[0]
    half = weight_ref.shape[2]
    squares = jnp.zeros((per, 1), F32)
    for z in range(groups):
        block = in_ref[z]
        lhs[:, z * columns : (z + 1) * columns] = block[:, :columns]
        res[:, z * columns : (z + 1) * columns] = res_ref[z]
        squares = squares + jnp.sum(block[:, columns:].astype(F32), axis=1, keepdims=True)
    scale = lax.rsqrt(squares / full_width + 1e-05)
    for k in range(halves):
        part = slice(k * half, (k + 1) * half)
        done = dot(lhs[...], weight_ref[k])
        out_ref[:, part] = (done * scale + res[:, part].astype(F32)).astype(BF16)


def call(kernel, outs, args, scratch=(), smem=0, name=None, mib=4):
    vmem = pl.BlockSpec(memory_space=pltpu.VMEM)
    specs = [pl.BlockSpec(memory_space=pltpu.SMEM)] * smem + [vmem] * (len(args) - smem)
    many = isinstance(outs, (tuple, list))
    return pl.pallas_call(
        kernel,
        out_shape=outs,
        in_specs=specs,
        out_specs=[vmem] * len(outs) if many else vmem,
        scratch_shapes=list(scratch),
        compiler_params=pltpu.CompilerParams(vmem_limit_bytes=mib << 20),
        name=name,
    )(*args)


def on_device(
    head_input,
    gate_input,
    input_map,
    output_map,
    step_size,
    log_decay,
    skip_gain,
    residual,
    boundary,
    norm_gain,
    out_weight,
):
    S = jax.ShapeDtypeStruct
    group = ("x", "core")
    parts = lax.axis_size(group)
    groups = lax.axis_size("y")
    shares = lax.axis_size("head")
    local_width, length = head_input.shape
    heads = step_size.shape[0]
    full_width = out_weight.shape[1]
    slots = length // 4
    per = slots // shares
    used = local_width // parts
    height = used + 8

    held = lax.optimization_barrier
    flags = boundary.reshape(length // Q, Q)

    state = call(
        functools.partial(final_state_kernel, heads, parts),
        S((parts, height, Q), BF16),
        (head_input, input_map, step_size, log_decay),
        [pltpu.VMEM((local_width, length), BF16)],
        name="final_state",
        mib=8,
    )
    state, flags, out_weight = held((state, flags, out_weight))
    half = full_width // lax.axis_size("core")
    own = lax.dynamic_slice_in_dim(out_weight, lax.axis_index("core") * half, half, 1)
    weight = lax.all_gather(own[None], ("core", "head"), axis=0, tiled=True)
    weight = weight.reshape(lax.axis_size("core"), shares * local_width, half)
    moved = lax.all_to_all(state, group, 0, 0, tiled=True)
    silu, since, rows, picked = call(
        functools.partial(pick_kernel, heads),
        (
            S((slots, local_width), F32),
            S((slots, local_width), F32),
            S((slots, Q), BF16),
            S((shares, per, local_width), BF16),
        ),
        (gate_input, residual, output_map, log_decay, flags),
        [pltpu.VMEM((24, length), F32), pltpu.VMEM((slots, length), BF16)],
        name="pick",
        mib=12,
    )
    moved, picked = held((moved, picked))
    before, factor, total = call(
        functools.partial(group_scan_kernel, heads),
        (
            S((parts, used, Q), F32),
            S((parts, used, Q), F32),
            S((groups, height, Q), BF16),
        ),
        (moved,),
        name="group_scan",
    )
    total, flags, picked = held((total, flags, picked))
    totals = lax.all_to_all(total, "y", 0, 0, tiled=True)
    kept = lax.all_to_all(picked, "head", 0, 0, tiled=True)
    value = call(
        functools.partial(ssd_kernel, heads),
        S((slots, local_width), F32),
        (skip_gain, head_input, input_map, output_map, step_size, log_decay, flags),
        [
            pltpu.VMEM((local_width, length), BF16),
            pltpu.VMEM((local_width, Q), BF16),
            pltpu.VMEM((local_width, Q), F32),
            pltpu.VMEM((slots, length), BF16),
        ],
        smem=1,
        name="ssd",
        mib=12,
    )
    totals, value = held((totals, value))
    incoming = call(
        functools.partial(combine_kernel, heads),
        S((parts, used, Q), BF16),
        (totals, before, factor),
        name="combine",
    )
    incoming = lax.all_to_all(incoming, group, 0, 0, tiled=True)
    gated = call(
        functools.partial(gate_kernel, heads),
        S((shares, per, -(-(local_width + 3) // Q) * Q), BF16),
        (incoming, rows, value, since, silu, norm_gain.reshape(1, local_width)),
        name="gated",
        mib=6,
    )
    gathered = lax.all_to_all(gated, "head", 0, 0, tiled=True)
    return call(
        functools.partial(project_kernel, full_width),
        S((per, full_width), BF16),
        (gathered, kept, weight),
        [pltpu.VMEM((per, full_width), BF16), pltpu.VMEM((per, full_width), BF16)],
        name="project",
        mib=10,
    )


def solution(mesh):
    heads = mesh.shape["head"]
    segs = mesh.shape["seg"]
    core, x = (2, 4) if segs % 8 == 0 else (1, 1)
    if segs == 8:
        x = 2
    fine = Mesh(mesh.devices.reshape(segs // (x * core), x, core, heads), ("y", "x", "core", "head"))
    seg = ("y", "x", "core")
    return jax.shard_map(
        on_device,
        mesh=fine,
        in_specs=(
            P("head", seg),
            P("head", seg),
            P(seg, None),
            P(seg, None),
            P("head", seg),
            P("head", seg),
            P("head"),
            P("head", seg),
            P(seg),
            P("head"),
            P("head", None),
        ),
        out_specs=P((*seg, "head"), None),
        check_vma=False,
    )
```

```python
import functools

import jax
import jax.numpy as jnp
from jax import lax
from jax.experimental import pallas as pl
from jax.experimental.pallas import tpu as pltpu
from jax.sharding import Mesh
from jax.sharding import PartitionSpec as P

F32 = jnp.float32
BF16 = jnp.bfloat16
Q = 128
NT = (((1,), (1,)), ((), ()))
NN = (((1,), (0,)), ((), ()))


def dot(a, b, dims=NN):
    return lax.dot_general(a, b, dims, preferred_element_type=F32)


def pieces(v):
    hi = v.astype(BF16)
    rest = v - hi.astype(F32)
    mid = rest.astype(BF16)
    low = (rest - mid.astype(F32)).astype(BF16)
    return hi, mid, low


def dot3(v, b, dims=NN):
    return sum(dot(p, b, dims) for p in pieces(v))


def dot3r(a, v, dims=NT):
    return sum(dot(a, p, dims) for p in pieces(v))


def below(shape, strict=False):
    i = lax.broadcasted_iota(jnp.int32, shape, 0)
    j = lax.broadcasted_iota(jnp.int32, shape, 1)
    return jnp.where((i < j) if strict else (i <= j), 1.0, 0.0).astype(BF16)


def chunk_rows(ref, heads):
    n = ref.shape[1] // Q
    return jnp.concatenate([ref[:, c * Q : (c + 1) * Q] for c in range(n)], axis=0)


def log_tile(total, rows):
    heads = total.shape[0]
    lane = lax.broadcasted_iota(jnp.int32, (heads, Q), 1)
    hi, mid, low = pieces(jnp.broadcast_to(total, (heads, Q)))
    tile = jnp.where(
        lane == 0,
        hi.astype(F32),
        jnp.where(lane == 1, mid.astype(F32), jnp.where(lane == 2, low.astype(F32), 0.0)),
    )
    return jnp.concatenate([tile, jnp.zeros((rows - heads, Q), F32)], axis=0)


def final_state_kernel(heads, parts, x, in_map, step, decay, out_ref, scaled):
    width = x.shape[0] // heads
    length = x.shape[1]
    chunks = length // Q
    rows = width // parts
    logs = chunk_rows(decay(), heads)
    after = lax.broadcasted_iota(jnp.int32, (Q, Q), 0) > lax.broadcasted_iota(
        jnp.int32, (Q, Q), 1
    )
    suffix = dot3(logs, jnp.where(after, 1.0, 0.0).astype(BF16))
    sums = jnp.sum(logs, axis=1, keepdims=True)
    later = jnp.zeros((heads, 1), F32)
    step_ref = step()
    x_ref = x()
    for c in reversed(range(chunks)):
        here = slice(c * heads, (c + 1) * heads)
        lanes = slice(c * Q, (c + 1) * Q)
        factor = step_ref[:, lanes] * jnp.exp(suffix[here] + later)
        for h in range(heads):
            part = slice(h * width, (h + 1) * width)
            scaled[part, lanes] = (x_ref[part, lanes].astype(F32) * factor[h : h + 1]).astype(BF16)
        later = later + sums[here]
    state = dot(scaled[...], in_map()[...])
    tail = log_tile(later, out_ref.shape[1] - heads * rows)
    for j in range(parts):
        own = [state[h * width + j * rows : h * width + (j + 1) * rows] for h in range(heads)]
        out_ref[j] = jnp.concatenate(own + [tail], axis=0).astype(BF16)


def read_logs(block, heads, start):
    sums = jnp.sum(block[start:].astype(F32), axis=1, keepdims=True)
    return sums[:heads]


def spread(column, rows):
    return jnp.concatenate(
        [jnp.broadcast_to(column[h : h + 1], (rows, Q)) for h in range(column.shape[0])], axis=0
    )


def group_scan_kernel(heads, in_ref, before_ref, factor_ref, total_ref):
    parts = in_ref.shape[0]
    used = before_ref.shape[1]
    rows = used // heads
    state = jnp.zeros((used, Q), F32)
    log = jnp.zeros((heads, 1), F32)
    for i in range(parts):
        block = in_ref[i].astype(F32)
        before_ref[i] = state
        factor_ref[i] = spread(jnp.exp(log), rows)
        own = read_logs(block, heads, used)
        state = spread(jnp.exp(own), rows) * state + block[:used]
        log = log + own
    tail = log_tile(log, in_ref.shape[1] - used)
    whole = jnp.concatenate([state, tail], axis=0).astype(BF16)
    for j in range(total_ref.shape[0]):
        total_ref[j] = whole


def combine_kernel(heads, in_ref, before_ref, factor_ref, out_ref):
    used = before_ref.shape[1]
    rows = used // heads
    me = lax.axis_index("y")
    state = jnp.zeros((used, Q), F32)
    for g in range(in_ref.shape[0] - 1):
        block = in_ref[g].astype(F32)
        moved = spread(jnp.exp(read_logs(block, heads, used)), rows) * state + block[:used]
        state = jnp.where(g < me, moved, state)
    for i in range(before_ref.shape[0]):
        out_ref[i] = (before_ref[i] + factor_ref[i] * state).astype(BF16)


def ranks(flag_ref):
    chunks = flag_ref.shape[0]
    flags = flag_ref[...].astype(F32)
    within = dot(flags.astype(BF16), below((Q, Q)))
    sums = jnp.broadcast_to(within[:, Q - 1 : Q], (chunks, Q)).astype(BF16)
    earlier = dot(below((chunks, chunks), strict=True).T, sums)
    return jnp.where(flags > 0.0, within + earlier, 0.0) - 1.0


def fill_pick(pick, flag_ref):
    rank = ranks(flag_ref)
    slot = lax.broadcasted_iota(jnp.int32, (Q, Q), 0).astype(F32)
    for g in range(pick.shape[0] // Q):
        for c in range(flag_ref.shape[0]):
            hit = (rank[c : c + 1] - float(g * Q)) == slot
            pick[g * Q : (g + 1) * Q, c * Q : (c + 1) * Q] = jnp.where(hit, 1.0, 0.0).astype(BF16)


def pick_kernel(
    heads,
    gate,
    res,
    out_map,
    decay,
    flags,
    silu_out,
    factor_out,
    rows_out,
    picked_out,
    cums,
    pick,
):
    width = gate.shape[0] // heads
    flag_ref = flags()
    chunks = flag_ref.shape[0]
    fill_pick(pick, flag_ref)
    run_row = dot3(chunk_rows(decay(), heads), below((Q, Q)))
    before = jnp.zeros((heads, 1), F32)
    for c in range(chunks):
        run = run_row[c * heads : (c + 1) * heads]
        for i, piece in enumerate(pieces(run + before)):
            cums[i * 8 : i * 8 + heads, c * Q : (c + 1) * Q] = piece.astype(F32)
        before = before + run[:, Q - 1 : Q]
    log_pieces = cums[...].astype(BF16)
    gate_ref = gate()
    out_map_ref = out_map()
    res_ref = res()
    for g in range(pick.shape[0] // Q):
        these = slice(g * Q, (g + 1) * Q)
        chosen = pick[these]
        at = dot(chosen, gate_ref[...], NT)
        silu_out.ref[these] = at / (1.0 + jnp.exp(-at))
        logs_at = dot(chosen, log_pieces, NT)
        for h in range(heads):
            run = logs_at[:, h : h + 1] + logs_at[:, 8 + h : 9 + h] + logs_at[:, 16 + h : 17 + h]
            factor_out.ref[these, h * width : (h + 1) * width] = jnp.broadcast_to(
                jnp.exp(run), (Q, width)
            )
        rows_out.ref[these] = dot(chosen, out_map_ref[...]).astype(BF16)
        picked_out.ref[these] = dot(chosen, res_ref[...], NT).astype(BF16)
        for out in (silu_out, factor_out, rows_out, picked_out):
            out.send(these)


def ssd_kernel(
    heads,
    skip_ref,
    x,
    in_map,
    out_map,
    step,
    decay,
    flags,
    value_out,
    y_all,
    scaled,
    state,
    pick,
):
    width = x.shape[0] // heads
    flag_ref = flags()
    chunks = flag_ref.shape[0]
    fill_pick(pick, flag_ref)
    row = lax.broadcasted_iota(jnp.int32, (Q, Q), 0)
    col = lax.broadcasted_iota(jnp.int32, (Q, Q), 1)
    mask = row <= col
    logs = chunk_rows(decay(), heads)
    run_row = dot3(logs, below((Q, Q)))
    run_col = dot3r(jnp.where(col <= row, 1.0, 0.0).astype(BF16), logs)
    state[...] = jnp.zeros_like(state)
    step_ref = step()
    in_ref = in_map()
    out_map_ref = out_map()
    x_ref = x()
    for c in range(chunks):
        lanes = slice(c * Q, (c + 1) * Q)
        b = in_ref[lanes, :]
        o = out_map_ref[lanes, :]
        scores = dot(b, o, NT)
        outer = dot(state[...].astype(BF16), o, NT)
        for h in range(heads):
            k = c * heads + h
            part = slice(h * width, (h + 1) * width)
            run = run_row[k : k + 1]
            last = run[:, Q - 1 : Q]
            decay = jnp.where(mask, jnp.exp(run - run_col[:, k : k + 1]), 0.0)
            weights = (scores * decay).astype(BF16)
            xf = x_ref[part, lanes].astype(F32)
            stepped = xf * step_ref[h : h + 1, lanes]
            y = dot(stepped.astype(BF16), weights) + skip_ref[h] * xf
            y_all[part, lanes] = (y + outer[part] * jnp.exp(run)).astype(BF16)
            scaled[part] = (stepped * jnp.exp(last - run)).astype(BF16)
            state[part] = state[part] * jnp.exp(last)
        if c < chunks - 1:
            state[...] += dot(scaled[...], b)
    for g in range(pick.shape[0] // Q):
        these = slice(g * Q, (g + 1) * Q)
        value_out.ref[these] = dot(pick[these], y_all[...], NT)
        value_out.send(these)


def gate_kernel(heads, in_ref, rows, value, factor, silu, picked, out_ref):
    parts = in_ref.shape[0]
    rows_each = in_ref.shape[1] // heads
    per = out_ref.shape[1]
    columns = value.shape[1]
    held = in_ref[...].astype(F32)
    states = [
        held[:, h * rows_each : (h + 1) * rows_each].reshape(parts * rows_each, Q)
        for h in range(heads)
    ]
    incoming = jnp.concatenate(states, axis=0).astype(BF16)
    outer = dot(rows()[...], incoming, NT)
    gated = ((value()[...] + factor()[...] * outer) * silu()[...]).astype(BF16)
    kept = picked()[...]
    for j in range(out_ref.shape[0]):
        these = slice(j * per, (j + 1) * per)
        out_ref[j, :, :columns] = gated[these]
        out_ref[j, :, columns:] = kept[these]


def project_kernel(full_width, in_ref, weight, out_ref, lhs, res):
    groups, per, columns = in_ref.shape
    columns = columns // 2
    squares = jnp.zeros((per, 1), F32)
    for z in range(groups):
        block = in_ref[z]
        own = block[:, :columns]
        lhs[:, z * columns : (z + 1) * columns] = own
        res[:, z * columns : (z + 1) * columns] = block[:, columns:]
        own = own.astype(F32)
        squares = squares + jnp.sum(own * own, axis=1, keepdims=True)
    scale = lax.rsqrt(squares / full_width + 1e-05)
    halves, _, half = weight.shape
    for k in range(halves):
        part = slice(k * half, (k + 1) * half)
        done = dot(lhs[...], weight(k)[...])
        out_ref[:, part] = (done * scale + res[:, part].astype(F32)).astype(BF16)


class Source:
    def __init__(self, hbm, ref, sem, split):
        self.shape = hbm.shape
        if split:
            n = hbm.shape[0]
            self.parts = [ref.at[k] for k in range(n)]
            self.copies = [
                pltpu.make_async_copy(hbm.at[k], ref.at[k], sem.at[k]) for k in range(n)
            ]
        else:
            self.parts = [ref]
            self.copies = [pltpu.make_async_copy(hbm, ref, sem.at[0])]
        for copy in self.copies:
            copy.start()

    def __call__(self, k=0):
        self.copies[k].wait()
        return self.parts[k]


class Target:
    def __init__(self, hbm, ref, sem):
        self.hbm, self.ref, self.sem, self.copies = hbm, ref, sem, []

    def send(self, these):
        k = len(self.copies)
        copy = pltpu.make_async_copy(self.ref.at[these], self.hbm.at[these], self.sem.at[k])
        copy.start()
        self.copies.append(copy)


def call(kernel, outs, args, scratch=(), places="", to="v", name=None, mib=0):
    spaces = {"v": pltpu.VMEM, "s": pltpu.SMEM, "h": pltpu.HBM, "p": pltpu.HBM}
    many = isinstance(outs, (tuple, list))
    results = list(outs) if many else [outs]
    far_in = [i for i, p in enumerate(places) if p in "hp"]
    far_out = [i for i, p in enumerate(to) if p == "h"]
    buffers = [pltpu.VMEM(args[i].shape, args[i].dtype) for i in far_in]
    buffers += [pltpu.VMEM(results[i].shape, results[i].dtype) for i in far_out]
    sems = [
        pltpu.SemaphoreType.DMA((args[i].shape[0] if places[i] == "p" else 1,)) for i in far_in
    ]
    sems += [pltpu.SemaphoreType.DMA((4,)) for _ in far_out]

    def body(*refs):
        ins = list(refs[: len(args)])
        res = list(refs[len(args) : len(args) + len(results)])
        rest = refs[len(args) + len(results) :]
        own = rest[: len(scratch)]
        held = rest[len(scratch) : len(scratch) + len(buffers)]
        flagged = rest[len(scratch) + len(buffers) :]
        for k, i in enumerate(far_in):
            ins[i] = Source(ins[i], held[k], flagged[k], places[i] == "p")
        for k, i in enumerate(far_out):
            res[i] = Target(res[i], held[len(far_in) + k], flagged[len(far_in) + k])
        kernel(*ins, *res, *own)
        for i in far_out:
            for copy in res[i].copies:
                copy.wait()

    out_specs = [pl.BlockSpec(memory_space=spaces[p]) for p in to]
    return pl.pallas_call(
        body,
        out_shape=outs,
        in_specs=[pl.BlockSpec(memory_space=spaces[p]) for p in places],
        out_specs=out_specs if many else out_specs[0],
        scratch_shapes=[*scratch, *buffers, *sems],
        compiler_params=pltpu.CompilerParams(vmem_limit_bytes=mib << 20) if mib else None,
        name=name,
    )(*args)


def on_device(
    head_input,
    gate_input,
    input_map,
    output_map,
    step_size,
    log_decay,
    skip_gain,
    residual,
    boundary,
    norm_gain,
    out_weight,
):
    S = jax.ShapeDtypeStruct
    group = ("x", "core")
    parts = lax.axis_size(group)
    groups = lax.axis_size("y")
    shares = lax.axis_size("head")
    local_width, length = head_input.shape
    heads = step_size.shape[0]
    full_width = out_weight.shape[1]
    slots = length // 4
    per = slots // shares
    used = local_width // parts
    height = used + 8

    held = lax.optimization_barrier
    flags = boundary.reshape(length // Q, Q)

    state = call(
        functools.partial(final_state_kernel, heads, parts),
        S((parts, height, Q), BF16),
        (head_input, input_map, step_size, log_decay),
        [pltpu.VMEM((local_width, length), BF16)],
        places="hhhh",
        name="final_state",
    )
    state, flags, out_weight = held((state, flags, out_weight))
    half = full_width // lax.axis_size("core")
    own = lax.dynamic_slice_in_dim(out_weight, lax.axis_index("core") * half, half, 1)
    own = (own.astype(F32) * norm_gain.astype(F32)[:, None]).astype(BF16)
    weight = lax.all_gather(own[None], ("core", "head"), axis=0, tiled=True)
    weight = weight.reshape(lax.axis_size("core"), shares * local_width, half)
    moved = lax.all_to_all(state, group, 0, 0, tiled=True)
    silu, since, rows, picked = call(
        functools.partial(pick_kernel, heads),
        (
            S((slots, local_width), F32),
            S((slots, local_width), F32),
            S((slots, Q), BF16),
            S((slots, local_width), BF16),
        ),
        (gate_input, residual, output_map, log_decay, flags),
        [pltpu.VMEM((24, length), F32), pltpu.VMEM((slots, length), BF16)],
        places="hhhhh",
        to="hhhh",
        name="pick",
    )
    moved, picked = held((moved, picked))
    before, factor, total = call(
        functools.partial(group_scan_kernel, heads),
        (
            S((parts, used, Q), F32),
            S((parts, used, Q), F32),
            S((groups, height, Q), BF16),
        ),
        (moved,),
        places="v",
        to="vvv",
        name="group_scan",
        mib=2,
    )
    total, flags = held((total, flags))
    totals = lax.all_to_all(total, "y", 0, 0, tiled=True)
    value = call(
        functools.partial(ssd_kernel, heads),
        S((slots, local_width), F32),
        (skip_gain, head_input, input_map, output_map, step_size, log_decay, flags),
        [
            pltpu.VMEM((local_width, length), BF16),
            pltpu.VMEM((local_width, Q), BF16),
            pltpu.VMEM((local_width, Q), F32),
            pltpu.VMEM((slots, length), BF16),
        ],
        places="shhhhhh",
        to="h",
        name="ssd",
    )
    totals, value = held((totals, value))
    incoming = call(
        functools.partial(combine_kernel, heads),
        S((parts, used, Q), BF16),
        (totals, before, factor),
        places="vvv",
        name="combine",
        mib=2,
    )
    incoming = lax.all_to_all(incoming, group, 0, 0, tiled=True)
    gated = call(
        functools.partial(gate_kernel, heads),
        S((shares, per, 2 * local_width), BF16),
        (incoming, rows, value, since, silu, picked),
        places="vhhhhh",
        name="gated",
    )
    gathered = lax.all_to_all(gated, "head", 0, 0, tiled=True)
    return call(
        functools.partial(project_kernel, full_width),
        S((per, full_width), BF16),
        (gathered, weight),
        [pltpu.VMEM((per, full_width), BF16), pltpu.VMEM((per, full_width), BF16)],
        places="vp",
        name="project",
    )


def solution(mesh):
    heads = mesh.shape["head"]
    segs = mesh.shape["seg"]
    core, x = (2, 4) if segs % 8 == 0 else (1, 1)
    if segs == 8:
        x = 2
    fine = Mesh(mesh.devices.reshape(segs // (x * core), x, core, heads), ("y", "x", "core", "head"))
    seg = ("y", "x", "core")
    return jax.shard_map(
        on_device,
        mesh=fine,
        in_specs=(
            P("head", seg),
            P("head", seg),
            P(seg, None),
            P(seg, None),
            P("head", seg),
            P("head", seg),
            P("head"),
            P("head", seg),
            P(seg),
            P("head"),
            P("head", None),
        ),
        out_specs=P((*seg, "head"), None),
        check_vma=False,
    )
```

```python
import functools

import jax
import jax.numpy as jnp
from jax import lax
from jax.experimental import pallas as pl
from jax.experimental.pallas import tpu as pltpu
from jax.sharding import Mesh
from jax.sharding import PartitionSpec as P

F32 = jnp.float32
BF16 = jnp.bfloat16
Q = 128
NT = (((1,), (1,)), ((), ()))
NN = (((1,), (0,)), ((), ()))


def dot(a, b, dims=NN):
    return lax.dot_general(a, b, dims, preferred_element_type=F32)


def pieces(v):
    hi = v.astype(BF16)
    rest = v - hi.astype(F32)
    mid = rest.astype(BF16)
    low = (rest - mid.astype(F32)).astype(BF16)
    return hi, mid, low


def dot3(v, b, dims=NN):
    return sum(dot(p, b, dims) for p in pieces(v))


def dot3r(a, v, dims=NT):
    return sum(dot(a, p, dims) for p in pieces(v))


def below(shape, strict=False):
    i = lax.broadcasted_iota(jnp.int32, shape, 0)
    j = lax.broadcasted_iota(jnp.int32, shape, 1)
    return jnp.where((i < j) if strict else (i <= j), 1.0, 0.0).astype(BF16)


def chunk_rows(ref, heads):
    n = ref.shape[1] // Q
    return jnp.concatenate([ref[:, c * Q : (c + 1) * Q] for c in range(n)], axis=0)


def log_tile(total, rows):
    heads = total.shape[0]
    lane = lax.broadcasted_iota(jnp.int32, (heads, Q), 1)
    hi, mid, low = pieces(jnp.broadcast_to(total, (heads, Q)))
    tile = jnp.where(
        lane == 0,
        hi.astype(F32),
        jnp.where(lane == 1, mid.astype(F32), jnp.where(lane == 2, low.astype(F32), 0.0)),
    )
    return jnp.concatenate([tile, jnp.zeros((rows - heads, Q), F32)], axis=0)


def final_state_kernel(
    heads, parts, gain_ref, weight_hbm, x, in_map, step, decay, out_ref, weight_out, scaled, taken, sem
):
    half = taken.shape[1]
    first = pl.multiple_of(lax.axis_index("core") * half, Q)
    fetch = pltpu.make_async_copy(weight_hbm.at[:, pl.ds(first, half)], taken, sem)
    fetch.start()
    width = x.shape[0] // heads
    length = x.shape[1]
    chunks = length // Q
    rows = width // parts
    logs = chunk_rows(decay(), heads)
    after = lax.broadcasted_iota(jnp.int32, (Q, Q), 0) > lax.broadcasted_iota(
        jnp.int32, (Q, Q), 1
    )
    suffix = dot3(logs, jnp.where(after, 1.0, 0.0).astype(BF16))
    sums = jnp.sum(logs, axis=1, keepdims=True)
    local = taken.shape[0]
    same = lax.broadcasted_iota(jnp.int32, (local, local), 0) == lax.broadcasted_iota(
        jnp.int32, (local, local), 1
    )
    gain = jnp.sum(jnp.where(same, gain_ref[...].astype(F32), 0.0), axis=1, keepdims=True)
    fetch.wait()
    for k in range(4):
        rows_k = slice(k * (local // 4), (k + 1) * (local // 4))
        weight_out.ref[rows_k] = (taken[rows_k].astype(F32) * gain[rows_k]).astype(BF16)
        weight_out.send(rows_k)
    later = jnp.zeros((heads, 1), F32)
    step_ref = step()
    x_ref = x()
    for c in reversed(range(chunks)):
        here = slice(c * heads, (c + 1) * heads)
        lanes = slice(c * Q, (c + 1) * Q)
        factor = step_ref[:, lanes] * jnp.exp(suffix[here] + later)
        for h in range(heads):
            part = slice(h * width, (h + 1) * width)
            scaled[part, lanes] = (x_ref[part, lanes].astype(F32) * factor[h : h + 1]).astype(BF16)
        later = later + sums[here]
    state = dot(scaled[...], in_map()[...])
    tail = log_tile(later, out_ref.shape[1] - heads * rows)
    for j in range(parts):
        own = [state[h * width + j * rows : h * width + (j + 1) * rows] for h in range(heads)]
        out_ref[j] = jnp.concatenate(own + [tail], axis=0).astype(BF16)


def read_logs(block, heads, start):
    sums = jnp.sum(block[start:].astype(F32), axis=1, keepdims=True)
    return sums[:heads]


def spread(column, rows):
    return jnp.concatenate(
        [jnp.broadcast_to(column[h : h + 1], (rows, Q)) for h in range(column.shape[0])], axis=0
    )


def group_scan_kernel(heads, in_ref, before_ref, factor_ref, total_ref):
    parts = in_ref.shape[0]
    used = before_ref.shape[1]
    rows = used // heads
    state = jnp.zeros((used, Q), F32)
    log = jnp.zeros((heads, 1), F32)
    for i in range(parts):
        block = in_ref[i].astype(F32)
        before_ref[i] = state
        factor_ref[i] = spread(jnp.exp(log), rows)
        own = read_logs(block, heads, used)
        state = spread(jnp.exp(own), rows) * state + block[:used]
        log = log + own
    tail = log_tile(log, in_ref.shape[1] - used)
    whole = jnp.concatenate([state, tail], axis=0).astype(BF16)
    for j in range(total_ref.shape[0]):
        total_ref[j] = whole


def combine_kernel(heads, in_ref, before_ref, factor_ref, out_ref):
    used = before_ref.shape[1]
    rows = used // heads
    me = lax.axis_index("y")
    state = jnp.zeros((used, Q), F32)
    for g in range(in_ref.shape[0] - 1):
        block = in_ref[g].astype(F32)
        moved = spread(jnp.exp(read_logs(block, heads, used)), rows) * state + block[:used]
        state = jnp.where(g < me, moved, state)
    for i in range(before_ref.shape[0]):
        out_ref[i] = (before_ref[i] + factor_ref[i] * state).astype(BF16)


def ranks(flag_ref):
    chunks = flag_ref.shape[0]
    flags = flag_ref[...].astype(F32)
    within = dot(flags.astype(BF16), below((Q, Q)))
    sums = jnp.broadcast_to(within[:, Q - 1 : Q], (chunks, Q)).astype(BF16)
    earlier = dot(below((chunks, chunks), strict=True).T, sums)
    return jnp.where(flags > 0.0, within + earlier, 0.0) - 1.0


def fill_pick(pick, flag_ref):
    rank = ranks(flag_ref)
    slot = lax.broadcasted_iota(jnp.int32, (Q, Q), 0).astype(F32)
    for g in range(pick.shape[0] // Q):
        for c in range(flag_ref.shape[0]):
            hit = (rank[c : c + 1] - float(g * Q)) == slot
            pick[g * Q : (g + 1) * Q, c * Q : (c + 1) * Q] = jnp.where(hit, 1.0, 0.0).astype(BF16)


def pick_kernel(heads, gate, res, out_map, decay, flags, picked_out, factor_out, cums, pick):
    local = gate.shape[0]
    flag_ref = flags()
    chunks = flag_ref.shape[0]
    fill_pick(pick, flag_ref)
    run_row = dot3(chunk_rows(decay(), heads), below((Q, Q)))
    before = jnp.zeros((heads, 1), F32)
    for c in range(chunks):
        run = run_row[c * heads : (c + 1) * heads]
        for i, piece in enumerate(pieces(run + before)):
            cums[i * 8 : i * 8 + heads, c * Q : (c + 1) * Q] = piece.astype(F32)
        before = before + run[:, Q - 1 : Q]
    chosen = pick[...]
    logs = dot(chosen, cums[...].astype(BF16), NT)
    logs = logs[:, 0:heads] + logs[:, 8 : 8 + heads] + logs[:, 16 : 16 + heads]
    factor_out.ref[:, 0:heads] = jnp.exp(logs)
    factor_out.send(slice(None))
    ref = picked_out.ref
    ref[:, :local] = dot(chosen, gate()[...], NT).astype(BF16)
    ref[:, local : 2 * local] = dot(chosen, res()[...], NT).astype(BF16)
    ref[:, 2 * local :] = dot(chosen, out_map()[...]).astype(BF16)
    picked_out.send(slice(None))


def ssd_kernel(
    heads,
    skip_ref,
    x,
    in_map,
    out_map,
    step,
    decay,
    flags,
    value_out,
    y_all,
    scaled,
    state,
    pick,
):
    width = x.shape[0] // heads
    flag_ref = flags()
    chunks = flag_ref.shape[0]
    fill_pick(pick, flag_ref)
    row = lax.broadcasted_iota(jnp.int32, (Q, Q), 0)
    col = lax.broadcasted_iota(jnp.int32, (Q, Q), 1)
    mask = row <= col
    logs = chunk_rows(decay(), heads)
    run_row = dot3(logs, below((Q, Q)))
    run_col = dot3r(jnp.where(col <= row, 1.0, 0.0).astype(BF16), logs)
    state[...] = jnp.zeros_like(state)
    step_ref = step()
    in_ref = in_map()
    out_map_ref = out_map()
    x_ref = x()
    for c in range(chunks):
        lanes = slice(c * Q, (c + 1) * Q)
        b = in_ref[lanes, :]
        o = out_map_ref[lanes, :]
        scores = dot(b, o, NT)
        outer = dot(state[...].astype(BF16), o, NT)
        for h in range(heads):
            k = c * heads + h
            part = slice(h * width, (h + 1) * width)
            run = run_row[k : k + 1]
            last = run[:, Q - 1 : Q]
            decay = jnp.where(mask, jnp.exp(run - run_col[:, k : k + 1]), 0.0)
            weights = (scores * decay).astype(BF16)
            xf = x_ref[part, lanes].astype(F32)
            stepped = xf * step_ref[h : h + 1, lanes]
            y = dot(stepped.astype(BF16), weights) + skip_ref[h] * xf
            y_all[part, lanes] = (y + outer[part] * jnp.exp(run)).astype(BF16)
            scaled[part] = (stepped * jnp.exp(last - run)).astype(BF16)
            state[part] = state[part] * jnp.exp(last)
        if c < chunks - 1:
            state[...] += dot(scaled[...], b)
    value_out.ref[...] = dot(pick[...], y_all[...], NT).astype(BF16)
    value_out.send(slice(None))


def gate_kernel(heads, in_ref, picked, factor, value, out_ref):
    parts = in_ref.shape[0]
    rows_each = in_ref.shape[1] // heads
    per = out_ref.shape[1]
    columns = value.shape[1]
    width = columns // heads
    held = in_ref[...].astype(F32)
    states = [
        held[:, h * rows_each : (h + 1) * rows_each].reshape(parts * rows_each, Q)
        for h in range(heads)
    ]
    incoming = jnp.concatenate(states, axis=0).astype(BF16)
    picked_ref = picked()
    outer = dot(picked_ref[:, 2 * columns :], incoming, NT)
    factor_ref = factor()
    value_ref = value()
    for j in range(out_ref.shape[0]):
        these = slice(j * per, (j + 1) * per)
        since = jnp.concatenate(
            [jnp.broadcast_to(factor_ref[these, h : h + 1], (per, width)) for h in range(heads)],
            axis=1,
        )
        gate = picked_ref[these, :columns].astype(F32)
        y = value_ref[these].astype(F32) + since * outer[these]
        out_ref[j, :, :columns] = (y * (gate / (1.0 + jnp.exp(-gate)))).astype(BF16)
        out_ref[j, :, columns:] = picked_ref[these, columns : 2 * columns]


def project_kernel(full_width, in_ref, mine, other, out_ref, lhs, res):
    groups, per, columns = in_ref.shape
    columns = columns // 2
    squares = jnp.zeros((per, 1), F32)
    for z in range(groups):
        block = in_ref[z]
        own = block[:, :columns]
        lhs[:, z * columns : (z + 1) * columns] = own
        res[:, z * columns : (z + 1) * columns] = block[:, columns:]
        own = own.astype(F32)
        squares = squares + jnp.sum(own * own, axis=1, keepdims=True)
    scale = lax.rsqrt(squares / full_width + 1e-05)
    half = mine.shape[1]
    core = lax.axis_index("core")
    for weight, at in ((mine, core), (other, 1 - core)):
        step = half // 2
        for k in range(2):
            columns_k = pl.ds(pl.multiple_of(at * half + k * step, Q), step)
            done = dot(lhs[...], weight[:, k * step : (k + 1) * step])
            out_ref[:, columns_k] = (done * scale + res[:, columns_k].astype(F32)).astype(BF16)


class Source:
    def __init__(self, hbm, ref, sem, split):
        self.shape = hbm.shape
        if split:
            step = hbm.shape[1] // 2
            parts = [(slice(None), slice(k * step, (k + 1) * step)) for k in range(2)]
            self.parts = [ref.at[p] for p in parts]
            self.copies = [
                pltpu.make_async_copy(hbm.at[p], ref.at[p], sem.at[k]) for k, p in enumerate(parts)
            ]
        else:
            self.parts = [ref]
            self.copies = [pltpu.make_async_copy(hbm, ref, sem.at[0])]
        for copy in self.copies:
            copy.start()

    def __call__(self, k=0):
        self.copies[k].wait()
        return self.parts[k]


class Target:
    def __init__(self, hbm, ref, sem):
        self.hbm, self.ref, self.sem, self.copies = hbm, ref, sem, []

    def send(self, these):
        k = len(self.copies)
        copy = pltpu.make_async_copy(self.ref.at[these], self.hbm.at[these], self.sem.at[k])
        copy.start()
        self.copies.append(copy)


def call(kernel, outs, args, scratch=(), places="", to="v", name=None, mib=0):
    spaces = {"v": pltpu.VMEM, "s": pltpu.SMEM, "h": pltpu.HBM, "p": pltpu.HBM, "r": pltpu.HBM}
    many = isinstance(outs, (tuple, list))
    results = list(outs) if many else [outs]
    far_in = [i for i, p in enumerate(places) if p in "hp"]
    far_out = [i for i, p in enumerate(to) if p == "h"]
    buffers = [pltpu.VMEM(args[i].shape, args[i].dtype) for i in far_in]
    buffers += [pltpu.VMEM(results[i].shape, results[i].dtype) for i in far_out]
    sems = [
        pltpu.SemaphoreType.DMA((2,)) for i in far_in
    ]
    sems += [pltpu.SemaphoreType.DMA((4,)) for _ in far_out]

    def body(*refs):
        ins = list(refs[: len(args)])
        res = list(refs[len(args) : len(args) + len(results)])
        rest = refs[len(args) + len(results) :]
        own = rest[: len(scratch)]
        held = rest[len(scratch) : len(scratch) + len(buffers)]
        flagged = rest[len(scratch) + len(buffers) :]
        for k, i in enumerate(far_in):
            ins[i] = Source(ins[i], held[k], flagged[k], places[i] == "p")
        for k, i in enumerate(far_out):
            res[i] = Target(res[i], held[len(far_in) + k], flagged[len(far_in) + k])
        kernel(*ins, *res, *own)
        for i in far_out:
            for copy in res[i].copies:
                copy.wait()

    out_specs = [pl.BlockSpec(memory_space=spaces[p]) for p in to]
    return pl.pallas_call(
        body,
        out_shape=outs,
        in_specs=[pl.BlockSpec(memory_space=spaces[p]) for p in places],
        out_specs=out_specs if many else out_specs[0],
        scratch_shapes=[*scratch, *buffers, *sems],
        compiler_params=pltpu.CompilerParams(vmem_limit_bytes=mib << 20) if mib else None,
        name=name,
    )(*args)


def on_device(
    head_input,
    gate_input,
    input_map,
    output_map,
    step_size,
    log_decay,
    skip_gain,
    residual,
    boundary,
    norm_gain,
    out_weight,
):
    S = jax.ShapeDtypeStruct
    group = ("x", "core")
    parts = lax.axis_size(group)
    groups = lax.axis_size("y")
    shares = lax.axis_size("head")
    local_width, length = head_input.shape
    heads = step_size.shape[0]
    full_width = out_weight.shape[1]
    slots = length // 4
    per = slots // shares
    used = local_width // parts
    height = used + 8

    held = lax.optimization_barrier
    flags = boundary.reshape(length // Q, Q)

    half = full_width // lax.axis_size("core")
    state, scaled = call(
        functools.partial(final_state_kernel, heads, parts),
        (S((parts, height, Q), BF16), S((local_width, half), BF16)),
        (
            norm_gain.reshape(1, local_width),
            out_weight,
            head_input,
            input_map,
            step_size,
            log_decay,
        ),
        [
            pltpu.VMEM((local_width, length), BF16),
            pltpu.VMEM((local_width, half), BF16),
            pltpu.SemaphoreType.DMA,
        ],
        places="vrhhhh",
        to="vh",
        name="final_state",
    )
    state, flags = held((state, flags))
    mine = lax.all_gather(scaled, "head", axis=0, tiled=True)
    moved = lax.all_to_all(state, group, 0, 0, tiled=True)
    picked, since = call(
        functools.partial(pick_kernel, heads),
        (S((slots, 2 * local_width + Q), BF16), S((slots, Q), F32)),
        (gate_input, residual, output_map, log_decay, flags),
        [pltpu.VMEM((24, length), F32), pltpu.VMEM((slots, length), BF16)],
        places="hhhhh",
        to="hh",
        name="pick",
    )
    moved, picked = held((moved, picked))
    before, factor, total = call(
        functools.partial(group_scan_kernel, heads),
        (
            S((parts, used, Q), F32),
            S((parts, used, Q), F32),
            S((groups, height, Q), BF16),
        ),
        (moved,),
        places="v",
        to="vvv",
        name="group_scan",
        mib=2,
    )
    total, flags = held((total, flags))
    totals = lax.all_to_all(total, "y", 0, 0, tiled=True)
    value = call(
        functools.partial(ssd_kernel, heads),
        S((slots, local_width), BF16),
        (skip_gain, head_input, input_map, output_map, step_size, log_decay, flags),
        [
            pltpu.VMEM((local_width, length), BF16),
            pltpu.VMEM((local_width, Q), BF16),
            pltpu.VMEM((local_width, Q), F32),
            pltpu.VMEM((slots, length), BF16),
        ],
        places="shhhhhh",
        to="h",
        name="ssd",
    )
    totals, value = held((totals, value))
    incoming = call(
        functools.partial(combine_kernel, heads),
        S((parts, used, Q), BF16),
        (totals, before, factor),
        places="vvv",
        name="combine",
        mib=2,
    )
    incoming = lax.all_to_all(incoming, group, 0, 0, tiled=True)
    gated = call(
        functools.partial(gate_kernel, heads),
        S((shares, per, 2 * local_width), BF16),
        (incoming, picked, since, value),
        places="vhhh",
        name="gated",
    )
    gated, mine = held((gated, mine))
    cores = lax.axis_size("core")
    other = lax.ppermute(mine, "core", [(c, cores - 1 - c) for c in range(cores)])
    gathered = lax.all_to_all(gated, "head", 0, 0, tiled=True)
    return call(
        functools.partial(project_kernel, full_width),
        S((per, full_width), BF16),
        (gathered, mine, other),
        [pltpu.VMEM((per, full_width), BF16), pltpu.VMEM((per, full_width), BF16)],
        places="vvv",
        name="project",
        mib=8,
    )


def solution(mesh):
    heads = mesh.shape["head"]
    segs = mesh.shape["seg"]
    core, x = (2, 4) if segs % 8 == 0 else (1, 1)
    if segs == 8:
        x = 2
    fine = Mesh(mesh.devices.reshape(segs // (x * core), x, core, heads), ("y", "x", "core", "head"))
    seg = ("y", "x", "core")
    return jax.shard_map(
        on_device,
        mesh=fine,
        in_specs=(
            P("head", seg),
            P("head", seg),
            P(seg, None),
            P(seg, None),
            P("head", seg),
            P("head", seg),
            P("head"),
            P("head", seg),
            P(seg),
            P("head"),
            P("head", None),
        ),
        out_specs=P((*seg, "head"), None),
        check_vma=False,
    )
```

```python
import functools

import jax
import jax.numpy as jnp
from jax import lax
from jax.experimental import pallas as pl
from jax.experimental.pallas import tpu as pltpu
from jax.sharding import Mesh
from jax.sharding import PartitionSpec as P

F32 = jnp.float32
BF16 = jnp.bfloat16
Q = 128
NT = (((1,), (1,)), ((), ()))
NN = (((1,), (0,)), ((), ()))


def dot(a, b, dims=NN):
    return lax.dot_general(a, b, dims, preferred_element_type=F32)


def pieces(v):
    hi = v.astype(BF16)
    rest = v - hi.astype(F32)
    mid = rest.astype(BF16)
    low = (rest - mid.astype(F32)).astype(BF16)
    return hi, mid, low


def dot3(v, b, dims=NN):
    return sum(dot(p, b, dims) for p in pieces(v))


def dot3r(a, v, dims=NT):
    return sum(dot(a, p, dims) for p in pieces(v))


def below(shape, strict=False):
    i = lax.broadcasted_iota(jnp.int32, shape, 0)
    j = lax.broadcasted_iota(jnp.int32, shape, 1)
    return jnp.where((i < j) if strict else (i <= j), 1.0, 0.0).astype(BF16)


def chunk_rows(ref, heads):
    n = ref.shape[1] // Q
    return jnp.concatenate([ref[:, c * Q : (c + 1) * Q] for c in range(n)], axis=0)


def log_tile(total, rows):
    heads = total.shape[0]
    lane = lax.broadcasted_iota(jnp.int32, (heads, Q), 1)
    hi, mid, low = pieces(jnp.broadcast_to(total, (heads, Q)))
    tile = jnp.where(
        lane == 0,
        hi.astype(F32),
        jnp.where(lane == 1, mid.astype(F32), jnp.where(lane == 2, low.astype(F32), 0.0)),
    )
    return jnp.concatenate([tile, jnp.zeros((rows - heads, Q), F32)], axis=0)


def final_state_kernel(heads, parts, x, in_map, step, decay, out_ref, scaled):
    width = x.shape[0] // heads
    length = x.shape[1]
    chunks = length // Q
    rows = width // parts
    logs = chunk_rows(decay(), heads)
    after = lax.broadcasted_iota(jnp.int32, (Q, Q), 0) > lax.broadcasted_iota(
        jnp.int32, (Q, Q), 1
    )
    suffix = dot3(logs, jnp.where(after, 1.0, 0.0).astype(BF16))
    sums = jnp.sum(logs, axis=1, keepdims=True)
    later = jnp.zeros((heads, 1), F32)
    step_ref = step()
    x_ref = x()
    for c in reversed(range(chunks)):
        here = slice(c * heads, (c + 1) * heads)
        lanes = slice(c * Q, (c + 1) * Q)
        factor = step_ref[:, lanes] * jnp.exp(suffix[here] + later)
        for h in range(heads):
            part = slice(h * width, (h + 1) * width)
            scaled[part, lanes] = (x_ref[part, lanes].astype(F32) * factor[h : h + 1]).astype(BF16)
        later = later + sums[here]
    state = dot(scaled[...], in_map()[...])
    tail = log_tile(later, out_ref.shape[1] - heads * rows)
    for j in range(parts):
        own = [state[h * width + j * rows : h * width + (j + 1) * rows] for h in range(heads)]
        out_ref[j] = jnp.concatenate(own + [tail], axis=0).astype(BF16)


def read_logs(block, heads, start):
    sums = jnp.sum(block[start:].astype(F32), axis=1, keepdims=True)
    return sums[:heads]


def spread(column, rows):
    return jnp.concatenate(
        [jnp.broadcast_to(column[h : h + 1], (rows, Q)) for h in range(column.shape[0])], axis=0
    )


def group_scan_kernel(heads, in_ref, total_ref):
    used = in_ref.shape[1] - 8
    rows = used // heads
    state = jnp.zeros((used, Q), F32)
    log = jnp.zeros((heads, 1), F32)
    for i in range(in_ref.shape[0]):
        block = in_ref[i].astype(F32)
        own = read_logs(block, heads, used)
        state = spread(jnp.exp(own), rows) * state + block[:used]
        log = log + own
    tail = log_tile(log, 8)
    whole = jnp.concatenate([state, tail], axis=0).astype(BF16)
    for j in range(total_ref.shape[0]):
        total_ref[j] = whole


def combine_kernel(heads, in_ref, own_ref, out_ref):
    used = out_ref.shape[1]
    rows = used // heads
    me = lax.axis_index("y")
    state = jnp.zeros((used, Q), F32)
    for g in range(in_ref.shape[0] - 1):
        block = in_ref[g].astype(F32)
        moved = spread(jnp.exp(read_logs(block, heads, used)), rows) * state + block[:used]
        state = jnp.where(g < me, moved, state)
    for i in range(own_ref.shape[0]):
        out_ref[i] = state.astype(BF16)
        block = own_ref[i].astype(F32)
        state = spread(jnp.exp(read_logs(block, heads, used)), rows) * state + block[:used]


def ranks(flag_ref):
    chunks = flag_ref.shape[0]
    flags = flag_ref[...].astype(F32)
    within = dot(flags.astype(BF16), below((Q, Q)))
    sums = jnp.broadcast_to(within[:, Q - 1 : Q], (chunks, Q)).astype(BF16)
    earlier = dot(below((chunks, chunks), strict=True).T, sums)
    return jnp.where(flags > 0.0, within + earlier, 0.0) - 1.0


def fill_pick(pick, flag_ref):
    rank = ranks(flag_ref)
    slot = lax.broadcasted_iota(jnp.int32, (Q, Q), 0).astype(F32)
    for g in range(pick.shape[0] // Q):
        for c in range(flag_ref.shape[0]):
            hit = (rank[c : c + 1] - float(g * Q)) == slot
            pick[g * Q : (g + 1) * Q, c * Q : (c + 1) * Q] = jnp.where(hit, 1.0, 0.0).astype(BF16)


def pick_kernel(
    heads, gate, res, out_map, decay, flags, gate_out, res_out, rows_out, factor_out, cums, pick
):
    flag_ref = flags()
    chunks = flag_ref.shape[0]
    fill_pick(pick, flag_ref)
    run_row = dot3(chunk_rows(decay(), heads), below((Q, Q)))
    before = jnp.zeros((heads, 1), F32)
    for c in range(chunks):
        run = run_row[c * heads : (c + 1) * heads]
        for i, piece in enumerate(pieces(run + before)):
            cums[i * 8 : i * 8 + heads, c * Q : (c + 1) * Q] = piece.astype(F32)
        before = before + run[:, Q - 1 : Q]
    log_pieces = cums[...].astype(BF16)
    gate_ref = gate()
    res_ref = res()
    map_ref = out_map()
    for g in range(pick.shape[0] // Q):
        these = slice(g * Q, (g + 1) * Q)
        chosen = pick[these]
        logs = dot(chosen, log_pieces, NT)
        logs = logs[:, 0:heads] + logs[:, 8 : 8 + heads] + logs[:, 16 : 16 + heads]
        factor_out.ref[these, 0:heads] = jnp.exp(logs)
        gate_out.ref[these] = dot(chosen, gate_ref[...], NT).astype(BF16)
        res_out.ref[these] = dot(chosen, res_ref[...], NT).astype(BF16)
        rows_out.ref[these] = dot(chosen, map_ref[...]).astype(BF16)
        for out in (factor_out, gate_out, res_out, rows_out):
            out.send(these)


def ssd_kernel(
    heads,
    skip_ref,
    x,
    in_map,
    out_map,
    step,
    decay,
    flags,
    value_ref,
    y_all,
    scaled,
    state,
    pick,
):
    width = x.shape[0] // heads
    flag_ref = flags()
    chunks = flag_ref.shape[0]
    fill_pick(pick, flag_ref)
    row = lax.broadcasted_iota(jnp.int32, (Q, Q), 0)
    col = lax.broadcasted_iota(jnp.int32, (Q, Q), 1)
    mask = row <= col
    logs = chunk_rows(decay(), heads)
    run_row = dot3(logs, below((Q, Q)))
    run_col = dot3r(jnp.where(col <= row, 1.0, 0.0).astype(BF16), logs)
    state[...] = jnp.zeros_like(state)
    step_ref = step()
    in_ref = in_map()
    out_map_ref = out_map()
    x_ref = x()
    for c in range(chunks):
        lanes = slice(c * Q, (c + 1) * Q)
        b = in_ref[lanes, :]
        o = out_map_ref[lanes, :]
        scores = dot(b, o, NT)
        outer = dot(state[...].astype(BF16), o, NT)
        for h in range(heads):
            k = c * heads + h
            part = slice(h * width, (h + 1) * width)
            run = run_row[k : k + 1]
            last = run[:, Q - 1 : Q]
            decay = jnp.where(mask, jnp.exp(run - run_col[:, k : k + 1]), 0.0)
            weights = (scores * decay).astype(BF16)
            xf = x_ref[part, lanes].astype(F32)
            stepped = xf * step_ref[h : h + 1, lanes]
            y = dot(stepped.astype(BF16), weights) + skip_ref[h] * xf
            y_all[part, lanes] = (y + outer[part] * jnp.exp(run)).astype(BF16)
            scaled[part] = (stepped * jnp.exp(last - run)).astype(BF16)
            state[part] = state[part] * jnp.exp(last)
        if c < chunks - 1:
            state[...] += dot(scaled[...], b)
    for g in range(pick.shape[0] // Q):
        these = slice(g * Q, (g + 1) * Q)
        value_ref[these] = dot(pick[these], y_all[...], NT).astype(BF16)


def gate_kernel(heads, in_ref, value_ref, gain_ref, gate, res, rows, factor, out):
    parts = in_ref.shape[0]
    rows_each = in_ref.shape[1] // heads
    columns = value_ref.shape[1]
    width = columns // heads
    out_ref = out.ref
    per = out_ref.shape[1] - 8
    held = in_ref[...].astype(F32)
    states = [
        held[:, h * rows_each : (h + 1) * rows_each].reshape(parts * rows_each, Q)
        for h in range(heads)
    ]
    incoming = jnp.concatenate(states, axis=0).astype(BF16)
    gain = gain_ref[...].astype(F32)
    ones = jnp.ones((8, columns), BF16)
    row = lax.broadcasted_iota(jnp.int32, (8, per), 0)
    outer = dot(rows()[...], incoming, NT)
    factor_ref = factor()
    gate_ref = gate()
    res_ref = res()
    for j in range(out_ref.shape[0]):
        these = slice(j * per, (j + 1) * per)
        since = jnp.concatenate(
            [jnp.broadcast_to(factor_ref[these, h : h + 1], (per, width)) for h in range(heads)],
            axis=1,
        )
        at = gate_ref[these].astype(F32)
        y = value_ref[these].astype(F32) + since * outer[these]
        gated = y * (at / (1.0 + jnp.exp(-at)))
        out_ref[j, :per, :columns] = (gated * gain).astype(BF16)
        out_ref[j, :per, columns:] = res_ref[these]
        squares = dot3r(ones, gated * gated)
        hi, mid, low = pieces(squares)
        stacked = jnp.where(
            row == 0, hi.astype(F32), jnp.where(row == 1, mid.astype(F32), low.astype(F32))
        )
        stacked = jnp.where(row < 3, stacked, 0.0)
        tail = jnp.concatenate([stacked, jnp.zeros((8, 2 * columns - per), F32)], axis=1)
        out_ref[j, per:, :] = tail.astype(BF16)
        out.send(j)


def project_kernel(full_width, in_ref, *refs):
    groups, tall, columns = in_ref.shape
    per = tall - 8
    columns = columns // 2
    blocks, (out_ref, res, acc) = refs[:-3], refs[-3:]
    me = lax.axis_index("head")
    half = full_width // 2
    total = jnp.zeros((1, per), F32)
    for z in range(groups):
        res[:, z * columns : (z + 1) * columns] = in_ref[z, :per, columns:]
        sums = in_ref[z, per:, :].astype(F32)
        total = total + jnp.sum(sums, axis=0, keepdims=True)[:, :per]
    same = lax.broadcasted_iota(jnp.int32, (per, per), 0) == lax.broadcasted_iota(
        jnp.int32, (per, per), 1
    )
    squares = jnp.sum(jnp.where(same, total, 0.0), axis=1, keepdims=True)
    scale = lax.rsqrt(squares / full_width + 1e-05)
    far = groups // 2
    order = [0]
    for k in range(1, far):
        order += [k, -k]
    for i, k in enumerate(order):
        own = in_ref[lax.rem(me + (groups - k), groups), :per, :columns]
        done = dot(own, blocks[i]()[...])
        if i == 0:
            acc[...] = done
        else:
            acc[...] += done
    own = in_ref[lax.rem(me + far, groups), :per, :columns]
    for i in range(2):
        part = slice(i * half, (i + 1) * half)
        done = acc[:, part] + dot(own, blocks[len(order) + i]()[...])
        out_ref[:, part] = (done * scale + res[:, part].astype(F32)).astype(BF16)


class Source:
    def __init__(self, hbm, ref, sem, split):
        self.shape = hbm.shape
        if split:
            step = hbm.shape[1] // 2
            parts = [(slice(None), slice(k * step, (k + 1) * step)) for k in range(2)]
            self.parts = [ref.at[p] for p in parts]
            self.copies = [
                pltpu.make_async_copy(hbm.at[p], ref.at[p], sem.at[k]) for k, p in enumerate(parts)
            ]
        else:
            self.parts = [ref]
            self.copies = [pltpu.make_async_copy(hbm, ref, sem.at[0])]
        for copy in self.copies:
            copy.start()

    def __call__(self, k=0):
        self.copies[k].wait()
        return self.parts[k]


class Target:
    def __init__(self, hbm, ref, sem):
        self.hbm, self.ref, self.sem, self.copies = hbm, ref, sem, []

    def send(self, these):
        k = len(self.copies)
        copy = pltpu.make_async_copy(self.ref.at[these], self.hbm.at[these], self.sem.at[k])
        copy.start()
        self.copies.append(copy)


def call(kernel, outs, args, scratch=(), places="", to="v", name=None, mib=0):
    spaces = {"v": pltpu.VMEM, "s": pltpu.SMEM, "h": pltpu.HBM, "p": pltpu.HBM, "r": pltpu.HBM}
    many = isinstance(outs, (tuple, list))
    results = list(outs) if many else [outs]
    far_in = [i for i, p in enumerate(places) if p in "hp"]
    far_out = [i for i, p in enumerate(to) if p == "h"]
    buffers = [pltpu.VMEM(args[i].shape, args[i].dtype) for i in far_in]
    buffers += [pltpu.VMEM(results[i].shape, results[i].dtype) for i in far_out]
    sems = [
        pltpu.SemaphoreType.DMA((2,)) for i in far_in
    ]
    sems += [pltpu.SemaphoreType.DMA((8,)) for _ in far_out]

    def body(*refs):
        ins = list(refs[: len(args)])
        res = list(refs[len(args) : len(args) + len(results)])
        rest = refs[len(args) + len(results) :]
        own = rest[: len(scratch)]
        held = rest[len(scratch) : len(scratch) + len(buffers)]
        flagged = rest[len(scratch) + len(buffers) :]
        for k, i in enumerate(far_in):
            ins[i] = Source(ins[i], held[k], flagged[k], places[i] == "p")
        for k, i in enumerate(far_out):
            res[i] = Target(res[i], held[len(far_in) + k], flagged[len(far_in) + k])
        kernel(*ins, *res, *own)
        for i in far_out:
            for copy in res[i].copies:
                copy.wait()

    out_specs = [pl.BlockSpec(memory_space=spaces[p]) for p in to]
    return pl.pallas_call(
        body,
        out_shape=outs,
        in_specs=[pl.BlockSpec(memory_space=spaces[p]) for p in places],
        out_specs=out_specs if many else out_specs[0],
        scratch_shapes=[*scratch, *buffers, *sems],
        compiler_params=pltpu.CompilerParams(vmem_limit_bytes=mib << 20) if mib else None,
        name=name,
    )(*args)


def on_device(
    head_input,
    gate_input,
    input_map,
    output_map,
    step_size,
    log_decay,
    skip_gain,
    residual,
    boundary,
    norm_gain,
    out_weight,
):
    S = jax.ShapeDtypeStruct
    group = ("x", "core")
    parts = lax.axis_size(group)
    groups = lax.axis_size("y")
    shares = lax.axis_size("head")
    local_width, length = head_input.shape
    heads = step_size.shape[0]
    full_width = out_weight.shape[1]
    slots = length // 4
    per = slots // shares
    used = local_width // parts
    height = used + 8

    held = lax.optimization_barrier
    flags = boundary.reshape(length // Q, Q)

    def shift(block, by):
        return lax.ppermute(block, "head", [(z, (z + by) % shares) for z in range(shares)])

    def step(onward, back):
        return shift(onward, 1), shift(back, -1)

    half = full_width // 2
    ring = []
    onward, back = step(out_weight, out_weight)
    ring += [onward, back]
    state = call(
        functools.partial(final_state_kernel, heads, parts),
        S((parts, height, Q), BF16),
        (head_input, input_map, step_size, log_decay),
        [pltpu.VMEM((local_width, length), BF16)],
        places="hhhh",
        name="final_state",
    )
    state, flags = held((state, flags))
    moved = lax.all_to_all(state, group, 0, 0, tiled=True)
    gate, res, rows, since = call(
        functools.partial(pick_kernel, heads),
        (
            S((slots, local_width), BF16),
            S((slots, local_width), BF16),
            S((slots, Q), BF16),
            S((slots, Q), F32),
        ),
        (gate_input, residual, output_map, log_decay, flags),
        [pltpu.VMEM((24, length), F32), pltpu.VMEM((slots, length), BF16)],
        places="hhhhh",
        to="hhhh",
        name="pick",
    )
    moved, gate, onward, back = held((moved, gate, onward, back))
    total = call(
        functools.partial(group_scan_kernel, heads),
        S((groups, height, Q), BF16),
        (moved,),
        places="v",
        name="group_scan",
        mib=2,
    )
    if shares > 4:
        onward, back = step(onward, back)
        ring += [onward, back]
    total, flags = held((total, flags))
    totals = lax.all_to_all(total, "y", 0, 0, tiled=True)
    value = call(
        functools.partial(ssd_kernel, heads),
        S((slots, local_width), BF16),
        (skip_gain, head_input, input_map, output_map, step_size, log_decay, flags),
        [
            pltpu.VMEM((local_width, length), BF16),
            pltpu.VMEM((local_width, Q), BF16),
            pltpu.VMEM((local_width, Q), F32),
            pltpu.VMEM((slots, length), BF16),
        ],
        places="shhhhhh",
        name="ssd",
    )
    totals, value, onward, back = held((totals, value, onward, back))
    incoming = call(
        functools.partial(combine_kernel, heads),
        S((parts, used, Q), BF16),
        (totals, moved),
        places="vv",
        name="combine",
        mib=2,
    )
    if shares > 4:
        onward, back = step(onward, back)
        ring += [onward, back]
    incoming = lax.all_to_all(incoming, group, 0, 0, tiled=True)
    gated = call(
        functools.partial(gate_kernel, heads),
        S((shares, per + 8, 2 * local_width), BF16),
        (incoming, value, norm_gain.reshape(1, local_width), gate, res, rows, since),
        places="vvvhhhh",
        to="h",
        name="gated",
    )
    gated, onward, back = held((gated, onward, back))
    last = (shift(onward[:, :half], 1), shift(back[:, half:], -1))
    gathered = lax.all_to_all(gated, "head", 0, 0, tiled=True)
    blocks = (out_weight, *ring[: shares - 2], *last)
    return call(
        functools.partial(project_kernel, full_width),
        S((per, full_width), BF16),
        (gathered, *blocks),
        [pltpu.VMEM((per, full_width), BF16), pltpu.VMEM((per, full_width), F32)],
        places="v" + "h" * len(blocks),
        name="project",
    )


def solution(mesh):
    heads = mesh.shape["head"]
    segs = mesh.shape["seg"]
    core, x = (2, 4) if segs % 8 == 0 else (1, 1)
    if segs == 8:
        x = 2
    fine = Mesh(mesh.devices.reshape(segs // (x * core), x, core, heads), ("y", "x", "core", "head"))
    seg = ("y", "x", "core")
    return jax.shard_map(
        on_device,
        mesh=fine,
        in_specs=(
            P("head", seg),
            P("head", seg),
            P(seg, None),
            P(seg, None),
            P("head", seg),
            P("head", seg),
            P("head"),
            P("head", seg),
            P(seg),
            P("head"),
            P("head", None),
        ),
        out_specs=P((*seg, "head"), None),
        check_vma=False,
    )
```

```python
import functools

import jax
import jax.numpy as jnp
from jax import lax
from jax.experimental import pallas as pl
from jax.experimental.pallas import tpu as pltpu
from jax.sharding import Mesh
from jax.sharding import PartitionSpec as P

F32 = jnp.float32
BF16 = jnp.bfloat16
PARTS = 4
Q = 128
NT = (((1,), (1,)), ((), ()))
NN = (((1,), (0,)), ((), ()))


def dot(a, b, dims=NN):
    return lax.dot_general(a, b, dims, preferred_element_type=F32)


def pieces(v):
    hi = v.astype(BF16)
    rest = v - hi.astype(F32)
    mid = rest.astype(BF16)
    low = (rest - mid.astype(F32)).astype(BF16)
    return hi, mid, low


def dot3(v, b, dims=NN):
    return sum(dot(p, b, dims) for p in pieces(v))


def dot3r(a, v, dims=NT):
    return sum(dot(a, p, dims) for p in pieces(v))


def below(shape, strict=False):
    i = lax.broadcasted_iota(jnp.int32, shape, 0)
    j = lax.broadcasted_iota(jnp.int32, shape, 1)
    return jnp.where((i < j) if strict else (i <= j), 1.0, 0.0).astype(BF16)


def chunk_rows(ref, heads):
    n = ref.shape[1] // Q
    return jnp.concatenate([ref[:, c * Q : (c + 1) * Q] for c in range(n)], axis=0)


def log_tile(total, rows):
    heads = total.shape[0]
    lane = lax.broadcasted_iota(jnp.int32, (heads, Q), 1)
    hi, mid, low = pieces(jnp.broadcast_to(total, (heads, Q)))
    tile = jnp.where(
        lane == 0,
        hi.astype(F32),
        jnp.where(lane == 1, mid.astype(F32), jnp.where(lane == 2, low.astype(F32), 0.0)),
    )
    return jnp.concatenate([tile, jnp.zeros((rows - heads, Q), F32)], axis=0)


def final_state_kernel(heads, parts, x, in_map, step, decay, out_ref, scaled):
    width = x.shape[0] // heads
    length = x.shape[1]
    chunks = length // Q
    rows = width // parts
    logs = chunk_rows(decay(), heads)
    after = lax.broadcasted_iota(jnp.int32, (Q, Q), 0) > lax.broadcasted_iota(
        jnp.int32, (Q, Q), 1
    )
    suffix = dot3(logs, jnp.where(after, 1.0, 0.0).astype(BF16))
    sums = jnp.sum(logs, axis=1, keepdims=True)
    later = [jnp.zeros((heads, 1), F32)]
    for c in reversed(range(chunks)):
        later.insert(0, later[0] + sums[c * heads : (c + 1) * heads])
    step_ref = step()
    state = jnp.zeros((x.shape[0], Q), F32)
    every = chunks // PARTS
    for c in range(chunks):
        if c % every == 0:
            x_ref = x(c // every)
        lanes = slice(c * Q, (c + 1) * Q)
        factor = step_ref[:, lanes] * jnp.exp(suffix[c * heads : (c + 1) * heads] + later[c + 1])
        for h in range(heads):
            part = slice(h * width, (h + 1) * width)
            scaled[part, lanes] = (x_ref[part, lanes].astype(F32) * factor[h : h + 1]).astype(BF16)
        if c % every == every - 1:
            span = slice((c + 1 - every) * Q, (c + 1) * Q)
            state = state + dot(scaled[:, span], in_map(c // every)[span, :])
    tail = log_tile(later[0], out_ref.shape[1] - heads * rows)
    for j in range(parts):
        own = [state[h * width + j * rows : h * width + (j + 1) * rows] for h in range(heads)]
        out_ref[j] = jnp.concatenate(own + [tail], axis=0).astype(BF16)


def read_logs(block, heads, start):
    sums = jnp.sum(block[start:].astype(F32), axis=1, keepdims=True)
    return sums[:heads]


def spread(column, rows):
    return jnp.concatenate(
        [jnp.broadcast_to(column[h : h + 1], (rows, Q)) for h in range(column.shape[0])], axis=0
    )


def group_scan_kernel(heads, in_ref, total_ref):
    used = in_ref.shape[1] - 8
    rows = used // heads
    state = jnp.zeros((used, Q), F32)
    log = jnp.zeros((heads, 1), F32)
    for i in range(in_ref.shape[0]):
        block = in_ref[i].astype(F32)
        own = read_logs(block, heads, used)
        state = spread(jnp.exp(own), rows) * state + block[:used]
        log = log + own
    tail = log_tile(log, 8)
    whole = jnp.concatenate([state, tail], axis=0).astype(BF16)
    for j in range(total_ref.shape[0]):
        total_ref[j] = whole


def combine_kernel(heads, in_ref, own_ref, out_ref):
    used = out_ref.shape[1]
    rows = used // heads
    me = lax.axis_index("y")
    state = jnp.zeros((used, Q), F32)
    for g in range(in_ref.shape[0] - 1):
        block = in_ref[g].astype(F32)
        moved = spread(jnp.exp(read_logs(block, heads, used)), rows) * state + block[:used]
        state = jnp.where(g < me, moved, state)
    for i in range(own_ref.shape[0]):
        out_ref[i] = state.astype(BF16)
        block = own_ref[i].astype(F32)
        state = spread(jnp.exp(read_logs(block, heads, used)), rows) * state + block[:used]


def ranks(flag_ref):
    chunks = flag_ref.shape[0]
    flags = flag_ref[...].astype(F32)
    within = dot(flags.astype(BF16), below((Q, Q)))
    sums = jnp.broadcast_to(within[:, Q - 1 : Q], (chunks, Q)).astype(BF16)
    earlier = dot(below((chunks, chunks), strict=True).T, sums)
    return jnp.where(flags > 0.0, within + earlier, 0.0) - 1.0


def fill_pick(pick, flag_ref):
    rank = ranks(flag_ref)
    slot = lax.broadcasted_iota(jnp.int32, (Q, Q), 0).astype(F32)
    for g in range(pick.shape[0] // Q):
        for c in range(flag_ref.shape[0]):
            hit = (rank[c : c + 1] - float(g * Q)) == slot
            pick[g * Q : (g + 1) * Q, c * Q : (c + 1) * Q] = jnp.where(hit, 1.0, 0.0).astype(BF16)


def pick_kernel(heads, gate, res, out_map, decay, flags, gate_out, res_out, rows_out, cums, pick):
    columns = gate.shape[0]
    flag_ref = flags()
    chunks = flag_ref.shape[0]
    fill_pick(pick, flag_ref)
    run_row = dot3(chunk_rows(decay(), heads), below((Q, Q)))
    before = jnp.zeros((heads, 1), F32)
    for c in range(chunks):
        run = run_row[c * heads : (c + 1) * heads]
        for i, piece in enumerate(pieces(run + before)):
            cums[i * 8 : i * 8 + heads, c * Q : (c + 1) * Q] = piece.astype(F32)
        before = before + run[:, Q - 1 : Q]
    log_pieces = cums[...].astype(BF16)
    blocks = [slice(g * Q, (g + 1) * Q) for g in range(pick.shape[0] // Q)]
    gate_ref = gate()
    for these in blocks:
        logs = dot(pick[these], log_pieces, NT)
        logs = logs[:, 0:heads] + logs[:, 8 : 8 + heads] + logs[:, 16 : 16 + heads]
        for i, piece in enumerate(pieces(jnp.exp(logs))):
            gate_out.ref[these, columns + i * heads : columns + (i + 1) * heads] = piece
        gate_out.ref[these, :columns] = dot(pick[these], gate_ref[...], NT).astype(BF16)
        gate_out.send(these)
    map_ref = out_map()
    for these in blocks:
        rows_out.ref[these] = dot(pick[these], map_ref[...]).astype(BF16)
        rows_out.send(these)
    res_ref = res()
    for these in blocks:
        res_out.ref[these] = dot(pick[these], res_ref[...], NT).astype(BF16)
        res_out.send(these)


def ssd_kernel(
    heads,
    skip_ref,
    x,
    in_map,
    out_map,
    step,
    decay,
    flags,
    value_ref,
    y_all,
    stepped,
    starts,
    pick,
):
    width = x.shape[0] // heads
    flag_ref = flags()
    chunks = flag_ref.shape[0]
    fill_pick(pick, flag_ref)
    row = lax.broadcasted_iota(jnp.int32, (Q, Q), 0)
    col = lax.broadcasted_iota(jnp.int32, (Q, Q), 1)
    mask = row <= col
    logs = chunk_rows(decay(), heads)
    run_row = dot3(logs, below((Q, Q)))
    run_col = dot3r(jnp.where(col <= row, 1.0, 0.0).astype(BF16), logs)
    step_ref = step()
    every = chunks // PARTS
    state = jnp.zeros((heads * width, Q), F32)
    for c in range(chunks):
        lanes = slice(c * Q, (c + 1) * Q)
        if c % every == 0:
            x_ref = x(c // every)
            in_ref = in_map(c // every)
        starts[c] = state.astype(BF16)
        scaled = []
        for h in range(heads):
            part = slice(h * width, (h + 1) * width)
            run = run_row[c * heads + h : c * heads + h + 1]
            moved = x_ref[part, lanes].astype(F32) * step_ref[h : h + 1, lanes]
            stepped[part, lanes] = moved.astype(BF16)
            scaled.append((moved * jnp.exp(run[:, Q - 1 : Q] - run)).astype(BF16))
        last = run_row[c * heads : (c + 1) * heads, Q - 1 : Q]
        state = spread(jnp.exp(last), width) * state + dot(
            jnp.concatenate(scaled, axis=0), in_ref[lanes, :]
        )
    for c in range(chunks):
        lanes = slice(c * Q, (c + 1) * Q)
        if c % every == 0:
            out_map_ref = out_map(c // every)
        o = out_map_ref[lanes, :]
        scores = dot(in_ref[lanes, :], o, NT)
        outer = dot(starts[c], o, NT)
        for h in range(heads):
            k = c * heads + h
            part = slice(h * width, (h + 1) * width)
            run = run_row[k : k + 1]
            decayed = jnp.where(mask, jnp.exp(run - run_col[:, k : k + 1]), 0.0)
            weights = (scores * decayed).astype(BF16)
            y = dot(stepped[part, lanes], weights) + outer[part] * jnp.exp(run)
            y = y + skip_ref[h] * x_ref[part, lanes].astype(F32)
            y_all[part, lanes] = y.astype(BF16)
    for g in range(pick.shape[0] // Q):
        these = slice(g * Q, (g + 1) * Q)
        value_ref[these] = dot(pick[these], y_all[...], NT).astype(BF16)


def gate_kernel(heads, in_ref, value_ref, gain_ref, rows, gate, res, out):
    parts = in_ref.shape[0]
    rows_each = in_ref.shape[1] // heads
    columns = value_ref.shape[1]
    width = columns // heads
    out_ref = out.ref
    per = out_ref.shape[1] - 8
    held = in_ref[...].astype(F32)
    states = [
        held[:, h * rows_each : (h + 1) * rows_each].reshape(parts * rows_each, Q)
        for h in range(heads)
    ]
    incoming = jnp.concatenate(states, axis=0).astype(BF16)
    gain = gain_ref[...].astype(F32)
    ones = jnp.ones((8, columns), BF16)
    row = lax.broadcasted_iota(jnp.int32, (8, per), 0)
    outer = dot(rows()[...], incoming, NT)
    gate_ref = gate()
    res_ref = res()
    for j in range(out_ref.shape[0]):
        these = slice(j * per, (j + 1) * per)
        decay = gate_ref[these, columns:].astype(F32)
        decay = decay[:, :heads] + decay[:, heads : 2 * heads] + decay[:, 2 * heads : 3 * heads]
        since = jnp.concatenate(
            [jnp.broadcast_to(decay[:, h : h + 1], (per, width)) for h in range(heads)], axis=1
        )
        at = gate_ref[these, :columns].astype(F32)
        y = value_ref[these].astype(F32) + since * outer[these]
        gated = y * (at / (1.0 + jnp.exp(-at)))
        out_ref[j, :per, :columns] = (gated * gain).astype(BF16)
        out_ref[j, :per, columns:] = res_ref[these]
        squares = dot3r(ones, gated * gated)
        hi, mid, low = pieces(squares)
        stacked = jnp.where(
            row == 0, hi.astype(F32), jnp.where(row == 1, mid.astype(F32), low.astype(F32))
        )
        stacked = jnp.where(row < 3, stacked, 0.0)
        tail = jnp.concatenate([stacked, jnp.zeros((8, 2 * columns - per), F32)], axis=1)
        out_ref[j, per:, :] = tail.astype(BF16)
        out.send(j)


def project_kernel(full_width, in_ref, weight, out_ref, lhs, res):
    groups, tall, columns = in_ref.shape
    per = tall - 8
    columns = columns // 2
    total = jnp.zeros((1, per), F32)
    for z in range(groups):
        lhs[:, z * columns : (z + 1) * columns] = in_ref[z, :per, :columns]
        res[:, z * columns : (z + 1) * columns] = in_ref[z, :per, columns:]
        sums = in_ref[z, per:, :].astype(F32)
        total = total + jnp.sum(sums, axis=0, keepdims=True)[:, :per]
    same = lax.broadcasted_iota(jnp.int32, (per, per), 0) == lax.broadcasted_iota(
        jnp.int32, (per, per), 1
    )
    squares = jnp.sum(jnp.where(same, total, 0.0), axis=1, keepdims=True)
    scale = lax.rsqrt(squares / full_width + 1e-05)
    planes, depth, half = weight.shape
    step = depth // PARTS
    for n in range(planes):
        part = slice(n * half, (n + 1) * half)
        done = jnp.zeros((per, half), F32)
        for k in range(PARTS):
            span = slice(k * step, (k + 1) * step)
            done = done + dot(lhs[:, span], weight(n * PARTS + k)[n, span])
        out_ref[:, part] = (done * scale + res[:, part].astype(F32)).astype(BF16)


class Source:
    def __init__(self, hbm, ref, sem, split):
        self.shape, self.ref = hbm.shape, ref
        if split == "h":
            parts = [slice(None)]
        elif split == "w":
            step = hbm.shape[1] // PARTS
            parts = [
                (n, slice(k * step, (k + 1) * step)) for n in range(hbm.shape[0]) for k in range(PARTS)
            ]
        else:
            step = hbm.shape[split == "c"] // PARTS
            parts = [slice(k * step, (k + 1) * step) for k in range(PARTS)]
            if split == "c":
                parts = [(slice(None), p) for p in parts]
        self.copies = [
            pltpu.make_async_copy(hbm.at[p], ref.at[p], sem.at[k]) for k, p in enumerate(parts)
        ]

    def start(self, k):
        if k < len(self.copies):
            self.copies[k].start()

    def __call__(self, k=0):
        self.copies[k].wait()
        return self.ref


class Target:
    def __init__(self, hbm, ref, sem):
        self.hbm, self.ref, self.sem, self.copies = hbm, ref, sem, []

    def send(self, these):
        k = len(self.copies)
        copy = pltpu.make_async_copy(self.ref.at[these], self.hbm.at[these], self.sem.at[k])
        copy.start()
        self.copies.append(copy)


def call(kernel, outs, args, scratch=(), places="", to="v", name=None, mib=0):
    spaces = {"v": pltpu.VMEM, "s": pltpu.SMEM}
    many = isinstance(outs, (tuple, list))
    results = list(outs) if many else [outs]
    far_in = [i for i, p in enumerate(places) if p in "hcqw"]
    far_out = [i for i, p in enumerate(to) if p == "h"]
    buffers = [pltpu.VMEM(args[i].shape, args[i].dtype) for i in far_in]
    buffers += [pltpu.VMEM(results[i].shape, results[i].dtype) for i in far_out]
    sems = [pltpu.SemaphoreType.DMA((2 * PARTS,)) for _ in far_in]
    sems += [pltpu.SemaphoreType.DMA((8,)) for _ in far_out]

    def body(*refs):
        ins = list(refs[: len(args)])
        res = list(refs[len(args) : len(args) + len(results)])
        rest = refs[len(args) + len(results) :]
        own = rest[: len(scratch)]
        held = rest[len(scratch) : len(scratch) + len(buffers)]
        flagged = rest[len(scratch) + len(buffers) :]
        for k, i in enumerate(far_in):
            ins[i] = Source(ins[i], held[k], flagged[k], places[i])
        for part in range(2 * PARTS):
            for i in far_in:
                ins[i].start(part)
        for k, i in enumerate(far_out):
            res[i] = Target(res[i], held[len(far_in) + k], flagged[len(far_in) + k])
        kernel(*ins, *res, *own)
        for i in far_out:
            for copy in res[i].copies:
                copy.wait()

    out_specs = [pl.BlockSpec(memory_space=spaces.get(p, pltpu.HBM)) for p in to]
    return pl.pallas_call(
        body,
        out_shape=outs,
        in_specs=[pl.BlockSpec(memory_space=spaces.get(p, pltpu.HBM)) for p in places],
        out_specs=out_specs if many else out_specs[0],
        scratch_shapes=[*scratch, *buffers, *sems],
        compiler_params=pltpu.CompilerParams(vmem_limit_bytes=mib << 20) if mib else None,
        name=name,
    )(*args)


def on_device(
    head_input,
    gate_input,
    input_map,
    output_map,
    step_size,
    log_decay,
    skip_gain,
    residual,
    boundary,
    norm_gain,
    out_weight,
):
    S = jax.ShapeDtypeStruct
    group = ("x", "core")
    parts = lax.axis_size(group)
    groups = lax.axis_size("y")
    shares = lax.axis_size("head")
    local_width, length = head_input.shape
    heads = step_size.shape[0]
    full_width = out_weight.shape[1]
    slots = length // 4
    per = slots // shares
    used = local_width // parts
    height = used + 8

    held = lax.optimization_barrier
    flags = boundary.reshape(length // Q, Q)

    state = call(
        functools.partial(final_state_kernel, heads, parts),
        S((parts, height, Q), BF16),
        (head_input, input_map, step_size, log_decay),
        [pltpu.VMEM((local_width, length), BF16)],
        places="cqhh",
        name="final_state",
    )
    state, out_weight = held((state, out_weight))
    cores = lax.axis_size("core")
    half = full_width // cores
    own = lax.dynamic_slice_in_dim(out_weight, lax.axis_index("core") * half, half, 1)
    weight = lax.all_gather(own[None], ("core", "head"), axis=0, tiled=True)
    moved = lax.all_to_all(state, group, 0, 0, tiled=True)
    total = call(
        functools.partial(group_scan_kernel, heads),
        S((groups, height, Q), BF16),
        (moved,),
        places="v",
        name="group_scan",
        mib=2,
    )
    total, flags = held((total, flags))
    totals = lax.all_to_all(total, "y", 0, 0, tiled=True)
    value = call(
        functools.partial(ssd_kernel, heads),
        S((slots, local_width), BF16),
        (skip_gain, head_input, input_map, output_map, step_size, log_decay, flags),
        [
            pltpu.VMEM((local_width, length), BF16),
            pltpu.VMEM((local_width, length), BF16),
            pltpu.VMEM((length // Q, local_width, Q), BF16),
            pltpu.VMEM((slots, length), BF16),
        ],
        places="scqqhhh",
        name="ssd",
    )
    totals, value = held((totals, value))
    incoming = call(
        functools.partial(combine_kernel, heads),
        S((parts, used, Q), BF16),
        (totals, moved),
        places="vv",
        name="combine",
        mib=2,
    )
    incoming, flags = held((incoming, flags))
    incoming = lax.all_to_all(incoming, group, 0, 0, tiled=True)
    wide = -(-(local_width + 3 * heads) // Q) * Q
    gate, res, rows = call(
        functools.partial(pick_kernel, heads),
        (
            S((slots, wide), BF16),
            S((slots, local_width), BF16),
            S((slots, Q), BF16),
        ),
        (gate_input, residual, output_map, log_decay, flags),
        [pltpu.VMEM((24, length), F32), pltpu.VMEM((slots, length), BF16)],
        places="hhhhh",
        to="hhh",
        name="pick",
    )
    gated = call(
        functools.partial(gate_kernel, heads),
        S((shares, per + 8, 2 * local_width), BF16),
        (incoming, value, norm_gain.reshape(1, local_width), rows, gate, res),
        places="vvvhhh",
        to="h",
        name="gated",
    )
    gathered = lax.all_to_all(gated, "head", 0, 0, tiled=True)
    weight = weight.reshape(cores, shares * local_width, half)
    return call(
        functools.partial(project_kernel, full_width),
        S((per, full_width), BF16),
        (gathered, weight),
        [pltpu.VMEM((per, full_width), BF16), pltpu.VMEM((per, full_width), BF16)],
        places="vw",
        name="project",
    )


def solution(mesh):
    heads = mesh.shape["head"]
    segs = mesh.shape["seg"]
    core, x = (2, 4) if segs % 8 == 0 else (1, 1)
    if segs == 8:
        x = 2
    fine = Mesh(mesh.devices.reshape(segs // (x * core), x, core, heads), ("y", "x", "core", "head"))
    seg = ("y", "x", "core")
    return jax.shard_map(
        on_device,
        mesh=fine,
        in_specs=(
            P("head", seg),
            P("head", seg),
            P(seg, None),
            P(seg, None),
            P("head", seg),
            P("head", seg),
            P("head"),
            P("head", seg),
            P(seg),
            P("head"),
            P("head", None),
        ),
        out_specs=P((*seg, "head"), None),
        check_vma=False,
    )
```

```python
import functools

import jax
import jax.numpy as jnp
from jax import lax
from jax.experimental import pallas as pl
from jax.experimental.pallas import tpu as pltpu
from jax.sharding import Mesh
from jax.sharding import PartitionSpec as P

F32 = jnp.float32
BF16 = jnp.bfloat16
PARTS = 4
Q = 128
NT = (((1,), (1,)), ((), ()))
NN = (((1,), (0,)), ((), ()))


def dot(a, b, dims=NN):
    return lax.dot_general(a, b, dims, preferred_element_type=F32)


def pieces(v):
    hi = v.astype(BF16)
    rest = v - hi.astype(F32)
    mid = rest.astype(BF16)
    low = (rest - mid.astype(F32)).astype(BF16)
    return hi, mid, low


def dot3(v, b, dims=NN):
    return sum(dot(p, b, dims) for p in pieces(v))


def dot3r(a, v, dims=NT):
    return sum(dot(a, p, dims) for p in pieces(v))


def below(shape, strict=False):
    i = lax.broadcasted_iota(jnp.int32, shape, 0)
    j = lax.broadcasted_iota(jnp.int32, shape, 1)
    return jnp.where((i < j) if strict else (i <= j), 1.0, 0.0).astype(BF16)


def chunk_rows(ref, heads):
    n = ref.shape[1] // Q
    return jnp.concatenate([ref[:, c * Q : (c + 1) * Q] for c in range(n)], axis=0)


def log_tile(total, rows):
    heads = total.shape[0]
    lane = lax.broadcasted_iota(jnp.int32, (heads, Q), 1)
    hi, mid, low = pieces(jnp.broadcast_to(total, (heads, Q)))
    tile = jnp.where(
        lane == 0,
        hi.astype(F32),
        jnp.where(lane == 1, mid.astype(F32), jnp.where(lane == 2, low.astype(F32), 0.0)),
    )
    return jnp.concatenate([tile, jnp.zeros((rows - heads, Q), F32)], axis=0)


def final_state_kernel(heads, parts, x, in_map, step, decay, out_ref, scaled):
    width = x.shape[0] // heads
    length = x.shape[1]
    chunks = length // Q
    rows = width // parts
    logs = chunk_rows(decay(), heads)
    after = lax.broadcasted_iota(jnp.int32, (Q, Q), 0) > lax.broadcasted_iota(
        jnp.int32, (Q, Q), 1
    )
    suffix = dot3(logs, jnp.where(after, 1.0, 0.0).astype(BF16))
    sums = jnp.sum(logs, axis=1, keepdims=True)
    later = jnp.zeros((heads, 1), F32)
    step_ref = step()
    x_ref = x()
    for c in reversed(range(chunks)):
        here = slice(c * heads, (c + 1) * heads)
        lanes = slice(c * Q, (c + 1) * Q)
        factor = step_ref[:, lanes] * jnp.exp(suffix[here] + later)
        for h in range(heads):
            part = slice(h * width, (h + 1) * width)
            scaled[part, lanes] = (x_ref[part, lanes].astype(F32) * factor[h : h + 1]).astype(BF16)
        later = later + sums[here]
    state = dot(scaled[...], in_map()[...])
    tail = log_tile(later, out_ref.shape[1] - heads * rows)
    for j in range(parts):
        own = [state[h * width + j * rows : h * width + (j + 1) * rows] for h in range(heads)]
        out_ref[j] = jnp.concatenate(own + [tail], axis=0).astype(BF16)


def read_logs(block, heads, start):
    sums = jnp.sum(block[start:].astype(F32), axis=1, keepdims=True)
    return sums[:heads]


def spread(column, rows):
    return jnp.concatenate(
        [jnp.broadcast_to(column[h : h + 1], (rows, Q)) for h in range(column.shape[0])], axis=0
    )


def group_scan_kernel(heads, in_ref, total_ref):
    used = in_ref.shape[1] - 8
    rows = used // heads
    state = jnp.zeros((used, Q), F32)
    log = jnp.zeros((heads, 1), F32)
    for i in range(in_ref.shape[0]):
        block = in_ref[i].astype(F32)
        own = read_logs(block, heads, used)
        state = spread(jnp.exp(own), rows) * state + block[:used]
        log = log + own
    tail = log_tile(log, 8)
    whole = jnp.concatenate([state, tail], axis=0).astype(BF16)
    for j in range(total_ref.shape[0]):
        total_ref[j] = whole


def combine_kernel(heads, in_ref, own_ref, out_ref):
    used = out_ref.shape[1]
    rows = used // heads
    me = lax.axis_index("y")
    state = jnp.zeros((used, Q), F32)
    for g in range(in_ref.shape[0] - 1):
        block = in_ref[g].astype(F32)
        moved = spread(jnp.exp(read_logs(block, heads, used)), rows) * state + block[:used]
        state = jnp.where(g < me, moved, state)
    for i in range(own_ref.shape[0]):
        out_ref[i] = state.astype(BF16)
        block = own_ref[i].astype(F32)
        state = spread(jnp.exp(read_logs(block, heads, used)), rows) * state + block[:used]


def ranks(flag_ref):
    chunks = flag_ref.shape[0]
    flags = flag_ref[...].astype(F32)
    within = dot(flags.astype(BF16), below((Q, Q)))
    sums = jnp.broadcast_to(within[:, Q - 1 : Q], (chunks, Q)).astype(BF16)
    earlier = dot(below((chunks, chunks), strict=True).T, sums)
    return jnp.where(flags > 0.0, within + earlier, 0.0) - 1.0


def fill_pick(pick, flag_ref):
    rank = ranks(flag_ref)
    slot = lax.broadcasted_iota(jnp.int32, (Q, Q), 0).astype(F32).astype(BF16)
    one, zero = jnp.ones((Q, Q), BF16), jnp.zeros((Q, Q), BF16)
    for g in range(pick.shape[0] // Q):
        here = (rank - float(g * Q)).astype(BF16)
        for c in range(flag_ref.shape[0]):
            hit = here[c : c + 1] == slot
            pick[g * Q : (g + 1) * Q, c * Q : (c + 1) * Q] = jnp.where(hit, one, zero)


def pick_kernel(
    heads, gate, y, res, out_map, decay, flags, value_out, gate_out, res_out, rows_out, table, pick
):
    columns = gate.shape[0]
    flag_ref = flags()
    chunks = flag_ref.shape[0]
    fill_pick(pick, flag_ref)
    run_row = dot3(chunk_rows(decay(), heads), below((Q, Q)))
    before = jnp.zeros((heads, 1), F32)
    none = jnp.zeros((8 - heads, Q), F32)
    for c in range(chunks):
        run = run_row[c * heads : (c + 1) * heads]
        split = []
        for piece in pieces(run + before):
            split += [piece.astype(F32), none]
        split.append(jnp.zeros((8, Q), F32))
        table[columns:, c * Q : (c + 1) * Q] = jnp.concatenate(split, axis=0).astype(BF16)
        before = before + run[:, Q - 1 : Q]
    blocks = [slice(g * Q, (g + 1) * Q) for g in range(pick.shape[0] // Q)]
    table[:columns] = gate()[...]
    for these in blocks:
        both = dot(pick[these], table[...], NT)
        logs = both[:, columns : columns + heads]
        for i in (8, 16):
            logs = logs + both[:, columns + i : columns + i + heads]
        for i, piece in enumerate(pieces(jnp.exp(logs))):
            gate_out.ref[these, columns + i * heads : columns + (i + 1) * heads] = piece
        gate_out.ref[these, :columns] = both[:, :columns].astype(BF16)
        gate_out.send(these)
    for source, out in ((y, value_out), (res, res_out)):
        ref = source()
        for these in blocks:
            out.ref[these] = dot(pick[these], ref[...], NT).astype(BF16)
            out.send(these)
    map_ref = out_map()
    for these in blocks:
        rows_out.ref[these] = dot(pick[these], map_ref[...]).astype(BF16)
        rows_out.send(these)


def ssd_kernel(
    heads,
    skip_ref,
    x,
    in_map,
    out_map,
    step,
    decay,
    y_out,
    scaled,
    state,
):
    width = x.shape[0] // heads
    chunks = x.shape[1] // Q
    row = lax.broadcasted_iota(jnp.int32, (Q, Q), 0)
    col = lax.broadcasted_iota(jnp.int32, (Q, Q), 1)
    mask = row <= col
    logs = chunk_rows(decay(), heads)
    run_row = dot3(logs, below((Q, Q)))
    run_col = dot3r(jnp.where(col <= row, 1.0, 0.0).astype(BF16), logs)
    state[...] = jnp.zeros_like(state)
    step_ref = step()
    in_ref = in_map()
    out_map_ref = out_map()
    x_ref = x()
    for c in range(chunks):
        lanes = slice(c * Q, (c + 1) * Q)
        b = in_ref[lanes, :]
        o = out_map_ref[lanes, :]
        scores = dot(b, o, NT)
        outer = dot(state[...].astype(BF16), o, NT)
        for h in range(heads):
            k = c * heads + h
            part = slice(h * width, (h + 1) * width)
            run = run_row[k : k + 1]
            last = run[:, Q - 1 : Q]
            decay = jnp.where(mask, jnp.exp(run - run_col[:, k : k + 1]), 0.0)
            weights = (scores * decay).astype(BF16)
            xf = x_ref[part, lanes].astype(F32)
            stepped = xf * step_ref[h : h + 1, lanes]
            y = dot(stepped.astype(BF16), weights) + skip_ref[h] * xf
            y_out.ref[part, lanes] = (y + outer[part] * jnp.exp(run)).astype(BF16)
            scaled[part] = (stepped * jnp.exp(last - run)).astype(BF16)
            state[part] = state[part] * jnp.exp(last)
        if c < chunks - 1:
            state[...] += dot(scaled[...], b)
        if c % 4 == 3:
            y_out.send((slice(None), slice((c - 3) * Q, (c + 1) * Q)))


def gate_kernel(heads, in_ref, gain_ref, rows, value, gate, res, out):
    parts = in_ref.shape[0]
    rows_each = in_ref.shape[1] // heads
    columns = value.shape[1]
    width = columns // heads
    out_ref = out.ref
    per = out_ref.shape[1] - 8
    held = in_ref[...].astype(F32)
    states = [
        held[:, h * rows_each : (h + 1) * rows_each].reshape(parts * rows_each, Q)
        for h in range(heads)
    ]
    incoming = jnp.concatenate(states, axis=0).astype(BF16)
    gain = gain_ref[...].astype(F32)
    ones = jnp.ones((8, columns), BF16)
    row = lax.broadcasted_iota(jnp.int32, (8, per), 0)
    outer = dot(rows()[...], incoming, NT)
    value_ref = value()
    gate_ref = gate()
    res_ref = res()
    for j in range(out_ref.shape[0]):
        these = slice(j * per, (j + 1) * per)
        decay = gate_ref[these, columns:].astype(F32)
        decay = decay[:, :heads] + decay[:, heads : 2 * heads] + decay[:, 2 * heads : 3 * heads]
        since = jnp.concatenate(
            [jnp.broadcast_to(decay[:, h : h + 1], (per, width)) for h in range(heads)], axis=1
        )
        at = gate_ref[these, :columns].astype(F32)
        y = value_ref[these].astype(F32) + since * outer[these]
        gated = y * (at / (1.0 + jnp.exp(-at)))
        out_ref[j, :per, :columns] = (gated * gain).astype(BF16)
        out_ref[j, :per, columns:] = res_ref[these]
        squares = dot3r(ones, gated * gated)
        hi, mid, low = pieces(squares)
        stacked = jnp.where(
            row == 0, hi.astype(F32), jnp.where(row == 1, mid.astype(F32), low.astype(F32))
        )
        stacked = jnp.where(row < 3, stacked, 0.0)
        tail = jnp.concatenate([stacked, jnp.zeros((8, 2 * columns - per), F32)], axis=1)
        out_ref[j, per:, :] = tail.astype(BF16)
        out.send(j)


def project_kernel(full_width, in_ref, weight, out_ref, lhs, res):
    groups, tall, columns = in_ref.shape
    per = tall - 8
    columns = columns // 2
    total = jnp.zeros((1, per), F32)
    for z in range(groups):
        lhs[:, z * columns : (z + 1) * columns] = in_ref[z, :per, :columns]
        res[:, z * columns : (z + 1) * columns] = in_ref[z, :per, columns:]
        sums = in_ref[z, per:, :].astype(F32)
        total = total + jnp.sum(sums, axis=0, keepdims=True)[:, :per]
    same = lax.broadcasted_iota(jnp.int32, (per, per), 0) == lax.broadcasted_iota(
        jnp.int32, (per, per), 1
    )
    squares = jnp.sum(jnp.where(same, total, 0.0), axis=1, keepdims=True)
    scale = lax.rsqrt(squares / full_width + 1e-05)
    planes, depth, half = weight.shape
    step = depth // PARTS
    for n in range(planes):
        part = slice(n * half, (n + 1) * half)
        done = jnp.zeros((per, half), F32)
        for k in range(PARTS):
            span = slice(k * step, (k + 1) * step)
            done = done + dot(lhs[:, span], weight(n * PARTS + k)[n, span])
        out_ref[:, part] = (done * scale + res[:, part].astype(F32)).astype(BF16)


class Source:
    def __init__(self, hbm, ref, sem, split):
        self.shape, self.ref = hbm.shape, ref
        if split == "h":
            parts = [slice(None)]
        elif split == "w":
            step = hbm.shape[1] // PARTS
            parts = [
                (n, slice(k * step, (k + 1) * step)) for n in range(hbm.shape[0]) for k in range(PARTS)
            ]
        else:
            step = hbm.shape[split == "c"] // PARTS
            parts = [slice(k * step, (k + 1) * step) for k in range(PARTS)]
            if split == "c":
                parts = [(slice(None), p) for p in parts]
        self.copies = [
            pltpu.make_async_copy(hbm.at[p], ref.at[p], sem.at[k]) for k, p in enumerate(parts)
        ]

    def start(self, k):
        if k < len(self.copies):
            self.copies[k].start()

    def __call__(self, k=0):
        self.copies[k].wait()
        return self.ref


class Target:
    def __init__(self, hbm, ref, sem):
        self.hbm, self.ref, self.sem, self.copies = hbm, ref, sem, []

    def send(self, these):
        k = len(self.copies)
        copy = pltpu.make_async_copy(self.ref.at[these], self.hbm.at[these], self.sem.at[k])
        copy.start()
        self.copies.append(copy)


def call(kernel, outs, args, scratch=(), places="", to="v", name=None, mib=0, flags=None):
    spaces = {"v": pltpu.VMEM, "s": pltpu.SMEM}
    many = isinstance(outs, (tuple, list))
    results = list(outs) if many else [outs]
    far_in = [i for i, p in enumerate(places) if p in "hcqw"]
    far_out = [i for i, p in enumerate(to) if p == "h"]
    buffers = [pltpu.VMEM(args[i].shape, args[i].dtype) for i in far_in]
    buffers += [pltpu.VMEM(results[i].shape, results[i].dtype) for i in far_out]
    sems = [pltpu.SemaphoreType.DMA((2 * PARTS,)) for _ in far_in]
    sems += [pltpu.SemaphoreType.DMA((8,)) for _ in far_out]

    def body(*refs):
        ins = list(refs[: len(args)])
        res = list(refs[len(args) : len(args) + len(results)])
        rest = refs[len(args) + len(results) :]
        own = rest[: len(scratch)]
        held = rest[len(scratch) : len(scratch) + len(buffers)]
        flagged = rest[len(scratch) + len(buffers) :]
        for k, i in enumerate(far_in):
            ins[i] = Source(ins[i], held[k], flagged[k], places[i])
        for part in range(2 * PARTS):
            for i in far_in:
                ins[i].start(part)
        for k, i in enumerate(far_out):
            res[i] = Target(res[i], held[len(far_in) + k], flagged[len(far_in) + k])
        kernel(*ins, *res, *own)
        for i in far_out:
            for copy in res[i].copies:
                copy.wait()

    out_specs = [pl.BlockSpec(memory_space=spaces.get(p, pltpu.HBM)) for p in to]
    return pl.pallas_call(
        body,
        out_shape=outs,
        in_specs=[pl.BlockSpec(memory_space=spaces.get(p, pltpu.HBM)) for p in places],
        out_specs=out_specs if many else out_specs[0],
        scratch_shapes=[*scratch, *buffers, *sems],
        compiler_params=pltpu.CompilerParams(vmem_limit_bytes=mib << 20 if mib else None, flags=flags),
        name=name,
    )(*args)


def on_device(
    head_input,
    gate_input,
    input_map,
    output_map,
    step_size,
    log_decay,
    skip_gain,
    residual,
    boundary,
    norm_gain,
    out_weight,
):
    S = jax.ShapeDtypeStruct
    group = ("x", "core")
    parts = lax.axis_size(group)
    groups = lax.axis_size("y")
    shares = lax.axis_size("head")
    local_width, length = head_input.shape
    heads = step_size.shape[0]
    full_width = out_weight.shape[1]
    slots = length // 4
    per = slots // shares
    used = local_width // parts
    height = used + 8

    held = lax.optimization_barrier
    flags = boundary.reshape(length // Q, Q)

    state = call(
        functools.partial(final_state_kernel, heads, parts),
        S((parts, height, Q), BF16),
        (head_input, input_map, step_size, log_decay),
        [pltpu.VMEM((local_width, length), BF16)],
        places="hhhh",
        name="final_state",
    )
    state, out_weight = held((state, out_weight))
    cores = lax.axis_size("core")
    half = full_width // cores
    own = lax.dynamic_slice_in_dim(out_weight, lax.axis_index("core") * half, half, 1)
    weight = lax.all_gather(own[None], ("core", "head"), axis=0, tiled=True)
    moved = lax.all_to_all(state, group, 0, 0, tiled=True)
    total = call(
        functools.partial(group_scan_kernel, heads),
        S((groups, height, Q), BF16),
        (moved,),
        places="v",
        name="group_scan",
        mib=2,
    )
    total, input_map = held((total, input_map))
    totals = lax.all_to_all(total, "y", 0, 0, tiled=True)
    y = call(
        functools.partial(ssd_kernel, heads),
        S((local_width, length), BF16),
        (skip_gain, head_input, input_map, output_map, step_size, log_decay),
        [pltpu.VMEM((local_width, Q), BF16), pltpu.VMEM((local_width, Q), F32)],
        places="shhhhh",
        to="h",
        name="ssd",
    )
    totals, y = held((totals, y))
    incoming = call(
        functools.partial(combine_kernel, heads),
        S((parts, used, Q), BF16),
        (totals, moved),
        places="vv",
        name="combine",
        mib=2,
    )
    incoming, flags = held((incoming, flags))
    incoming = lax.all_to_all(incoming, group, 0, 0, tiled=True)
    wide = -(-(local_width + 3 * heads) // Q) * Q
    value, gate, res, rows = call(
        functools.partial(pick_kernel, heads),
        (
            S((slots, local_width), BF16),
            S((slots, wide), BF16),
            S((slots, local_width), BF16),
            S((slots, Q), BF16),
        ),
        (gate_input, y, residual, output_map, log_decay, flags),
        [pltpu.VMEM((local_width + 32, length), BF16), pltpu.VMEM((slots, length), BF16)],
        places="hhhhhh",
        to="hhhh",
        name="pick",
    )
    gated = call(
        functools.partial(gate_kernel, heads),
        S((shares, per + 8, 2 * local_width), BF16),
        (incoming, norm_gain.reshape(1, local_width), rows, value, gate, res),
        places="vvhhhh",
        to="h",
        name="gated",
    )
    gathered = lax.all_to_all(gated, "head", 0, 0, tiled=True)
    weight = weight.reshape(cores, shares * local_width, half)
    return call(
        functools.partial(project_kernel, full_width),
        S((per, full_width), BF16),
        (gathered, weight),
        [pltpu.VMEM((per, full_width), BF16), pltpu.VMEM((per, full_width), BF16)],
        places="vw",
        name="project",
    )


def solution(mesh):
    heads = mesh.shape["head"]
    segs = mesh.shape["seg"]
    core, x = (2, 4) if segs % 8 == 0 else (1, 1)
    if segs == 8:
        x = 2
    fine = Mesh(mesh.devices.reshape(segs // (x * core), x, core, heads), ("y", "x", "core", "head"))
    seg = ("y", "x", "core")
    return jax.shard_map(
        on_device,
        mesh=fine,
        in_specs=(
            P("head", seg),
            P("head", seg),
            P(seg, None),
            P(seg, None),
            P("head", seg),
            P("head", seg),
            P("head"),
            P("head", seg),
            P(seg),
            P("head"),
            P("head", None),
        ),
        out_specs=P((*seg, "head"), None),
        check_vma=False,
    )
```

```python
import functools

import jax
import jax.numpy as jnp
from jax import lax
from jax.experimental import pallas as pl
from jax.experimental.pallas import tpu as pltpu
from jax.sharding import Mesh
from jax.sharding import PartitionSpec as P

F32 = jnp.float32
BF16 = jnp.bfloat16
PARTS = 4
Q = 128
NT = (((1,), (1,)), ((), ()))
NN = (((1,), (0,)), ((), ()))


def dot(a, b, dims=NN):
    return lax.dot_general(a, b, dims, preferred_element_type=F32)


def pieces(v):
    hi = v.astype(BF16)
    rest = v - hi.astype(F32)
    mid = rest.astype(BF16)
    low = (rest - mid.astype(F32)).astype(BF16)
    return hi, mid, low


def dot3(v, b, dims=NN):
    return sum(dot(p, b, dims) for p in pieces(v))


def dot3r(a, v, dims=NT):
    return sum(dot(a, p, dims) for p in pieces(v))


def below(shape, strict=False):
    i = lax.broadcasted_iota(jnp.int32, shape, 0)
    j = lax.broadcasted_iota(jnp.int32, shape, 1)
    return jnp.where((i < j) if strict else (i <= j), 1.0, 0.0).astype(BF16)


def chunk_rows(ref, heads):
    n = ref.shape[1] // Q
    return jnp.concatenate([ref[:, c * Q : (c + 1) * Q] for c in range(n)], axis=0)


def log_tile(total, rows):
    heads = total.shape[0]
    lane = lax.broadcasted_iota(jnp.int32, (heads, Q), 1)
    hi, mid, low = pieces(jnp.broadcast_to(total, (heads, Q)))
    tile = jnp.where(
        lane == 0,
        hi.astype(F32),
        jnp.where(lane == 1, mid.astype(F32), jnp.where(lane == 2, low.astype(F32), 0.0)),
    )
    return jnp.concatenate([tile, jnp.zeros((rows - heads, Q), F32)], axis=0)


def final_state_kernel(heads, parts, x, in_map, step, decay, out_ref, scaled):
    width = x.shape[0] // heads
    length = x.shape[1]
    chunks = length // Q
    rows = width // parts
    logs = chunk_rows(decay(), heads)
    after = lax.broadcasted_iota(jnp.int32, (Q, Q), 0) > lax.broadcasted_iota(
        jnp.int32, (Q, Q), 1
    )
    suffix = dot3(logs, jnp.where(after, 1.0, 0.0).astype(BF16))
    sums = jnp.sum(logs, axis=1, keepdims=True)
    later = jnp.zeros((heads, 1), F32)
    step_ref = step()
    x_ref = x()
    for c in reversed(range(chunks)):
        here = slice(c * heads, (c + 1) * heads)
        lanes = slice(c * Q, (c + 1) * Q)
        factor = step_ref[:, lanes] * jnp.exp(suffix[here] + later)
        for h in range(heads):
            part = slice(h * width, (h + 1) * width)
            scaled[part, lanes] = (x_ref[part, lanes].astype(F32) * factor[h : h + 1]).astype(BF16)
        later = later + sums[here]
    state = dot(scaled[...], in_map()[...])
    tail = log_tile(later, out_ref.shape[1] - heads * rows)
    for j in range(parts):
        own = [state[h * width + j * rows : h * width + (j + 1) * rows] for h in range(heads)]
        out_ref[j] = jnp.concatenate(own + [tail], axis=0).astype(BF16)


def read_logs(block, heads, start):
    sums = jnp.sum(block[start:].astype(F32), axis=1, keepdims=True)
    return sums[:heads]


def spread(column, rows):
    return jnp.concatenate(
        [jnp.broadcast_to(column[h : h + 1], (rows, Q)) for h in range(column.shape[0])], axis=0
    )


def group_scan_kernel(heads, in_ref, total_ref):
    used = in_ref.shape[1] - 8
    rows = used // heads
    state = jnp.zeros((used, Q), F32)
    log = jnp.zeros((heads, 1), F32)
    for i in range(in_ref.shape[0]):
        block = in_ref[i].astype(F32)
        own = read_logs(block, heads, used)
        state = spread(jnp.exp(own), rows) * state + block[:used]
        log = log + own
    tail = log_tile(log, 8)
    whole = jnp.concatenate([state, tail], axis=0).astype(BF16)
    for j in range(total_ref.shape[0]):
        total_ref[j] = whole


def combine_kernel(heads, in_ref, own_ref, out_ref):
    used = out_ref.shape[1]
    rows = used // heads
    me = lax.axis_index("y")
    state = jnp.zeros((used, Q), F32)
    for g in range(in_ref.shape[0] - 1):
        block = in_ref[g].astype(F32)
        moved = spread(jnp.exp(read_logs(block, heads, used)), rows) * state + block[:used]
        state = jnp.where(g < me, moved, state)
    for i in range(own_ref.shape[0]):
        out_ref[i] = state.astype(BF16)
        block = own_ref[i].astype(F32)
        state = spread(jnp.exp(read_logs(block, heads, used)), rows) * state + block[:used]


def ranks(flag_ref):
    chunks = flag_ref.shape[0]
    flags = flag_ref[...].astype(F32)
    within = dot(flags.astype(BF16), below((Q, Q)))
    sums = jnp.broadcast_to(within[:, Q - 1 : Q], (chunks, Q)).astype(BF16)
    earlier = dot(below((chunks, chunks), strict=True).T, sums)
    return jnp.where(flags > 0.0, within + earlier, 0.0) - 1.0


def fill_pick(pick, flag_ref):
    rank = ranks(flag_ref)
    slot = lax.broadcasted_iota(jnp.int32, (Q, Q), 0).astype(F32).astype(BF16)
    one, zero = jnp.ones((Q, Q), BF16), jnp.zeros((Q, Q), BF16)
    for g in range(pick.shape[0] // Q):
        here = (rank - float(g * Q)).astype(BF16)
        for c in range(flag_ref.shape[0]):
            hit = here[c : c + 1] == slot
            pick[g * Q : (g + 1) * Q, c * Q : (c + 1) * Q] = jnp.where(hit, one, zero)


def pick_kernel(
    heads, gate, early, late, res, out_map, decay, flags, value_out, gate_out, res_out, rows_out, table, pick
):
    columns = gate.shape[0]
    flag_ref = flags()
    chunks = flag_ref.shape[0]
    fill_pick(pick, flag_ref)
    run_row = dot3(chunk_rows(decay(), heads), below((Q, Q)))
    before = jnp.zeros((heads, 1), F32)
    none = jnp.zeros((8 - heads, Q), F32)
    for c in range(chunks):
        run = run_row[c * heads : (c + 1) * heads]
        split = []
        for piece in pieces(run + before):
            split += [piece.astype(F32), none]
        split.append(jnp.zeros((8, Q), F32))
        table[columns:, c * Q : (c + 1) * Q] = jnp.concatenate(split, axis=0).astype(BF16)
        before = before + run[:, Q - 1 : Q]
    blocks = [slice(g * Q, (g + 1) * Q) for g in range(pick.shape[0] // Q)]
    table[:columns] = gate()[...]
    for these in blocks:
        both = dot(pick[these], table[...], NT)
        logs = both[:, columns : columns + heads]
        for i in (8, 16):
            logs = logs + both[:, columns + i : columns + i + heads]
        for i, piece in enumerate(pieces(jnp.exp(logs))):
            gate_out.ref[these, columns + i * heads : columns + (i + 1) * heads] = piece
        gate_out.ref[these, :columns] = both[:, :columns].astype(BF16)
        gate_out.send(these)
    early_ref, late_ref = early(), late()
    middle = early_ref.shape[1]
    for these in blocks:
        value = dot(pick[these, :middle], early_ref[...], NT)
        value = value + dot(pick[these, middle:], late_ref[...], NT)
        value_out.ref[these] = value.astype(BF16)
        value_out.send(these)
    res_ref = res()
    for these in blocks:
        res_out.ref[these] = dot(pick[these], res_ref[...], NT).astype(BF16)
        res_out.send(these)
    map_ref = out_map()
    for these in blocks:
        rows_out.ref[these] = dot(pick[these], map_ref[...]).astype(BF16)
        rows_out.send(these)


def ssd_kernel(
    heads,
    skip_ref,
    start_ref,
    x,
    in_map,
    out_map,
    step,
    decay,
    y_out,
    state,
    scaled,
):
    width = x.shape[0] // heads
    chunks = x.shape[1] // Q
    row = lax.broadcasted_iota(jnp.int32, (Q, Q), 0)
    col = lax.broadcasted_iota(jnp.int32, (Q, Q), 1)
    mask = row <= col
    logs = chunk_rows(decay(), heads)
    run_row = dot3(logs, below((Q, Q)))
    run_col = dot3r(jnp.where(col <= row, 1.0, 0.0).astype(BF16), logs)
    state[...] = start_ref[...]
    step_ref = step()
    in_ref = in_map()
    out_map_ref = out_map()
    x_ref = x()
    for c in range(chunks):
        lanes = slice(c * Q, (c + 1) * Q)
        b = in_ref[lanes, :]
        o = out_map_ref[lanes, :]
        scores = dot(b, o, NT)
        outer = dot(state[...].astype(BF16), o, NT)
        for h in range(heads):
            k = c * heads + h
            part = slice(h * width, (h + 1) * width)
            run = run_row[k : k + 1]
            last = run[:, Q - 1 : Q]
            decay = jnp.where(mask, jnp.exp(run - run_col[:, k : k + 1]), 0.0)
            weights = (scores * decay).astype(BF16)
            xf = x_ref[part, lanes].astype(F32)
            stepped = xf * step_ref[h : h + 1, lanes]
            y = dot(stepped.astype(BF16), weights) + skip_ref[h] * xf
            y_out.ref[part, lanes] = (y + outer[part] * jnp.exp(run)).astype(BF16)
            scaled[part] = (stepped * jnp.exp(last - run)).astype(BF16)
            state[part] = state[part] * jnp.exp(last)
        state[...] += dot(scaled[...], b)
        if c % 4 == 3:
            y_out.send((slice(None), slice((c - 3) * Q, (c + 1) * Q)))


def gate_kernel(heads, in_ref, gain_ref, rows, value, gate, res, out):
    parts = in_ref.shape[0]
    rows_each = in_ref.shape[1] // heads
    columns = value.shape[1]
    width = columns // heads
    out_ref = out.ref
    per = out_ref.shape[1] - 8
    held = in_ref[...].astype(F32)
    states = [
        held[:, h * rows_each : (h + 1) * rows_each].reshape(parts * rows_each, Q)
        for h in range(heads)
    ]
    incoming = jnp.concatenate(states, axis=0).astype(BF16)
    gain = gain_ref[...].astype(F32)
    ones = jnp.ones((8, columns), BF16)
    row = lax.broadcasted_iota(jnp.int32, (8, per), 0)
    outer = dot(rows()[...], incoming, NT)
    value_ref = value()
    gate_ref = gate()
    res_ref = res()
    for j in range(out_ref.shape[0]):
        these = slice(j * per, (j + 1) * per)
        decay = gate_ref[these, columns:].astype(F32)
        decay = decay[:, :heads] + decay[:, heads : 2 * heads] + decay[:, 2 * heads : 3 * heads]
        since = jnp.concatenate(
            [jnp.broadcast_to(decay[:, h : h + 1], (per, width)) for h in range(heads)], axis=1
        )
        at = gate_ref[these, :columns].astype(F32)
        y = value_ref[these].astype(F32) + since * outer[these]
        gated = y * (at / (1.0 + jnp.exp(-at)))
        out_ref[j, :per, :columns] = (gated * gain).astype(BF16)
        out_ref[j, :per, columns:] = res_ref[these]
        squares = dot3r(ones, gated * gated)
        hi, mid, low = pieces(squares)
        stacked = jnp.where(
            row == 0, hi.astype(F32), jnp.where(row == 1, mid.astype(F32), low.astype(F32))
        )
        stacked = jnp.where(row < 3, stacked, 0.0)
        tail = jnp.concatenate([stacked, jnp.zeros((8, 2 * columns - per), F32)], axis=1)
        out_ref[j, per:, :] = tail.astype(BF16)
        out.send(j)


def project_kernel(full_width, in_ref, weight, out_ref, lhs, res):
    groups, tall, columns = in_ref.shape
    per = tall - 8
    columns = columns // 2
    total = jnp.zeros((1, per), F32)
    for z in range(groups):
        lhs[:, z * columns : (z + 1) * columns] = in_ref[z, :per, :columns]
        res[:, z * columns : (z + 1) * columns] = in_ref[z, :per, columns:]
        sums = in_ref[z, per:, :].astype(F32)
        total = total + jnp.sum(sums, axis=0, keepdims=True)[:, :per]
    same = lax.broadcasted_iota(jnp.int32, (per, per), 0) == lax.broadcasted_iota(
        jnp.int32, (per, per), 1
    )
    squares = jnp.sum(jnp.where(same, total, 0.0), axis=1, keepdims=True)
    scale = lax.rsqrt(squares / full_width + 1e-05)
    planes, depth, half = weight.shape
    step = depth // PARTS
    for n in range(planes):
        part = slice(n * half, (n + 1) * half)
        done = jnp.zeros((per, half), F32)
        for k in range(PARTS):
            span = slice(k * step, (k + 1) * step)
            done = done + dot(lhs[:, span], weight(n * PARTS + k)[n, span])
        out_ref[:, part] = (done * scale + res[:, part].astype(F32)).astype(BF16)


class Source:
    def __init__(self, hbm, ref, sem, split, window):
        self.shape, self.ref = ref.shape, ref
        if split == "h":
            parts = [slice(None)]
        elif split in "cq":
            at = slice(window * ref.shape[split == "c"], (window + 1) * ref.shape[split == "c"])
            far = hbm.at[:, at] if split == "c" else hbm.at[at]
            self.copies = [pltpu.make_async_copy(far, ref, sem.at[0])]
            return
        elif split == "w":
            step = hbm.shape[1] // PARTS
            parts = [
                (n, slice(k * step, (k + 1) * step)) for n in range(hbm.shape[0]) for k in range(PARTS)
            ]
        self.copies = [
            pltpu.make_async_copy(hbm.at[p], ref.at[p], sem.at[k]) for k, p in enumerate(parts)
        ]

    def start(self, k):
        if k < len(self.copies):
            self.copies[k].start()

    def __call__(self, k=0):
        self.copies[k].wait()
        return self.ref


class Target:
    def __init__(self, hbm, ref, sem):
        self.hbm, self.ref, self.sem, self.copies = hbm, ref, sem, []

    def send(self, these):
        k = len(self.copies)
        copy = pltpu.make_async_copy(self.ref.at[these], self.hbm.at[these], self.sem.at[k])
        copy.start()
        self.copies.append(copy)


def call(kernel, outs, args, scratch=(), places="", to="v", name=None, mib=0, flags=None, window=(0, 1)):
    spaces = {"v": pltpu.VMEM, "s": pltpu.SMEM}
    many = isinstance(outs, (tuple, list))
    results = list(outs) if many else [outs]
    far_in = [i for i, p in enumerate(places) if p in "hcqw"]
    far_out = [i for i, p in enumerate(to) if p == "h"]

    def held_shape(i):
        shape = list(args[i].shape)
        if places[i] in "cq":
            shape[places[i] == "c"] //= window[1]
        return tuple(shape)

    buffers = [pltpu.VMEM(held_shape(i), args[i].dtype) for i in far_in]
    buffers += [pltpu.VMEM(results[i].shape, results[i].dtype) for i in far_out]
    sems = [pltpu.SemaphoreType.DMA((2 * PARTS,)) for _ in far_in]
    sems += [pltpu.SemaphoreType.DMA((8,)) for _ in far_out]

    def body(*refs):
        ins = list(refs[: len(args)])
        res = list(refs[len(args) : len(args) + len(results)])
        rest = refs[len(args) + len(results) :]
        own = rest[: len(scratch)]
        held = rest[len(scratch) : len(scratch) + len(buffers)]
        flagged = rest[len(scratch) + len(buffers) :]
        for k, i in enumerate(far_in):
            ins[i] = Source(ins[i], held[k], flagged[k], places[i], window[0])
        for part in range(2 * PARTS):
            for i in sorted(far_in, key=lambda i: args[i].size):
                ins[i].start(part)
        for k, i in enumerate(far_out):
            res[i] = Target(res[i], held[len(far_in) + k], flagged[len(far_in) + k])
        kernel(*ins, *res, *own)
        for i in far_out:
            for copy in res[i].copies:
                copy.wait()

    out_specs = [pl.BlockSpec(memory_space=spaces.get(p, pltpu.HBM)) for p in to]
    return pl.pallas_call(
        body,
        out_shape=outs,
        in_specs=[pl.BlockSpec(memory_space=spaces.get(p, pltpu.HBM)) for p in places],
        out_specs=out_specs if many else out_specs[0],
        scratch_shapes=[*scratch, *buffers, *sems],
        compiler_params=pltpu.CompilerParams(vmem_limit_bytes=mib << 20 if mib else None, flags=flags),
        name=name,
    )(*args)


def on_device(
    head_input,
    gate_input,
    input_map,
    output_map,
    step_size,
    log_decay,
    skip_gain,
    residual,
    boundary,
    norm_gain,
    out_weight,
):
    S = jax.ShapeDtypeStruct
    group = ("x", "core")
    parts = lax.axis_size(group)
    groups = lax.axis_size("y")
    shares = lax.axis_size("head")
    local_width, length = head_input.shape
    heads = step_size.shape[0]
    full_width = out_weight.shape[1]
    slots = length // 4
    per = slots // shares
    used = local_width // parts
    height = used + 8

    held = lax.optimization_barrier
    flags = boundary.reshape(length // Q, Q)

    state = call(
        functools.partial(final_state_kernel, heads, parts),
        S((parts, height, Q), BF16),
        (head_input, input_map, step_size, log_decay),
        [pltpu.VMEM((local_width, length), BF16)],
        places="hhhh",
        name="final_state",
    )
    state, out_weight = held((state, out_weight))
    cores = lax.axis_size("core")
    half = full_width // cores
    own = lax.dynamic_slice_in_dim(out_weight, lax.axis_index("core") * half, half, 1)
    weight = lax.all_gather(own[None], ("core", "head"), axis=0, tiled=True)
    def ssd(start, at):
        return call(
            functools.partial(ssd_kernel, heads),
            (S((local_width, length // 2), BF16), S((local_width, Q), F32)),
            (skip_gain, start, head_input, input_map, output_map, step_size, log_decay),
            [pltpu.VMEM((local_width, Q), BF16)],
            places="svcqqcc",
            to="hv",
            name="ssd",
            window=(at, 2),
        )

    moved = lax.all_to_all(state, group, 0, 0, tiled=True)
    state, input_map = held((state, input_map))
    early, middle = ssd(jnp.zeros((local_width, Q), F32), 0)
    moved, early, gain = held((moved, early, norm_gain.reshape(1, local_width)))
    total = call(
        functools.partial(group_scan_kernel, heads),
        S((groups, height, Q), BF16),
        (moved,),
        places="v",
        name="group_scan",
        mib=2,
    )
    total, middle = held((total, middle))
    totals = lax.all_to_all(total, "y", 0, 0, tiled=True)
    late, _ = ssd(middle, 1)
    totals, late = held((totals, late))
    incoming = call(
        functools.partial(combine_kernel, heads),
        S((parts, used, Q), BF16),
        (totals, moved),
        places="vv",
        name="combine",
        mib=2,
    )
    incoming, flags = held((incoming, flags))
    incoming = lax.all_to_all(incoming, group, 0, 0, tiled=True)
    wide = -(-(local_width + 3 * heads) // Q) * Q
    value, gate, res, rows = call(
        functools.partial(pick_kernel, heads),
        (
            S((slots, local_width), BF16),
            S((slots, wide), BF16),
            S((slots, local_width), BF16),
            S((slots, Q), BF16),
        ),
        (gate_input, early, late, residual, output_map, log_decay, flags),
        [pltpu.VMEM((local_width + 32, length), BF16), pltpu.VMEM((slots, length), BF16)],
        places="hhhhhhh",
        to="hhhh",
        name="pick",
    )
    gated = call(
        functools.partial(gate_kernel, heads),
        S((shares, per + 8, 2 * local_width), BF16),
        (incoming, gain, rows, value, gate, res),
        places="vvhhhh",
        to="h",
        name="gated",
    )
    gathered = lax.all_to_all(gated, "head", 0, 0, tiled=True)
    weight = weight.reshape(cores, shares * local_width, half)
    return call(
        functools.partial(project_kernel, full_width),
        S((per, full_width), BF16),
        (gathered, weight),
        [pltpu.VMEM((per, full_width), BF16), pltpu.VMEM((per, full_width), BF16)],
        places="vw",
        name="project",
    )


def solution(mesh):
    heads = mesh.shape["head"]
    segs = mesh.shape["seg"]
    core, x = (2, 4) if segs % 8 == 0 else (1, 1)
    if segs == 8:
        x = 2
    fine = Mesh(mesh.devices.reshape(segs // (x * core), x, core, heads), ("y", "x", "core", "head"))
    seg = ("y", "x", "core")
    return jax.shard_map(
        on_device,
        mesh=fine,
        in_specs=(
            P("head", seg),
            P("head", seg),
            P(seg, None),
            P(seg, None),
            P("head", seg),
            P("head", seg),
            P("head"),
            P("head", seg),
            P(seg),
            P("head"),
            P("head", None),
        ),
        out_specs=P((*seg, "head"), None),
        check_vma=False,
    )
```

```python
import functools

import jax
import jax.numpy as jnp
from jax import lax
from jax.experimental import pallas as pl
from jax.experimental.pallas import tpu as pltpu
from jax.sharding import Mesh
from jax.sharding import PartitionSpec as P

F32 = jnp.float32
BF16 = jnp.bfloat16
PARTS = 4
Q = 128
NT = (((1,), (1,)), ((), ()))
NN = (((1,), (0,)), ((), ()))


def dot(a, b, dims=NN):
    return lax.dot_general(a, b, dims, preferred_element_type=F32)


def pieces(v):
    hi = v.astype(BF16)
    rest = v - hi.astype(F32)
    mid = rest.astype(BF16)
    low = (rest - mid.astype(F32)).astype(BF16)
    return hi, mid, low


def dot3(v, b, dims=NN):
    return sum(dot(p, b, dims) for p in pieces(v))


def dot3r(a, v, dims=NT):
    return sum(dot(a, p, dims) for p in pieces(v))


def below(shape, strict=False):
    i = lax.broadcasted_iota(jnp.int32, shape, 0)
    j = lax.broadcasted_iota(jnp.int32, shape, 1)
    return jnp.where((i < j) if strict else (i <= j), 1.0, 0.0).astype(BF16)


def chunk_rows(ref, heads):
    n = ref.shape[1] // Q
    return jnp.concatenate([ref[:, c * Q : (c + 1) * Q] for c in range(n)], axis=0)


def log_tile(total, rows):
    heads = total.shape[0]
    lane = lax.broadcasted_iota(jnp.int32, (heads, Q), 1)
    hi, mid, low = pieces(jnp.broadcast_to(total, (heads, Q)))
    tile = jnp.where(
        lane == 0,
        hi.astype(F32),
        jnp.where(lane == 1, mid.astype(F32), jnp.where(lane == 2, low.astype(F32), 0.0)),
    )
    return jnp.concatenate([tile, jnp.zeros((rows - heads, Q), F32)], axis=0)


def final_state_kernel(heads, parts, x, in_map, step, decay, out_ref, scaled):
    width = x.shape[0] // heads
    length = x.shape[1]
    chunks = length // Q
    rows = width // parts
    logs = chunk_rows(decay(), heads)
    after = lax.broadcasted_iota(jnp.int32, (Q, Q), 0) > lax.broadcasted_iota(
        jnp.int32, (Q, Q), 1
    )
    suffix = dot3(logs, jnp.where(after, 1.0, 0.0).astype(BF16))
    sums = jnp.sum(logs, axis=1, keepdims=True)
    later = jnp.zeros((heads, 1), F32)
    step_ref = step()
    x_ref = x()
    for c in reversed(range(chunks)):
        here = slice(c * heads, (c + 1) * heads)
        lanes = slice(c * Q, (c + 1) * Q)
        factor = step_ref[:, lanes] * jnp.exp(suffix[here] + later)
        for h in range(heads):
            part = slice(h * width, (h + 1) * width)
            scaled[part, lanes] = (x_ref[part, lanes].astype(F32) * factor[h : h + 1]).astype(BF16)
        later = later + sums[here]
    state = dot(scaled[...], in_map()[...])
    tail = log_tile(later, out_ref.shape[1] - heads * rows)
    for j in range(parts):
        own = [state[h * width + j * rows : h * width + (j + 1) * rows] for h in range(heads)]
        out_ref[j] = jnp.concatenate(own + [tail], axis=0).astype(BF16)


def read_logs(block, heads, start):
    sums = jnp.sum(block[start:].astype(F32), axis=1, keepdims=True)
    return sums[:heads]


def spread(column, rows):
    return jnp.concatenate(
        [jnp.broadcast_to(column[h : h + 1], (rows, Q)) for h in range(column.shape[0])], axis=0
    )


def group_scan_kernel(heads, in_ref, total_ref):
    used = in_ref.shape[1] - 8
    rows = used // heads
    state = jnp.zeros((used, Q), F32)
    log = jnp.zeros((heads, 1), F32)
    for i in range(in_ref.shape[0]):
        block = in_ref[i].astype(F32)
        own = read_logs(block, heads, used)
        state = spread(jnp.exp(own), rows) * state + block[:used]
        log = log + own
    tail = log_tile(log, 8)
    whole = jnp.concatenate([state, tail], axis=0).astype(BF16)
    for j in range(total_ref.shape[0]):
        total_ref[j] = whole


def combine_kernel(heads, in_ref, own_ref, out_ref):
    used = out_ref.shape[1]
    rows = used // heads
    me = lax.axis_index("y")
    state = jnp.zeros((used, Q), F32)
    for g in range(in_ref.shape[0] - 1):
        block = in_ref[g].astype(F32)
        moved = spread(jnp.exp(read_logs(block, heads, used)), rows) * state + block[:used]
        state = jnp.where(g < me, moved, state)
    for i in range(own_ref.shape[0]):
        out_ref[i] = state.astype(BF16)
        block = own_ref[i].astype(F32)
        state = spread(jnp.exp(read_logs(block, heads, used)), rows) * state + block[:used]


def ranks(flag_ref):
    chunks = flag_ref.shape[0]
    flags = flag_ref[...].astype(F32)
    within = dot(flags.astype(BF16), below((Q, Q)))
    sums = jnp.broadcast_to(within[:, Q - 1 : Q], (chunks, Q)).astype(BF16)
    earlier = dot(below((chunks, chunks), strict=True).T, sums)
    return jnp.where(flags > 0.0, within + earlier, 0.0) - 1.0


def fill_pick(pick, flag_ref):
    rank = ranks(flag_ref)
    slot = lax.broadcasted_iota(jnp.int32, (Q, Q), 0).astype(F32).astype(BF16)
    one, zero = jnp.ones((Q, Q), BF16), jnp.zeros((Q, Q), BF16)
    for g in range(pick.shape[0] // Q):
        here = (rank - float(g * Q)).astype(BF16)
        for c in range(flag_ref.shape[0]):
            hit = here[c : c + 1] == slot
            pick[g * Q : (g + 1) * Q, c * Q : (c + 1) * Q] = jnp.where(hit, one, zero)


def pick_kernel(out_map, res, flags, rows_out, res_out, pick):
    fill_pick(pick, flags())
    blocks = [slice(g * Q, (g + 1) * Q) for g in range(pick.shape[0] // Q)]
    map_ref = out_map()
    for these in blocks:
        rows_out.ref[these] = dot(pick[these], map_ref[...]).astype(BF16)
        rows_out.send(these)
    res_ref = res()
    for these in blocks:
        res_out.ref[these] = dot(pick[these], res_ref[...], NT).astype(BF16)
        res_out.send(these)


def pick_gate_kernel(heads, gate, y, decay, flags, value_out, factor_out, table, pick):
    columns = gate.shape[0]
    width = columns // heads
    flag_ref = flags()
    chunks = flag_ref.shape[0]
    fill_pick(pick, flag_ref)
    run_row = dot3(chunk_rows(decay(), heads), below((Q, Q)))
    before = jnp.zeros((heads, 1), F32)
    none = jnp.zeros((8 - heads, Q), F32)
    for c in range(chunks):
        run = run_row[c * heads : (c + 1) * heads]
        split = []
        for piece in pieces(run + before):
            split += [piece.astype(F32), none]
        split.append(jnp.zeros((8, Q), F32))
        table[columns:, c * Q : (c + 1) * Q] = jnp.concatenate(split, axis=0).astype(BF16)
        before = before + run[:, Q - 1 : Q]
    table[:columns] = gate()[...]
    y_ref = y()
    for g in range(pick.shape[0] // Q):
        these = slice(g * Q, (g + 1) * Q)
        both = dot(pick[these], table[...], NT)
        at = both[:, :columns]
        silu = at / (1.0 + jnp.exp(-at))
        logs = both[:, columns : columns + heads]
        for i in (8, 16):
            logs = logs + both[:, columns + i : columns + i + heads]
        since = jnp.exp(logs)
        since = jnp.concatenate(
            [jnp.broadcast_to(since[:, h : h + 1], (Q, width)) for h in range(heads)], axis=1
        )
        factor_out.ref[these] = (since * silu).astype(BF16)
        factor_out.send(these)
        value_out.ref[these] = (dot(pick[these], y_ref[...], NT) * silu).astype(BF16)
        value_out.send(these)


def ssd_kernel(
    heads,
    skip_ref,
    x,
    in_map,
    out_map,
    step,
    decay,
    y_out,
    scaled,
    state,
):
    width = x.shape[0] // heads
    chunks = x.shape[1] // Q
    row = lax.broadcasted_iota(jnp.int32, (Q, Q), 0)
    col = lax.broadcasted_iota(jnp.int32, (Q, Q), 1)
    mask = row <= col
    logs = chunk_rows(decay(), heads)
    run_row = dot3(logs, below((Q, Q)))
    run_col = dot3r(jnp.where(col <= row, 1.0, 0.0).astype(BF16), logs)
    state[...] = jnp.zeros_like(state)
    step_ref = step()
    in_ref = in_map()
    out_map_ref = out_map()
    x_ref = x()
    for c in range(chunks):
        lanes = slice(c * Q, (c + 1) * Q)
        b = in_ref[lanes, :]
        o = out_map_ref[lanes, :]
        scores = dot(b, o, NT)
        outer = dot(state[...].astype(BF16), o, NT)
        for h in range(heads):
            k = c * heads + h
            part = slice(h * width, (h + 1) * width)
            run = run_row[k : k + 1]
            last = run[:, Q - 1 : Q]
            decay = jnp.where(mask, jnp.exp(run - run_col[:, k : k + 1]), 0.0)
            weights = (scores * decay).astype(BF16)
            xf = x_ref[part, lanes].astype(F32)
            stepped = xf * step_ref[h : h + 1, lanes]
            y = dot(stepped.astype(BF16), weights) + skip_ref[h] * xf
            y_out.ref[part, lanes] = (y + outer[part] * jnp.exp(run)).astype(BF16)
            scaled[part] = (stepped * jnp.exp(last - run)).astype(BF16)
            state[part] = state[part] * jnp.exp(last)
        if c < chunks - 1:
            state[...] += dot(scaled[...], b)
        if c % 4 == 3:
            y_out.send((slice(None), slice((c - 3) * Q, (c + 1) * Q)))


def gate_kernel(heads, in_ref, gain_ref, rows, factor, value, res, out):
    parts = in_ref.shape[0]
    rows_each = in_ref.shape[1] // heads
    columns = value.shape[1]
    out_ref = out.ref
    per = out_ref.shape[1] - 8
    held = in_ref[...].astype(F32)
    states = [
        held[:, h * rows_each : (h + 1) * rows_each].reshape(parts * rows_each, Q)
        for h in range(heads)
    ]
    incoming = jnp.concatenate(states, axis=0).astype(BF16)
    gain = gain_ref[...].astype(F32)
    ones = jnp.ones((8, columns), BF16)
    row = lax.broadcasted_iota(jnp.int32, (8, per), 0)
    outer = dot(rows()[...], incoming, NT)
    factor_ref = factor()
    value_ref = value()
    res_ref = res()
    for j in range(out_ref.shape[0]):
        these = slice(j * per, (j + 1) * per)
        gated = value_ref[these].astype(F32) + factor_ref[these].astype(F32) * outer[these]
        out_ref[j, :per, :columns] = (gated * gain).astype(BF16)
        out_ref[j, :per, columns:] = res_ref[these]
        squares = dot3r(ones, gated * gated)
        hi, mid, low = pieces(squares)
        stacked = jnp.where(
            row == 0, hi.astype(F32), jnp.where(row == 1, mid.astype(F32), low.astype(F32))
        )
        stacked = jnp.where(row < 3, stacked, 0.0)
        tail = jnp.concatenate([stacked, jnp.zeros((8, 2 * columns - per), F32)], axis=1)
        out_ref[j, per:, :] = tail.astype(BF16)
        out.send(j)


def project_kernel(full_width, in_ref, weight, out_ref, lhs, res):
    groups, tall, columns = in_ref.shape
    per = tall - 8
    columns = columns // 2
    total = jnp.zeros((1, per), F32)
    for z in range(groups):
        lhs[:, z * columns : (z + 1) * columns] = in_ref[z, :per, :columns]
        res[:, z * columns : (z + 1) * columns] = in_ref[z, :per, columns:]
        sums = in_ref[z, per:, :].astype(F32)
        total = total + jnp.sum(sums, axis=0, keepdims=True)[:, :per]
    same = lax.broadcasted_iota(jnp.int32, (per, per), 0) == lax.broadcasted_iota(
        jnp.int32, (per, per), 1
    )
    squares = jnp.sum(jnp.where(same, total, 0.0), axis=1, keepdims=True)
    scale = lax.rsqrt(squares / full_width + 1e-05)
    planes, depth, half = weight.shape
    step = depth // PARTS
    for n in range(planes):
        part = slice(n * half, (n + 1) * half)
        done = jnp.zeros((per, half), F32)
        for k in range(PARTS):
            span = slice(k * step, (k + 1) * step)
            done = done + dot(lhs[:, span], weight(n * PARTS + k)[n, span])
        out_ref[:, part] = (done * scale + res[:, part].astype(F32)).astype(BF16)


class Source:
    def __init__(self, hbm, ref, sem, split):
        self.shape, self.ref = hbm.shape, ref
        if split == "h":
            parts = [slice(None)]
        elif split == "w":
            step = hbm.shape[1] // PARTS
            parts = [
                (n, slice(k * step, (k + 1) * step)) for n in range(hbm.shape[0]) for k in range(PARTS)
            ]
        else:
            step = hbm.shape[split == "c"] // PARTS
            parts = [slice(k * step, (k + 1) * step) for k in range(PARTS)]
            if split == "c":
                parts = [(slice(None), p) for p in parts]
        self.copies = [
            pltpu.make_async_copy(hbm.at[p], ref.at[p], sem.at[k]) for k, p in enumerate(parts)
        ]

    def start(self, k):
        if k < len(self.copies):
            self.copies[k].start()

    def __call__(self, k=0):
        self.copies[k].wait()
        return self.ref


class Target:
    def __init__(self, hbm, ref, sem):
        self.hbm, self.ref, self.sem, self.copies = hbm, ref, sem, []

    def send(self, these):
        k = len(self.copies)
        copy = pltpu.make_async_copy(self.ref.at[these], self.hbm.at[these], self.sem.at[k])
        copy.start()
        self.copies.append(copy)


def call(kernel, outs, args, scratch=(), places="", to="v", name=None, mib=0, flags=None):
    spaces = {"v": pltpu.VMEM, "s": pltpu.SMEM}
    many = isinstance(outs, (tuple, list))
    results = list(outs) if many else [outs]
    far_in = [i for i, p in enumerate(places) if p in "hcqw"]
    far_out = [i for i, p in enumerate(to) if p == "h"]
    buffers = [pltpu.VMEM(args[i].shape, args[i].dtype) for i in far_in]
    buffers += [pltpu.VMEM(results[i].shape, results[i].dtype) for i in far_out]
    sems = [pltpu.SemaphoreType.DMA((2 * PARTS,)) for _ in far_in]
    sems += [pltpu.SemaphoreType.DMA((8,)) for _ in far_out]

    def body(*refs):
        ins = list(refs[: len(args)])
        res = list(refs[len(args) : len(args) + len(results)])
        rest = refs[len(args) + len(results) :]
        own = rest[: len(scratch)]
        held = rest[len(scratch) : len(scratch) + len(buffers)]
        flagged = rest[len(scratch) + len(buffers) :]
        for k, i in enumerate(far_in):
            ins[i] = Source(ins[i], held[k], flagged[k], places[i])
        for part in range(2 * PARTS):
            for i in sorted(far_in, key=lambda i: args[i].size):
                ins[i].start(part)
        for k, i in enumerate(far_out):
            res[i] = Target(res[i], held[len(far_in) + k], flagged[len(far_in) + k])
        kernel(*ins, *res, *own)
        for i in far_out:
            for copy in res[i].copies:
                copy.wait()

    out_specs = [pl.BlockSpec(memory_space=spaces.get(p, pltpu.HBM)) for p in to]
    return pl.pallas_call(
        body,
        out_shape=outs,
        in_specs=[pl.BlockSpec(memory_space=spaces.get(p, pltpu.HBM)) for p in places],
        out_specs=out_specs if many else out_specs[0],
        scratch_shapes=[*scratch, *buffers, *sems],
        compiler_params=pltpu.CompilerParams(vmem_limit_bytes=mib << 20 if mib else None, flags=flags),
        name=name,
    )(*args)


def on_device(
    head_input,
    gate_input,
    input_map,
    output_map,
    step_size,
    log_decay,
    skip_gain,
    residual,
    boundary,
    norm_gain,
    out_weight,
):
    S = jax.ShapeDtypeStruct
    group = ("x", "core")
    parts = lax.axis_size(group)
    groups = lax.axis_size("y")
    shares = lax.axis_size("head")
    local_width, length = head_input.shape
    heads = step_size.shape[0]
    full_width = out_weight.shape[1]
    slots = length // 4
    per = slots // shares
    used = local_width // parts
    height = used + 8

    held = lax.optimization_barrier
    flags = boundary.reshape(length // Q, Q)

    state = call(
        functools.partial(final_state_kernel, heads, parts),
        S((parts, height, Q), BF16),
        (head_input, input_map, step_size, log_decay),
        [pltpu.VMEM((local_width, length), BF16)],
        places="hhhh",
        name="final_state",
    )
    state, out_weight, flags = held((state, out_weight, flags))
    cores = lax.axis_size("core")
    half = full_width // cores
    own = lax.dynamic_slice_in_dim(out_weight, lax.axis_index("core") * half, half, 1)
    weight = lax.all_gather(own[None], ("core", "head"), axis=0, tiled=True)
    moved = lax.all_to_all(state, group, 0, 0, tiled=True)
    rows, res = call(
        pick_kernel,
        (S((slots, Q), BF16), S((slots, local_width), BF16)),
        (output_map, residual, flags),
        [pltpu.VMEM((slots, length), BF16)],
        places="hhh",
        to="hh",
        name="pick",
    )
    moved, rows, res = held((moved, rows, res))
    total = call(
        functools.partial(group_scan_kernel, heads),
        S((groups, height, Q), BF16),
        (moved,),
        places="v",
        name="group_scan",
        mib=2,
    )
    total, input_map, norm_gain = held((total, input_map, norm_gain))
    gain = norm_gain.reshape(1, local_width)
    totals = lax.all_to_all(total, "y", 0, 0, tiled=True)
    y = call(
        functools.partial(ssd_kernel, heads),
        S((local_width, length), BF16),
        (skip_gain, head_input, input_map, output_map, step_size, log_decay),
        [pltpu.VMEM((local_width, Q), BF16), pltpu.VMEM((local_width, Q), F32)],
        places="shhhhh",
        to="h",
        name="ssd",
    )
    totals, y, gain = held((totals, y, gain))
    incoming = call(
        functools.partial(combine_kernel, heads),
        S((parts, used, Q), BF16),
        (totals, moved),
        places="vv",
        name="combine",
        mib=2,
    )
    incoming, flags = held((incoming, flags))
    incoming = lax.all_to_all(incoming, group, 0, 0, tiled=True)
    value, factor = call(
        functools.partial(pick_gate_kernel, heads),
        (S((slots, local_width), BF16), S((slots, local_width), BF16)),
        (gate_input, y, log_decay, flags),
        [pltpu.VMEM((local_width + 32, length), BF16), pltpu.VMEM((slots, length), BF16)],
        places="hhhh",
        to="hh",
        name="pick_gate",
    )
    gated = call(
        functools.partial(gate_kernel, heads),
        S((shares, per + 8, 2 * local_width), BF16),
        (incoming, gain, rows, factor, value, res),
        places="vvhhhh",
        to="h",
        name="gated",
    )
    gathered = lax.all_to_all(gated, "head", 0, 0, tiled=True)
    weight = weight.reshape(cores, shares * local_width, half)
    return call(
        functools.partial(project_kernel, full_width),
        S((per, full_width), BF16),
        (gathered, weight),
        [pltpu.VMEM((per, full_width), BF16), pltpu.VMEM((per, full_width), BF16)],
        places="vw",
        name="project",
    )


def solution(mesh):
    heads = mesh.shape["head"]
    segs = mesh.shape["seg"]
    core, x = (2, 4) if segs % 8 == 0 else (1, 1)
    if segs == 8:
        x = 2
    fine = Mesh(mesh.devices.reshape(segs // (x * core), x, core, heads), ("y", "x", "core", "head"))
    seg = ("y", "x", "core")
    return jax.shard_map(
        on_device,
        mesh=fine,
        in_specs=(
            P("head", seg),
            P("head", seg),
            P(seg, None),
            P(seg, None),
            P("head", seg),
            P("head", seg),
            P("head"),
            P("head", seg),
            P(seg),
            P("head"),
            P("head", None),
        ),
        out_specs=P((*seg, "head"), None),
        check_vma=False,
    )
```

```python
import functools

import jax
import jax.numpy as jnp
from jax import lax
from jax.experimental import pallas as pl
from jax.experimental.pallas import tpu as pltpu
from jax.sharding import Mesh
from jax.sharding import PartitionSpec as P

F32 = jnp.float32
BF16 = jnp.bfloat16
PARTS = 4
Q = 128
NT = (((1,), (1,)), ((), ()))
NN = (((1,), (0,)), ((), ()))


def dot(a, b, dims=NN):
    return lax.dot_general(a, b, dims, preferred_element_type=F32)


def pieces(v):
    hi = v.astype(BF16)
    rest = v - hi.astype(F32)
    mid = rest.astype(BF16)
    low = (rest - mid.astype(F32)).astype(BF16)
    return hi, mid, low


def dot3(v, b, dims=NN):
    return sum(dot(p, b, dims) for p in pieces(v))


def dot3r(a, v, dims=NT):
    return sum(dot(a, p, dims) for p in pieces(v))


def below(shape, strict=False):
    i = lax.broadcasted_iota(jnp.int32, shape, 0)
    j = lax.broadcasted_iota(jnp.int32, shape, 1)
    return jnp.where((i < j) if strict else (i <= j), 1.0, 0.0).astype(BF16)


def chunk_rows(ref, heads):
    n = ref.shape[1] // Q
    return jnp.concatenate([ref[:, c * Q : (c + 1) * Q] for c in range(n)], axis=0)


def log_tile(total, rows):
    heads = total.shape[0]
    lane = lax.broadcasted_iota(jnp.int32, (heads, Q), 1)
    hi, mid, low = pieces(jnp.broadcast_to(total, (heads, Q)))
    tile = jnp.where(
        lane == 0,
        hi.astype(F32),
        jnp.where(lane == 1, mid.astype(F32), jnp.where(lane == 2, low.astype(F32), 0.0)),
    )
    return jnp.concatenate([tile, jnp.zeros((rows - heads, Q), F32)], axis=0)


def final_state_kernel(heads, parts, x, in_map, step, decay, out_ref, scaled):
    width = x.shape[0] // heads
    length = x.shape[1]
    chunks = length // Q
    rows = width // parts
    logs = chunk_rows(decay(), heads)
    after = lax.broadcasted_iota(jnp.int32, (Q, Q), 0) > lax.broadcasted_iota(
        jnp.int32, (Q, Q), 1
    )
    suffix = dot3(logs, jnp.where(after, 1.0, 0.0).astype(BF16))
    sums = jnp.sum(logs, axis=1, keepdims=True)
    later = jnp.zeros((heads, 1), F32)
    step_ref = step()
    x_ref = x()
    for c in reversed(range(chunks)):
        here = slice(c * heads, (c + 1) * heads)
        lanes = slice(c * Q, (c + 1) * Q)
        factor = step_ref[:, lanes] * jnp.exp(suffix[here] + later)
        for h in range(heads):
            part = slice(h * width, (h + 1) * width)
            scaled[part, lanes] = (x_ref[part, lanes].astype(F32) * factor[h : h + 1]).astype(BF16)
        later = later + sums[here]
    state = dot(scaled[...], in_map()[...])
    tail = log_tile(later, out_ref.shape[1] - heads * rows)
    for j in range(parts):
        own = [state[h * width + j * rows : h * width + (j + 1) * rows] for h in range(heads)]
        out_ref[j] = jnp.concatenate(own + [tail], axis=0).astype(BF16)


def read_logs(block, heads, start):
    sums = jnp.sum(block[start:].astype(F32), axis=1, keepdims=True)
    return sums[:heads]


def spread(column, rows):
    return jnp.concatenate(
        [jnp.broadcast_to(column[h : h + 1], (rows, Q)) for h in range(column.shape[0])], axis=0
    )


def group_scan_kernel(heads, in_ref, total_ref):
    used = in_ref.shape[1] - 8
    rows = used // heads
    state = jnp.zeros((used, Q), F32)
    log = jnp.zeros((heads, 1), F32)
    for i in range(in_ref.shape[0]):
        block = in_ref[i].astype(F32)
        own = read_logs(block, heads, used)
        state = spread(jnp.exp(own), rows) * state + block[:used]
        log = log + own
    tail = log_tile(log, 8)
    whole = jnp.concatenate([state, tail], axis=0).astype(BF16)
    for j in range(total_ref.shape[0]):
        total_ref[j] = whole


def combine_kernel(heads, in_ref, own_ref, out_ref):
    used = out_ref.shape[1]
    rows = used // heads
    me = lax.axis_index("y")
    state = jnp.zeros((used, Q), F32)
    for g in range(in_ref.shape[0] - 1):
        block = in_ref[g].astype(F32)
        moved = spread(jnp.exp(read_logs(block, heads, used)), rows) * state + block[:used]
        state = jnp.where(g < me, moved, state)
    for i in range(own_ref.shape[0]):
        out_ref[i] = state.astype(BF16)
        block = own_ref[i].astype(F32)
        state = spread(jnp.exp(read_logs(block, heads, used)), rows) * state + block[:used]


def ranks(flag_ref):
    chunks = flag_ref.shape[0]
    flags = flag_ref[...].astype(F32)
    within = dot(flags.astype(BF16), below((Q, Q)))
    sums = jnp.broadcast_to(within[:, Q - 1 : Q], (chunks, Q)).astype(BF16)
    earlier = dot(below((chunks, chunks), strict=True).T, sums)
    return jnp.where(flags > 0.0, within + earlier, 0.0) - 1.0


def fill_pick(pick, flag_ref):
    rank = ranks(flag_ref)
    slot = lax.broadcasted_iota(jnp.int32, (Q, Q), 0).astype(F32).astype(BF16)
    one, zero = jnp.ones((Q, Q), BF16), jnp.zeros((Q, Q), BF16)
    for g in range(pick.shape[0] // Q):
        here = (rank - float(g * Q)).astype(BF16)
        for c in range(flag_ref.shape[0]):
            hit = here[c : c + 1] == slot
            pick[g * Q : (g + 1) * Q, c * Q : (c + 1) * Q] = jnp.where(hit, one, zero)


def pick_kernel(out_map, res, flags, rows_out, res_out, pick):
    fill_pick(pick, flags())
    blocks = [slice(g * Q, (g + 1) * Q) for g in range(pick.shape[0] // Q)]
    map_ref = out_map()
    for these in blocks:
        rows_out.ref[these] = dot(pick[these], map_ref[...]).astype(BF16)
        rows_out.send(these)
    res_ref = res()
    for these in blocks:
        res_out.ref[these] = dot(pick[these], res_ref[...], NT).astype(BF16)
        res_out.send(these)


def pick_gate_kernel(heads, gate, y, decay, flags, value_out, factor_out, table, pick):
    columns = gate.shape[0]
    width = columns // heads
    flag_ref = flags()
    chunks = flag_ref.shape[0]
    fill_pick(pick, flag_ref)
    run_row = dot3(chunk_rows(decay(), heads), below((Q, Q)))
    before = jnp.zeros((heads, 1), F32)
    none = jnp.zeros((8 - heads, Q), F32)
    for c in range(chunks):
        run = run_row[c * heads : (c + 1) * heads]
        split = []
        for piece in pieces(run + before):
            split += [piece.astype(F32), none]
        split.append(jnp.zeros((8, Q), F32))
        table[columns:, c * Q : (c + 1) * Q] = jnp.concatenate(split, axis=0).astype(BF16)
        before = before + run[:, Q - 1 : Q]
    table[:columns] = gate()[...]
    y_ref = y()
    for g in range(pick.shape[0] // Q):
        these = slice(g * Q, (g + 1) * Q)
        both = dot(pick[these], table[...], NT)
        at = both[:, :columns]
        silu = at / (1.0 + jnp.exp(-at))
        logs = both[:, columns : columns + heads]
        for i in (8, 16):
            logs = logs + both[:, columns + i : columns + i + heads]
        since = jnp.exp(logs)
        since = jnp.concatenate(
            [jnp.broadcast_to(since[:, h : h + 1], (Q, width)) for h in range(heads)], axis=1
        )
        factor_out.ref[these] = (since * silu).astype(BF16)
        factor_out.send(these)
        value_out.ref[these] = (dot(pick[these], y_ref[...], NT) * silu).astype(BF16)
        value_out.send(these)


def ssd_kernel(
    heads,
    skip_ref,
    x,
    in_map,
    out_map,
    step,
    decay,
    y_out,
    scaled,
    state,
):
    width = x.shape[0] // heads
    chunks = x.shape[1] // Q
    row = lax.broadcasted_iota(jnp.int32, (Q, Q), 0)
    col = lax.broadcasted_iota(jnp.int32, (Q, Q), 1)
    mask = row <= col
    logs = chunk_rows(decay(), heads)
    run_row = dot3(logs, below((Q, Q)))
    run_col = dot3r(jnp.where(col <= row, 1.0, 0.0).astype(BF16), logs)
    state[...] = jnp.zeros_like(state)
    step_ref = step()
    in_ref = in_map()
    out_map_ref = out_map()
    x_ref = x()
    for c in range(chunks):
        lanes = slice(c * Q, (c + 1) * Q)
        b = in_ref[lanes, :]
        o = out_map_ref[lanes, :]
        scores = dot(b, o, NT)
        outer = dot(state[...].astype(BF16), o, NT)
        for h in range(heads):
            k = c * heads + h
            part = slice(h * width, (h + 1) * width)
            run = run_row[k : k + 1]
            last = run[:, Q - 1 : Q]
            decay = jnp.where(mask, jnp.exp(run - run_col[:, k : k + 1]), 0.0)
            weights = (scores * decay).astype(BF16)
            xf = x_ref[part, lanes].astype(F32)
            stepped = xf * step_ref[h : h + 1, lanes]
            y = dot(stepped.astype(BF16), weights) + skip_ref[h] * xf
            y_out.ref[part, lanes] = (y + outer[part] * jnp.exp(run)).astype(BF16)
            scaled[part] = (stepped * jnp.exp(last - run)).astype(BF16)
            state[part] = state[part] * jnp.exp(last)
        if c < chunks - 1:
            state[...] += dot(scaled[...], b)
        if c % 4 == 3:
            y_out.send((slice(None), slice((c - 3) * Q, (c + 1) * Q)))


def gate_kernel(heads, in_ref, gain_ref, rows, factor, value, res, out):
    parts = in_ref.shape[0]
    rows_each = in_ref.shape[1] // heads
    columns = value.shape[1]
    out_ref = out.ref
    per = out_ref.shape[1] - 8
    held = in_ref[...].astype(F32)
    states = [
        held[:, h * rows_each : (h + 1) * rows_each].reshape(parts * rows_each, Q)
        for h in range(heads)
    ]
    incoming = jnp.concatenate(states, axis=0).astype(BF16)
    gain = gain_ref[...].reshape(1, columns).astype(F32)
    ones = jnp.ones((8, columns), BF16)
    row = lax.broadcasted_iota(jnp.int32, (8, per), 0)
    outer = dot(rows()[...], incoming, NT)
    factor_ref = factor()
    value_ref = value()
    res_ref = res()
    for j in range(out_ref.shape[0]):
        these = slice(j * per, (j + 1) * per)
        gated = value_ref[these].astype(F32) + factor_ref[these].astype(F32) * outer[these]
        out_ref[j, :per, :columns] = (gated * gain).astype(BF16)
        out_ref[j, :per, columns:] = res_ref[these]
        squares = dot3r(ones, gated * gated)
        hi, mid, low = pieces(squares)
        stacked = jnp.where(
            row == 0, hi.astype(F32), jnp.where(row == 1, mid.astype(F32), low.astype(F32))
        )
        stacked = jnp.where(row < 3, stacked, 0.0)
        tail = jnp.concatenate([stacked, jnp.zeros((8, 2 * columns - per), F32)], axis=1)
        out_ref[j, per:, :] = tail.astype(BF16)
        out.send(j)


def project_kernel(full_width, in_ref, weight, out_ref, lhs, res):
    groups, tall, columns = in_ref.shape
    per = tall - 8
    columns = columns // 2
    total = jnp.zeros((1, per), F32)
    for z in range(groups):
        lhs[:, z * columns : (z + 1) * columns] = in_ref[z, :per, :columns]
        res[:, z * columns : (z + 1) * columns] = in_ref[z, :per, columns:]
        sums = in_ref[z, per:, :].astype(F32)
        total = total + jnp.sum(sums, axis=0, keepdims=True)[:, :per]
    same = lax.broadcasted_iota(jnp.int32, (per, per), 0) == lax.broadcasted_iota(
        jnp.int32, (per, per), 1
    )
    squares = jnp.sum(jnp.where(same, total, 0.0), axis=1, keepdims=True)
    scale = lax.rsqrt(squares / full_width + 1e-05)
    planes, depth, half = weight.shape
    step = depth // PARTS
    for n in range(planes):
        part = slice(n * half, (n + 1) * half)
        done = jnp.zeros((per, half), F32)
        for k in range(PARTS):
            span = slice(k * step, (k + 1) * step)
            done = done + dot(lhs[:, span], weight(n * PARTS + k)[n, span])
        out_ref[:, part] = (done * scale + res[:, part].astype(F32)).astype(BF16)


class Source:
    def __init__(self, hbm, ref, sem, split):
        self.shape, self.ref = hbm.shape, ref
        if split == "h":
            parts = [slice(None)]
        elif split == "w":
            step = hbm.shape[1] // PARTS
            parts = [
                (n, slice(k * step, (k + 1) * step)) for n in range(hbm.shape[0]) for k in range(PARTS)
            ]
        else:
            step = hbm.shape[split == "c"] // PARTS
            parts = [slice(k * step, (k + 1) * step) for k in range(PARTS)]
            if split == "c":
                parts = [(slice(None), p) for p in parts]
        self.copies = [
            pltpu.make_async_copy(hbm.at[p], ref.at[p], sem.at[k]) for k, p in enumerate(parts)
        ]

    def start(self, k):
        if k < len(self.copies):
            self.copies[k].start()

    def __call__(self, k=0):
        self.copies[k].wait()
        return self.ref


class Target:
    def __init__(self, hbm, ref, sem):
        self.hbm, self.ref, self.sem, self.copies = hbm, ref, sem, []

    def send(self, these):
        k = len(self.copies)
        copy = pltpu.make_async_copy(self.ref.at[these], self.hbm.at[these], self.sem.at[k])
        copy.start()
        self.copies.append(copy)


def call(kernel, outs, args, scratch=(), places="", to="v", name=None, mib=0, flags=None):
    spaces = {"v": pltpu.VMEM, "s": pltpu.SMEM}
    many = isinstance(outs, (tuple, list))
    results = list(outs) if many else [outs]
    far_in = [i for i, p in enumerate(places) if p in "hcqw"]
    far_out = [i for i, p in enumerate(to) if p == "h"]
    buffers = [pltpu.VMEM(args[i].shape, args[i].dtype) for i in far_in]
    buffers += [pltpu.VMEM(results[i].shape, results[i].dtype) for i in far_out]
    sems = [pltpu.SemaphoreType.DMA((2 * PARTS,)) for _ in far_in]
    sems += [pltpu.SemaphoreType.DMA((8,)) for _ in far_out]

    def body(*refs):
        ins = list(refs[: len(args)])
        res = list(refs[len(args) : len(args) + len(results)])
        rest = refs[len(args) + len(results) :]
        own = rest[: len(scratch)]
        held = rest[len(scratch) : len(scratch) + len(buffers)]
        flagged = rest[len(scratch) + len(buffers) :]
        for k, i in enumerate(far_in):
            ins[i] = Source(ins[i], held[k], flagged[k], places[i])
        for part in range(2 * PARTS):
            for i in sorted(far_in, key=lambda i: args[i].size):
                ins[i].start(part)
        for k, i in enumerate(far_out):
            res[i] = Target(res[i], held[len(far_in) + k], flagged[len(far_in) + k])
        kernel(*ins, *res, *own)
        for i in far_out:
            for copy in res[i].copies:
                copy.wait()

    out_specs = [pl.BlockSpec(memory_space=spaces.get(p, pltpu.HBM)) for p in to]
    return pl.pallas_call(
        body,
        out_shape=outs,
        in_specs=[pl.BlockSpec(memory_space=spaces.get(p, pltpu.HBM)) for p in places],
        out_specs=out_specs if many else out_specs[0],
        scratch_shapes=[*scratch, *buffers, *sems],
        compiler_params=pltpu.CompilerParams(vmem_limit_bytes=mib << 20 if mib else None, flags=flags),
        name=name,
    )(*args)


def on_device(
    head_input,
    gate_input,
    input_map,
    output_map,
    step_size,
    log_decay,
    skip_gain,
    residual,
    boundary,
    norm_gain,
    out_weight,
):
    S = jax.ShapeDtypeStruct
    group = ("x", "core")
    parts = lax.axis_size(group)
    groups = lax.axis_size("y")
    shares = lax.axis_size("head")
    local_width, length = head_input.shape
    heads = step_size.shape[0]
    full_width = out_weight.shape[1]
    slots = length // 4
    per = slots // shares
    used = local_width // parts
    height = used + 8

    held = lax.optimization_barrier
    flags = boundary.reshape(length // Q, Q)

    state = call(
        functools.partial(final_state_kernel, heads, parts),
        S((parts, height, Q), BF16),
        (head_input, input_map, step_size, log_decay),
        [pltpu.VMEM((local_width, length), BF16)],
        places="hhhh",
        name="final_state",
    )
    state, out_weight, flags = held((state, out_weight, flags))
    cores = lax.axis_size("core")
    half = full_width // cores
    own = lax.dynamic_slice_in_dim(out_weight, lax.axis_index("core") * half, half, 1)
    weight = lax.all_gather(own[None], ("core", "head"), axis=0, tiled=True)
    moved = lax.all_to_all(state, group, 0, 0, tiled=True)
    rows, res = call(
        pick_kernel,
        (S((slots, Q), BF16), S((slots, local_width), BF16)),
        (output_map, residual, flags),
        [pltpu.VMEM((slots, length), BF16)],
        places="hhh",
        to="hh",
        name="pick",
    )
    moved, rows, res = held((moved, rows, res))
    total = call(
        functools.partial(group_scan_kernel, heads),
        S((groups, height, Q), BF16),
        (moved,),
        places="v",
        name="group_scan",
        mib=2,
    )
    total, input_map = held((total, input_map))
    totals = lax.all_to_all(total, "y", 0, 0, tiled=True)
    y = call(
        functools.partial(ssd_kernel, heads),
        S((local_width, length), BF16),
        (skip_gain, head_input, input_map, output_map, step_size, log_decay),
        [pltpu.VMEM((local_width, Q), BF16), pltpu.VMEM((local_width, Q), F32)],
        places="shhhhh",
        to="h",
        name="ssd",
    )
    totals, y = held((totals, y))
    incoming = call(
        functools.partial(combine_kernel, heads),
        S((parts, used, Q), BF16),
        (totals, moved),
        places="vv",
        name="combine",
        mib=2,
    )
    incoming, flags = held((incoming, flags))
    incoming = lax.all_to_all(incoming, group, 0, 0, tiled=True)
    value, factor = call(
        functools.partial(pick_gate_kernel, heads),
        (S((slots, local_width), BF16), S((slots, local_width), BF16)),
        (gate_input, y, log_decay, flags),
        [pltpu.VMEM((local_width + 32, length), BF16), pltpu.VMEM((slots, length), BF16)],
        places="hhhh",
        to="hh",
        name="pick_gate",
    )
    gated = call(
        functools.partial(gate_kernel, heads),
        S((shares, per + 8, 2 * local_width), BF16),
        (incoming, norm_gain, rows, factor, value, res),
        places="vvhhhh",
        to="h",
        name="gated",
    )
    gathered = lax.all_to_all(gated, "head", 0, 0, tiled=True)
    weight = weight.reshape(cores, shares * local_width, half)
    return call(
        functools.partial(project_kernel, full_width),
        S((per, full_width), BF16),
        (gathered, weight),
        [pltpu.VMEM((per, full_width), BF16), pltpu.VMEM((per, full_width), BF16)],
        places="vw",
        name="project",
    )


def solution(mesh):
    heads = mesh.shape["head"]
    segs = mesh.shape["seg"]
    core, x = (2, 4) if segs % 8 == 0 else (1, 1)
    if segs == 8:
        x = 2
    fine = Mesh(mesh.devices.reshape(segs // (x * core), x, core, heads), ("y", "x", "core", "head"))
    seg = ("y", "x", "core")
    return jax.shard_map(
        on_device,
        mesh=fine,
        in_specs=(
            P("head", seg),
            P("head", seg),
            P(seg, None),
            P(seg, None),
            P("head", seg),
            P("head", seg),
            P("head"),
            P("head", seg),
            P(seg),
            P("head"),
            P("head", None),
        ),
        out_specs=P((*seg, "head"), None),
        check_vma=False,
    )
```
